256 devices in a mesh: slab: 32 (over y, z_lo, core), sub: 8 (over x, z_hi).
Axes of the slice: x: 4, y: 4, z: 8 (z_hi: 2, z_lo: 4; z = z_hi * 4 + z_lo), core: 2. Of those that a mesh axis runs over, the one named last changes fastest.
Arguments:
- rhs_interior: float32 [32, 32, 2, 256, 128], P('slab', 'sub'), may hold values from -6 to 6
- rhs_separator: float32 [32, 2, 512, 128], P('slab'), may hold values from -6 to 6
- inverse_blocks: float32 [32, 32, 2, 256, 256], P('slab', 'sub'), may hold values from -0.375 to 0.375
- coupling: float32 [32, 32, 2, 512, 256], P('slab', 'sub'), may hold values from -0.0625 to 0.0625
- separator_rows: int32 [32, 32, 512], P('slab', 'sub'), may hold values from 0 to 511, each once within a row
- separator_inverse: float32 [32, 2, 512, 512], P('slab'), may hold values from -1.1 to 1.1
- transfer: float32 [32, 2, 512, 512], P('slab'), may hold values from -1.1 to 1.1
Outputs:
- interior_solution: float32 [32, 32, 2, 256, 128], P('slab', 'sub')
- separator_solution: float32 [32, 2, 512, 128], P('slab')
The draws below stay inside these ranges and needn't reach their ends.
Inputs may be any that keep to these rules, and one draw needn't show every extreme that they name: Each block's separator_rows lists every separator row 0 to 511 exactly once.
All inputs are finite; a program needn't handle non-finite values.
Results may differ from the reference program's by a relative error of at most 0.0003.
Values sent between devices are 32-bit elements; how exact they have to be, the bound alone decides.
A program may use at most 128 MiB of HBM per device.

```python
import math
import jax
import jax.numpy as jnp
from jax import lax

M = 256
TRACE_UNKNOWNS = 512
SHOTS = 128
NB = 4
NBLK = 32
SLAB_COUNT = 32


def draw_separator_inverse(key, part):
    first, second = jax.random.split(jax.random.fold_in(key, 11))
    noise = jax.random.normal(first, (SLAB_COUNT, 2, TRACE_UNKNOWNS, TRACE_UNKNOWNS), jnp.float32)
    noise = jnp.clip(noise, -5.0, 5.0) * (0.5 / math.sqrt(TRACE_UNKNOWNS))
    diagonal = jax.random.uniform(second, (SLAB_COUNT, 1, TRACE_UNKNOWNS), jnp.float32, 0.35, 0.6)
    eye = jnp.eye(TRACE_UNKNOWNS, dtype=jnp.float32)
    real_mask = jnp.array([1.0, 0.0], jnp.float32)[None, :, None, None]
    return noise + real_mask * eye[None, None] * diagonal[..., None, :]


def draw_transfer(key, part):
    random_keys = jax.random.split(jax.random.fold_in(key, 23), 4)
    absolute_size = jnp.exp(jax.random.uniform(random_keys[0], (SLAB_COUNT, TRACE_UNKNOWNS), jnp.float32, math.log(0.3), math.log(0.97)))
    pulse_batch = jax.random.bernoulli(random_keys[1], 3.0 / SLAB_COUNT, (SLAB_COUNT, TRACE_UNKNOWNS))
    absolute_size = absolute_size * jnp.where(pulse_batch, 0.6, 1.0)
    phase = jax.random.uniform(random_keys[2], (SLAB_COUNT, TRACE_UNKNOWNS), jnp.float32, -math.pi, math.pi)
    noise = jnp.clip(jax.random.normal(random_keys[3], (SLAB_COUNT, 2, TRACE_UNKNOWNS, TRACE_UNKNOWNS), jnp.float32), -5.0, 5.0) * (0.2 / math.sqrt(2 * TRACE_UNKNOWNS))
    eye = jnp.eye(TRACE_UNKNOWNS, dtype=jnp.float32)
    diagonal = jnp.stack([absolute_size * jnp.cos(phase), absolute_size * jnp.sin(phase)], axis=1)
    return noise + eye[None, None] * diagonal[..., None, :]


def level_of(own_key, dims, cuts, low, high):
    level = 1.0
    for dim, blocks in cuts:
        heights = jax.random.uniform(jax.random.fold_in(jax.random.fold_in(own_key, 6), dim), (blocks,), jnp.float32, low / len(cuts), high / len(cuts))
        level = level * jnp.repeat(jnp.exp(heights), dims[dim] // blocks).reshape((-1,) + (1,) * (len(dims) - 1 - dim))
    return level


def scatter_about(rng, dims, scale, limit, shards=(), kind=jnp.bfloat16):
    values = jax.random.normal(rng, dims, jnp.float32) * scale
    if len(shards) > 0:
        values = level_of(rng, dims, shards, -0.22, 0.18) * values
    return jnp.clip(values, min=-limit, max=limit).astype(kind)


def setup_inputs(seed: int = 0) -> dict:
    splits = jax.random.split(jax.random.key(seed), 8)
    return {
        "rhs_interior": scatter_about(splits[0], (SLAB_COUNT, NBLK, 2, M, SHOTS), 1.0, 6.0, ((0, 32), (1, 8)), jnp.float32),
        "rhs_separator": scatter_about(splits[1], (SLAB_COUNT, 2, TRACE_UNKNOWNS, SHOTS), 1.0, 6.0, ((0, 32),), jnp.float32),
        "inverse_blocks": scatter_about(splits[2], (SLAB_COUNT, NBLK, 2, M, M), M ** -0.5, 0.375, ((0, 32), (1, 8)), jnp.float32),
        "coupling": scatter_about(splits[3], (SLAB_COUNT, NBLK, 2, TRACE_UNKNOWNS, M), (4 * TRACE_UNKNOWNS * NB) ** -0.5, 0.0625, ((0, 32), (1, 8)), jnp.float32),
        "separator_rows": jax.vmap(lambda own: jax.random.permutation(own, TRACE_UNKNOWNS))(jax.random.split(splits[4], SLAB_COUNT * NBLK)).reshape((SLAB_COUNT, NBLK, TRACE_UNKNOWNS)).astype(jnp.int32),
        "separator_inverse": draw_separator_inverse(jax.random.fold_in(splits[7], 71), 0),
        "transfer": draw_transfer(jax.random.fold_in(splits[7], 71), 0),
    }


HIGH = lax.Precision.HIGHEST


def multiply(left, right):
    return jnp.matmul(left, right, precision=HIGH)


def complex_product(left, right):
    real_part = multiply(left[..., 0, :, :], right[..., 0, :, :]) - multiply(left[..., 1, :, :], right[..., 1, :, :])
    imag_part = multiply(left[..., 0, :, :], right[..., 1, :, :]) + multiply(left[..., 1, :, :], right[..., 0, :, :])
    return jnp.stack([real_part, imag_part], axis=-3)


def flipped(matrix):
    return jnp.swapaxes(matrix, -1, -2)


def placed_coupling(weights, rows):
    count = rows.shape[-1]
    spread = (rows[:, None, :] == jnp.arange(count)[None, :, None]).astype(weights.dtype)
    return jnp.einsum("bpr,bcrm->bcpm", spread, weights, precision=HIGH)


def reference(rhs_interior, rhs_separator, inverse_blocks, coupling, separator_rows, separator_inverse, transfer):
    def slab_sum(items):
        loads, lower, weights, rows = items
        placed = placed_coupling(weights, rows)
        return jnp.sum(complex_product(placed, complex_product(lower, loads)), axis=0)

    sums = lax.map(slab_sum, (rhs_interior, inverse_blocks, coupling, separator_rows))
    local = complex_product(separator_inverse, rhs_separator - sums)
    traces = []
    incoming = jnp.zeros_like(local[0])
    for index in range(SLAB_COUNT):
        incoming = local[index] - complex_product(transfer[index], incoming)
        traces.append(incoming)
    finished_slabs = [None] * SLAB_COUNT
    carried = jnp.zeros_like(local[0])
    for index in reversed(range(SLAB_COUNT)):
        value = traces[index] - carried
        finished_slabs[index] = value
        carried = complex_product(flipped(transfer[index]), value)
    finished_slabs = jnp.stack(finished_slabs)

    def slab_solution(items):
        loads, lower, weights, rows, value = items
        placed = placed_coupling(weights, rows)
        eliminated = complex_product(lower, loads)
        return complex_product(flipped(lower), eliminated - complex_product(flipped(placed), value[None]))

    interior = lax.map(slab_solution, (rhs_interior, inverse_blocks, coupling, separator_rows, finished_slabs))
    return interior, finished_slabs
```

```python
import functools

import jax
import jax.numpy as jnp
from jax import lax
from jax.experimental import pallas as pl
from jax.experimental.pallas import tpu as pltpu
from jax.sharding import PartitionSpec as P

MESH = pl.DeviceIdType.MESH
F32 = jnp.float32
BF16 = jnp.bfloat16
NN = (((1,), (0,)), ((), ()))
NT = (((1,), (1,)), ((), ()))


def halves(value):
    high = value.astype(BF16)
    return high, (value - high.astype(F32)).astype(BF16)


def dot(left, right, dims=NN):
    return lax.dot_general(left, right, dims, preferred_element_type=F32)


def dot3(left, right, dims=NN):
    return dot(left[0], right[0], dims) + (
        dot(left[0], right[1], dims) + dot(left[1], right[0], dims)
    )


def times(value, high, low, dims):
    n = value.shape[0] // 2
    value_high, value_low = halves(value)
    both = jnp.concatenate([value_high, value_low], axis=0)
    out = []
    for part in range(2):
        whole = dot(both, high[part], dims)
        out.append(whole[: 2 * n] + (whole[2 * n :] + dot(value_high, low[part], dims)))
    return jnp.concatenate([out[0][:n] - out[1][n:], out[0][n:] + out[1][:n]], axis=0)


def load_kernel(rows_ref, rhs_ref, inverse_ref, coupling_ref, separator_ref, load_ref, elim_ref, total):
    block = pl.program_id(0)
    rhs = halves(jnp.concatenate([rhs_ref[0], rhs_ref[1]], axis=1))
    shots = rhs_ref.shape[-1]

    def product(matrix, right):
        real = dot3(halves(matrix[0]), right)
        imag = dot3(halves(matrix[1]), right)
        return jnp.concatenate(
            [real[:, :shots] - imag[:, shots:], real[:, shots:] + imag[:, :shots]], axis=1
        )

    eliminated = product(inverse_ref, rhs)
    elim_ref[...] = eliminated.T
    weighted = halves(product(coupling_ref, halves(eliminated)))
    count = rows_ref.shape[-1]
    spread = (lax.broadcasted_iota(jnp.int32, (count, count), 0) == rows_ref[...]).astype(BF16)
    placed = dot(spread, weighted[0]) + dot(spread, weighted[1])

    @pl.when(block == 0)
    def _():
        total[...] = placed

    @pl.when(block > 0)
    def _():
        total[...] += placed

    @pl.when(block == pl.num_programs(0) - 1)
    def _():
        given = jnp.concatenate([separator_ref[0], separator_ref[1]], axis=1)
        first = lax.axis_index("sub") == 0
        rest = (jnp.where(first, given, jnp.zeros_like(given)) - total[...]).T
        groups = shots // 8
        rest = rest.reshape(2, groups, 8, count)
        load_ref[...] = jnp.stack([rest[0], rest[1]], axis=1).reshape(load_ref.shape)


def loads_of(rhs_interior, rhs_separator, inverse_blocks, coupling, rows):
    nb, _, m, shots = rhs_interior.shape
    count = coupling.shape[2]
    subs = 8
    return pl.pallas_call(
        load_kernel,
        grid=(nb,),
        out_shape=(
            jax.ShapeDtypeStruct((subs, 2 * shots // subs, count), F32),
            jax.ShapeDtypeStruct((nb, 2 * shots, m), F32),
        ),
        in_specs=[
            pl.BlockSpec((None, 1, count), lambda b: (b, 0, 0)),
            pl.BlockSpec((None, 2, m, shots), lambda b: (b, 0, 0, 0)),
            pl.BlockSpec((None, 2, m, m), lambda b: (b, 0, 0, 0)),
            pl.BlockSpec((None, 2, count, m), lambda b: (b, 0, 0, 0)),
            pl.BlockSpec((2, count, shots), lambda b: (0, 0, 0)),
        ],
        out_specs=(
            pl.BlockSpec((subs, 2 * shots // subs, count), lambda b: (0, 0, 0)),
            pl.BlockSpec((None, 2 * shots, m), lambda b: (b, 0, 0)),
        ),
        scratch_shapes=[pltpu.VMEM((count, 2 * shots), F32)],
        compiler_params=pltpu.CompilerParams(vmem_limit_bytes=40 << 20),
    )(rows[:, None, :], rhs_interior, inverse_blocks, coupling, rhs_separator)


(C_MATRIX, C_X, C_Z, C_SWAP, C_AHEAD, C_BACK, C_CHIP, C_FAR, C_SIDE) = (0, 1, 4, 5, 6, 7, 8, 9, 10)
COPIES = 13


def sweep_kernel(
    load_ref,
    inverse_hbm,
    transfer_hbm,
    out_ref,
    pair,
    pair_high,
    pair_low,
    inverse,
    inverse_high,
    inverse_low,
    merged_high,
    merged_low,
    from_x,
    mine,
    from_z,
    local,
    spare,
    ahead_in,
    ahead_out,
    back_in,
    back_out,
    found,
    gathered,
    send_sem,
    recv_sem,
    here_sem,
):
    slab, sub = lax.axis_index("slab"), lax.axis_index("sub")
    chip, core = slab // 2, slab % 2
    chips = lax.axis_size("slab") // 2
    row, along = chip // 4, chip % 4
    x, far = sub // 2, sub % 2
    side = (far + row) % 2
    group = x * 2 + side
    partner = (slab + 1 - 2 * core, sub)
    opposite = (slab, x * 2 + (far + 1) % 2)
    ahead = ((slab + 2) % (2 * chips), x * 2 + (far + along // 3) % 2)
    behind = ((slab + 2 * chips - 2) % (2 * chips), x * 2 + (far + (3 - along) // 3) % 2)
    beside = [(slab, ((x + d) % 4) * 2 + far) for d in (1, 2, 3)]
    not_first, not_last = chip > 0, chip < chips - 1

    def remote(index, source, target, device):
        return pltpu.make_async_remote_copy(
            src_ref=source,
            dst_ref=target,
            send_sem=send_sem.at[index],
            recv_sem=recv_sem.at[index],
            device_id=device,
            device_id_type=MESH,
        )

    own_matrix = pltpu.make_async_copy(transfer_hbm, pair.at[core], here_sem.at[0])
    own_inverse = pltpu.make_async_copy(inverse_hbm, inverse, here_sem.at[1])
    own_matrix.start()
    own_inverse.start()

    barrier = pltpu.get_barrier_semaphore()

    def greet(device):
        pl.semaphore_signal(barrier, inc=1, device_id=device, device_id_type=MESH)

    for device in [partner, opposite] + beside:
        greet(device)
    pl.when(not_last)(lambda: greet(ahead))
    pl.when(not_first)(lambda: greet(behind))
    pl.semaphore_wait(
        barrier, 5 + (chip + chips - 1) // chips + (2 * chips - 2 - chip) // chips
    )

    x_copies = []
    for d in (1, 2, 3):
        to = (x + d) % 4
        copy = remote(C_X + d - 1, load_ref.at[pl.ds(2 * to, 2)], from_x.at[d - 1], beside[d - 1])
        copy.start()
        x_copies.append(copy)
    matrix_copy = remote(C_MATRIX, transfer_hbm, pair.at[core], partner)
    matrix_copy.start()

    size = pair.shape[-1]
    own_inverse.wait()

    def split_inverse(step, carry):
        at = pl.ds(pl.multiple_of(step * 128, 128), 128)
        for part in range(2):
            inverse_high[part, at, :], inverse_low[part, at, :] = halves(inverse[part, at, :])
        return carry

    lax.fori_loop(0, size // 128, split_inverse, 0)
    own_matrix.wait()
    for copy in x_copies:
        copy.wait_recv()
    mine[...] = (load_ref[pl.ds(2 * x, 2)] + from_x[0]) + (from_x[1] + from_x[2])
    z_copy = remote(C_Z, mine.at[1 - side], from_z, opposite)
    z_copy.start()

    remote(C_MATRIX, transfer_hbm, pair.at[1 - core], partner).wait_recv()

    def split_pair(step, carry):
        at = pl.ds(pl.multiple_of(step * 128, 128), 128)
        for slot in range(2):
            for part in range(2):
                pair_high[slot, part, at, :], pair_low[slot, part, at, :] = halves(
                    pair[slot, part, at, :]
                )
        return carry

    lax.fori_loop(0, size // 128, split_pair, 0)
    first = (pair_high.at[0], pair_low.at[0])
    second = (pair_high.at[1], pair_low.at[1])

    def merge(step, carry):
        at = pl.ds(pl.multiple_of(step * 128, 128), 128)
        left_high = jnp.concatenate([second[0][0, at, :], second[0][1, at, :]], axis=0)
        left_low = jnp.concatenate([second[1][0, at, :], second[1][1, at, :]], axis=0)
        out = [
            dot3((left_high, left_low), (first[0][part], first[1][part])) for part in range(2)
        ]
        merged = (out[0][:128] - out[1][128:], out[0][128:] + out[1][:128])
        for part in range(2):
            merged_high[part, at, :], merged_low[part, at, :] = halves(merged[part])
        return carry

    lax.fori_loop(0, size // 128, merge, 0)

    z_copy.wait_recv()
    summed = (mine[side] + from_z[...]).reshape(2, 2, 8, size)
    summed = jnp.stack([summed[:, 0], summed[:, 1]], axis=0).reshape(32, size)
    solved = times(summed, inverse_high, inverse_low, NT).reshape(2, 2, 8, size)
    solved = jnp.stack([solved[:, 0], solved[:, 1]], axis=0).reshape(2, 16, size)
    spare[...] = solved
    local[core] = spare[core]
    swap = remote(C_SWAP, spare.at[1 - core], local.at[core], partner)
    swap.start()

    @pl.when(chip == 0)
    def _():
        ahead_in[...] = jnp.zeros_like(ahead_in)

    @pl.when(chip == chips - 1)
    def _():
        back_in[...] = jnp.zeros_like(back_in)

    remote(C_SWAP, spare.at[0], local.at[1 - core], partner).wait_recv()

    start = local[1] - times(local[0], second[0], second[1], NT)
    ahead_copy = remote(C_AHEAD, ahead_out, ahead_in, ahead)
    pl.when(not_first)(ahead_copy.wait_recv)
    incoming = ahead_in[...]
    trace_second = start + times(incoming, merged_high, merged_low, NT)
    ahead_out[...] = trace_second
    pl.when(not_last)(ahead_copy.start)
    trace_first = local[0] - times(incoming, first[0], first[1], NT)
    queued = times(
        trace_first - times(trace_second, second[0], second[1], NN), first[0], first[1], NN
    )

    back_copy = remote(C_BACK, back_out, back_in, behind)
    pl.when(not_last)(back_copy.wait_recv)
    carried = back_in[...]

    @pl.when(not_first)
    def _():
        back_out[...] = queued + times(carried, merged_high, merged_low, NN)
        back_copy.start()

    found[1] = trace_second - carried
    found[0] = trace_first - times(found[1], second[0], second[1], NN)

    gathered[group, core] = found[core]
    chip_copy = remote(C_CHIP, found.at[1 - core], gathered.at[group, core], partner)
    chip_copy.start()
    remote(C_CHIP, found.at[0], gathered.at[group, 1 - core], partner).wait_recv()
    far_copy = remote(C_FAR, gathered.at[group], gathered.at[group], opposite)
    far_copy.start()
    other = x * 2 + 1 - side
    remote(C_FAR, gathered.at[other], gathered.at[other], opposite).wait_recv()
    for d in (1, 2, 3):
        piece = gathered.at[pl.ds(2 * x, 2)]
        remote(C_SIDE + d - 1, piece, piece, beside[d - 1]).start()
    for d in (1, 2, 3):
        piece = gathered.at[pl.ds(2 * ((x + 4 - d) % 4), 2)]
        remote(C_SIDE + d - 1, piece, piece, beside[d - 1]).wait_recv()
    out_ref[...] = gathered[...]

    for copy in x_copies:
        copy.wait_send()
    for copy in (matrix_copy, z_copy, swap, chip_copy, far_copy):
        copy.wait_send()
    pl.when(not_last)(ahead_copy.wait_send)
    pl.when(not_first)(back_copy.wait_send)
    for d in (1, 2, 3):
        piece = gathered.at[pl.ds(2 * x, 2)]
        remote(C_SIDE + d - 1, piece, piece, beside[d - 1]).wait_send()


def sweeps_of(load, separator_inverse, transfer):
    size = transfer.shape[-1]
    vmem = pltpu.VMEM
    return pl.pallas_call(
        sweep_kernel,
        out_shape=jax.ShapeDtypeStruct((8, 2, 16, size), F32),
        in_specs=[
            pl.BlockSpec(memory_space=pltpu.VMEM),
            pl.BlockSpec(memory_space=pl.ANY),
            pl.BlockSpec(memory_space=pl.ANY),
        ],
        out_specs=pl.BlockSpec(memory_space=pltpu.VMEM),
        scratch_shapes=[
            vmem((2, 2, size, size), F32),
            vmem((2, 2, size, size), BF16),
            vmem((2, 2, size, size), BF16),
            vmem((2, size, size), F32),
            vmem((2, size, size), BF16),
            vmem((2, size, size), BF16),
            vmem((2, size, size), BF16),
            vmem((2, size, size), BF16),
            vmem((3, 2, 32, size), F32),
            vmem((2, 32, size), F32),
            vmem((32, size), F32),
            vmem((2, 16, size), F32),
            vmem((2, 16, size), F32),
            vmem((16, size), F32),
            vmem((16, size), F32),
            vmem((16, size), F32),
            vmem((16, size), F32),
            vmem((2, 16, size), F32),
            vmem((8, 2, 16, size), F32),
            pltpu.SemaphoreType.DMA((COPIES,)),
            pltpu.SemaphoreType.DMA((COPIES,)),
            pltpu.SemaphoreType.DMA((2,)),
        ],
        compiler_params=pltpu.CompilerParams(
            collective_id=0, has_side_effects=True, vmem_limit_bytes=48 << 20
        ),
    )(load, separator_inverse, transfer)


def interior_kernel(
    rows_ref, found_ref, elim_ref, inverse_ref, coupling_ref, interior_ref, separator_ref, high, low
):
    shots = interior_ref.shape[-1]
    count = rows_ref.shape[-1]

    @pl.when(pl.program_id(0) == 0)
    def _():
        found = found_ref[...].reshape(shots // 8, 2, 8, count)
        value = jnp.stack([found[:, 0], found[:, 1]], axis=0).reshape(2 * shots, count)
        high[...], low[...] = halves(value)
        turned = value.T
        separator_ref[0] = turned[:, :shots]
        separator_ref[1] = turned[:, shots:]

    def product(left, matrix):
        left = halves(left)
        real = dot3(left, halves(matrix[0]))
        imag = dot3(left, halves(matrix[1]))
        return jnp.concatenate(
            [real[:shots] - imag[shots:], real[shots:] + imag[:shots]], axis=0
        )

    spread = (lax.broadcasted_iota(jnp.int32, (count, count), 0) == rows_ref[...]).astype(BF16)
    picked = dot(high[...], spread) + dot(low[...], spread)
    rest = elim_ref[...] - product(picked, coupling_ref)
    turned = product(rest, inverse_ref).T
    interior_ref[0] = turned[:, :shots]
    interior_ref[1] = turned[:, shots:]


def interiors_of(found, eliminated, inverse_blocks, coupling, rows):
    nb, _, count, m = coupling.shape
    shots = eliminated.shape[1] // 2
    return pl.pallas_call(
        interior_kernel,
        grid=(nb,),
        out_shape=(
            jax.ShapeDtypeStruct((nb, 2, m, shots), F32),
            jax.ShapeDtypeStruct((2, count, shots), F32),
        ),
        in_specs=[
            pl.BlockSpec((None, 1, count), lambda b: (b, 0, 0)),
            pl.BlockSpec(found.shape, lambda b: (0, 0, 0, 0)),
            pl.BlockSpec((None, 2 * shots, m), lambda b: (b, 0, 0)),
            pl.BlockSpec((None, 2, m, m), lambda b: (b, 0, 0, 0)),
            pl.BlockSpec((None, 2, count, m), lambda b: (b, 0, 0, 0)),
        ],
        out_specs=(
            pl.BlockSpec((None, 2, m, shots), lambda b: (b, 0, 0, 0)),
            pl.BlockSpec((2, count, shots), lambda b: (0, 0, 0)),
        ),
        scratch_shapes=[
            pltpu.VMEM((2 * shots, count), BF16),
            pltpu.VMEM((2 * shots, count), BF16),
        ],
        compiler_params=pltpu.CompilerParams(vmem_limit_bytes=40 << 20),
    )(rows[:, None, :], found, eliminated, inverse_blocks, coupling)


def body(
    rhs_interior,
    rhs_separator,
    inverse_blocks,
    coupling,
    separator_rows,
    separator_inverse,
    transfer,
):
    rows = separator_rows[0]
    load, eliminated = loads_of(
        rhs_interior[0], rhs_separator[0], inverse_blocks[0], coupling[0], rows
    )
    found = sweeps_of(load, separator_inverse[0], transfer[0])
    interior, separator = interiors_of(found, eliminated, inverse_blocks[0], coupling[0], rows)
    return (interior[None], separator[None])


def solution(mesh):
    in_specs = (
        P("slab", "sub", None, None, None),
        P("slab", None, None, None),
        P("slab", "sub", None, None, None),
        P("slab", "sub", None, None, None),
        P("slab", "sub", None),
        P("slab", None, None, None),
        P("slab", None, None, None),
    )
    out_specs = (P("slab", "sub", None, None, None), P("slab", None, None, None))
    return jax.shard_map(body, mesh=mesh, in_specs=in_specs, out_specs=out_specs, check_vma=False)
```

```python
import types

import jax
import jax.numpy as jnp
from jax import lax
from jax.experimental import pallas as pl
from jax.experimental.pallas import tpu as pltpu
from jax.sharding import PartitionSpec as P

MESH = pl.DeviceIdType.MESH
F32 = jnp.float32
BF16 = jnp.bfloat16
NN = (((1,), (0,)), ((), ()))
NT = (((1,), (1,)), ((), ()))
STRIP = 128


def halves(value):
    high = value.astype(BF16)
    return high, (value - high.astype(F32)).astype(BF16)


def dot(left, right, dims=NN):
    return lax.dot_general(left, right, dims, preferred_element_type=F32)


def dot3(left, right, dims=NN):
    return dot(left[0], right[0], dims) + (
        dot(left[0], right[1], dims) + dot(left[1], right[0], dims)
    )


def times(value, matrix, dims):
    high, low = matrix
    n = value.shape[0] // 2
    value_high, value_low = halves(value)
    both = jnp.concatenate([value_high, value_low], axis=0)
    out = []
    for part in range(2):
        whole = dot(both, high[part], dims)
        out.append(whole[: 2 * n] + (whole[2 * n :] + dot(value_high, low[part], dims)))
    return jnp.concatenate([out[0][:n] - out[1][n:], out[0][n:] + out[1][:n]], axis=0)


def kernel(names, *refs):
    r = types.SimpleNamespace(**dict(zip(names, refs)))
    slab, sub = lax.axis_index("slab"), lax.axis_index("sub")
    slabs = lax.axis_size("slab")
    core, role, duo = slab % 2, (slab // 2) % 2, slab // 4
    duos = slabs // 4
    x, far = sub // 2, sub % 2
    after, before = (2 * duos - 3 - duo) // (duos - 1), (duo + duos - 2) // (duos - 1)
    has_after, has_before = duo < duos - 1, duo > 0
    early, late = role == 0, role == 1
    blocks, _, size, m = r.coupling_hbm.shape
    shots = r.rhs_hbm.shape[-1]

    other_core, other_sub = slab + 1 - 2 * core, 2 * x + 1 - far
    partner = (other_core, sub)
    opposite = (slab, other_sub)
    across = (other_core, other_sub)
    mate = (slab + 2 - 4 * role, sub)
    beside = [(slab, ((x + d) % 4) * 2 + far) for d in (1, 2, 3)]
    next_late, next_early = ((slab + 4) % slabs, sub), ((slab + 2) % slabs, sub)
    last_early, last_late = ((slab + slabs - 4) % slabs, sub), ((slab + slabs - 2) % slabs, sub)

    count = [0]
    unsent = []

    def remote(index, source, target, device):
        return pltpu.make_async_remote_copy(
            src_ref=source,
            dst_ref=target,
            send_sem=r.send_sem.at[index],
            recv_sem=r.recv_sem.at[index],
            device_id=device,
            device_id_type=MESH,
        )

    def channel():
        count[0] += 1
        return count[0] - 1

    def send(index, source, target, device, when=None):
        copy = remote(index, source, target, device)
        if when is None:
            copy.start()
        unsent.append((copy, when))
        return copy

    def receive(index, target):
        remote(index, target, target, partner).wait_recv()

    def local_copies(b):
        return [
            pltpu.make_async_copy(r.inverse_hbm.at[b], r.inverse.at[b], r.block_sem.at[0, b]),
            pltpu.make_async_copy(r.rhs_hbm.at[b], r.rhs.at[b], r.block_sem.at[1, b]),
            pltpu.make_async_copy(r.coupling_hbm.at[b], r.coupling.at[b], r.block_sem.at[2, b]),
        ]

    own_transfer = pltpu.make_async_copy(r.transfer_hbm, r.pair.at[core], r.here_sem.at[0])
    own_given = pltpu.make_async_copy(r.separator_hbm, r.given, r.here_sem.at[1])
    own_schur = pltpu.make_async_copy(r.schur_hbm, r.schur, r.here_sem.at[2])
    own_transfer.start()

    barrier = pltpu.get_barrier_semaphore()

    def greet(device):
        pl.semaphore_signal(barrier, inc=1, device_id=device, device_id_type=MESH)

    for device in [partner, opposite, across, mate] + beside:
        greet(device)

    @pl.when(has_after)
    def _():
        greet(next_late)

        @pl.when(late)
        def _():
            greet(next_early)

    @pl.when(has_before)
    def _():
        greet(last_early)

        @pl.when(early)
        def _():
            greet(last_late)

    pl.semaphore_wait(barrier, 7 + after + before + role * after + (1 - role) * before)

    c_transfer = channel()
    send(c_transfer, r.transfer_hbm, r.pair.at[core], partner)
    for b in range(blocks):
        for copy in local_copies(b):
            copy.start()
    own_given.start()
    own_schur.start()

    own_transfer.wait()
    receive(c_transfer, r.pair.at[1 - core])

    def split_pair(step, carry):
        at = pl.ds(pl.multiple_of(step * STRIP, STRIP), STRIP)
        for slot in range(2):
            for part in range(2):
                r.pair_high[slot, part, at, :], r.pair_low[slot, part, at, :] = halves(
                    r.pair[slot, part, at, :]
                )
        return carry

    lax.fori_loop(0, size // STRIP, split_pair, 0)
    first = (r.pair_high.at[0], r.pair_low.at[0])
    second = (r.pair_high.at[1], r.pair_low.at[1])

    def merged_rows(left, at, right):
        rows_high = jnp.concatenate([left[0][0, at, :], left[0][1, at, :]], axis=0)
        rows_low = jnp.concatenate([left[1][0, at, :], left[1][1, at, :]], axis=0)
        out = [dot3((rows_high, rows_low), (right[0][part], right[1][part])) for part in range(2)]
        return out[0][:STRIP] - out[1][STRIP:], out[0][STRIP:] + out[1][:STRIP]

    half = size // 2

    def merge_two(step, carry):
        at = pl.ds(pl.multiple_of(core * half + step * STRIP, STRIP), STRIP)
        to = pl.ds(pl.multiple_of(step * STRIP, STRIP), STRIP)
        merged = merged_rows(second, at, first)
        for part in range(2):
            r.twos[role, core, part, to, :] = merged[part]
        return carry

    lax.fori_loop(0, half // STRIP, merge_two, 0)
    c_half, c_mate, c_pass = channel(), channel(), channel()
    send(c_mate, r.twos.at[role, core], r.twos.at[role, core], mate)
    send(c_half, r.twos.at[role, core], r.twos.at[role, core], partner)

    def combine(real, imag, axis):
        n = real.shape[axis] // 2
        if axis == 1:
            return jnp.concatenate(
                [real[:, :n] - imag[:, n:], real[:, n:] + imag[:, :n]], axis=1
            )
        return jnp.concatenate([real[:n] - imag[n:], real[n:] + imag[:n]], axis=0)

    r.total[...] = jnp.zeros_like(r.total)

    def load_of(b, carry):
        for copy in local_copies(b):
            copy.wait()
        for source, high, low in (
            (r.inverse, r.inverse_high, r.inverse_low),
            (r.coupling, r.coupling_high, r.coupling_low),
        ):
            for part in range(2):
                high[b, part], low[b, part] = halves(source[b, part])

        def product(high, low, right):
            right = halves(right)
            out = [dot3((high[b, part], low[b, part]), right) for part in range(2)]
            return combine(out[0], out[1], 1)

        eliminated = product(
            r.inverse_high, r.inverse_low, jnp.concatenate([r.rhs[b, 0], r.rhs[b, 1]], axis=1)
        )
        r.eliminated[b] = eliminated.T
        weighted = halves(product(r.coupling_high, r.coupling_low, eliminated))
        spread = (lax.broadcasted_iota(jnp.int32, (size, size), 0) == r.rows[b]).astype(BF16)
        r.spread[b] = spread
        r.total[...] += dot(spread, weighted[0]) + dot(spread, weighted[1])
        return carry

    lax.fori_loop(0, blocks, load_of, 0)
    own_given.wait()
    given = jnp.concatenate([r.given[0], r.given[1]], axis=1)
    rest = (jnp.where(sub == 0, given, jnp.zeros_like(given)) - r.total[...]).T
    rest = rest.reshape(2, shots // 8, 8, size)
    r.load[...] = jnp.stack([rest[0], rest[1]], axis=1).reshape(r.load.shape)

    c_x = [[channel() for d in range(3)] for which in range(2)]
    c_z = channel()
    for which in range(2):
        for d in (1, 2, 3):
            group = 2 * ((x + d) % 4) + (1 - far if which == 0 else far)
            send(
                c_x[which][d - 1], r.load.at[group], r.from_x.at[which, d - 1], beside[d - 1]
            )

    own_schur.wait()

    def split_schur(step, carry):
        at = pl.ds(pl.multiple_of(step * STRIP, STRIP), STRIP)
        for part in range(2):
            r.schur_high[part, :, at], r.schur_low[part, :, at] = halves(r.schur[part, at, :].T)
        return carry

    lax.fori_loop(0, size // STRIP, split_schur, 0)

    def side_sum(which, group):
        for d in range(3):
            receive(c_x[which][d], r.from_x.at[which, d])
        return (r.load[group] + r.from_x[which, 0]) + (r.from_x[which, 1] + r.from_x[which, 2])

    r.forward_sum[...] = side_sum(0, other_sub)
    send(c_z, r.forward_sum, r.from_z, opposite)
    own_sum = side_sum(1, sub)

    receive(c_half, r.twos.at[role, 1 - core])

    def split_two(which):
        def step_of(step, carry):
            piece, at = step // 2, pl.ds(pl.multiple_of((step % 2) * STRIP, STRIP), STRIP)
            to = pl.ds(pl.multiple_of(step * STRIP, STRIP), STRIP)
            for part in range(2):
                r.two_high[which, part, to, :], r.two_low[which, part, to, :] = halves(
                    r.twos[which, piece, part, at, :]
                )
            return carry

        lax.fori_loop(0, size // STRIP, step_of, 0)

    split_two(role)
    two_early = (r.two_high.at[0], r.two_low.at[0])
    two_late = (r.two_high.at[1], r.two_low.at[1])
    four = (r.four_high, r.four_low)

    receive(c_z, r.from_z)
    summed = (own_sum + r.from_z[...]).reshape(2, 2, 8, size)
    summed = jnp.stack([summed[:, 0], summed[:, 1]], axis=0).reshape(32, size)
    solved = times(summed, (r.schur_high, r.schur_low), NN).reshape(2, 2, 8, size)
    solved = jnp.stack([solved[:, 0], solved[:, 1]], axis=0).reshape(2, 16, size)
    r.spare[...] = solved
    r.local[core] = r.spare[core]
    c_swap = channel()
    send(c_swap, r.spare.at[1 - core], r.local.at[core], partner)

    @pl.when(jnp.logical_not(has_before))
    def _():
        r.ahead_in[...] = jnp.zeros_like(r.ahead_in)

    @pl.when(jnp.logical_not(has_after))
    def _():
        r.back_in[...] = jnp.zeros_like(r.back_in)

    receive(c_swap, r.local.at[1 - core])
    start = r.local[1] - times(r.local[0], second, NT)
    c_start = channel()
    start_copy = send(c_start, r.start, r.start_in, mate, early)
    r.start[...] = start
    pl.when(early)(start_copy.start)

    receive(c_mate, r.twos.at[1 - role, core])
    send(c_pass, r.twos.at[1 - role, core], r.twos.at[1 - role, core], partner)
    receive(c_pass, r.twos.at[1 - role, 1 - core])
    split_two(1 - role)

    @pl.when(late)
    def _():
        receive(c_start, r.start_in)
        r.start[...] += times(r.start_in[...], two_late, NT)

    @pl.when(jnp.logical_or(has_before, early))
    def _():
        def merge_four(step, carry):
            at = pl.ds(pl.multiple_of(step * STRIP, STRIP), STRIP)
            merged = merged_rows(two_late, at, two_early)

            @pl.when(early)
            def _():
                for part in range(2):
                    r.four_high[part, at, :], r.four_low[part, at, :] = halves(merged[part])

            @pl.when(late)
            def _():
                for part in range(2):
                    r.four_high[part, :, at], r.four_low[part, :, at] = halves(merged[part].T)

            return carry

        lax.fori_loop(0, size // STRIP, merge_four, 0)

    c_late, c_early = channel(), channel()
    goes_on = jnp.logical_and(late, has_after)
    late_copy = send(c_late, r.ahead_out, r.ahead_in, next_late, goes_on)
    early_copy = send(c_early, r.ahead_out, r.ahead_in, next_early, goes_on)

    @pl.when(late)
    def _():
        @pl.when(has_before)
        def _():
            receive(c_late, r.ahead_in)
            r.ahead_out[...] = r.start[...] + times(r.ahead_in[...], four, NN)

        @pl.when(jnp.logical_not(has_before))
        def _():
            r.ahead_out[...] = r.start[...]

        @pl.when(has_after)
        def _():
            late_copy.start()
            early_copy.start()

        r.trace[1] = r.ahead_out[...]
        inner = r.start_in[...] + times(r.ahead_in[...], two_early, NT)
        r.trace[0] = r.local[0] - times(inner, first, NT)

    @pl.when(early)
    def _():
        pl.when(has_before)(lambda: receive(c_early, r.ahead_in))
        r.trace[0] = r.local[0] - times(r.ahead_in[...], first, NT)
        r.trace[1] = r.local[1] - times(r.trace[0], second, NT)

    queued = times(r.trace[0] - times(r.trace[1], second, NN), first, NN)
    r.queued[...] = queued
    c_queued = channel()
    queued_copy = send(c_queued, r.queued, r.queued_in, mate, late)
    pl.when(late)(queued_copy.start)

    c_back_early, c_back_late = channel(), channel()
    goes_back = jnp.logical_and(early, has_before)
    back_early = send(c_back_early, r.back_out, r.back_in, last_early, goes_back)
    back_late = send(c_back_late, r.back_out, r.back_in, last_late, goes_back)

    @pl.when(early)
    def _():
        receive(c_queued, r.queued_in)
        r.queued[...] += times(r.queued_in[...], two_early, NN)

        @pl.when(has_after)
        def _():
            receive(c_back_early, r.back_in)

        @pl.when(has_before)
        def _():
            r.back_out[...] = r.queued[...] + times(r.back_in[...], four, NN)
            back_early.start()
            back_late.start()

        r.carried[...] = r.queued_in[...] + times(r.back_in[...], two_late, NN)

    @pl.when(late)
    def _():
        pl.when(has_after)(lambda: receive(c_back_late, r.back_in))
        r.carried[...] = r.back_in[...]

    r.found[1] = r.trace[1] - r.carried[...]
    r.found[0] = r.trace[0] - times(r.found[1], second, NN)

    c_chip, c_far, c_across = channel(), channel(), channel()
    c_side = [[channel() for d in range(3)] for which in range(2)]
    place = r.gathered.at[sub, core]
    send(c_chip, r.found.at[1 - core], place, partner)
    send(c_far, r.found.at[core], place, opposite)
    send(c_across, r.found.at[1 - core], place, across)
    r.gathered[sub, core] = r.found[core]
    receive(c_chip, r.gathered.at[sub, 1 - core])
    for d in (1, 2, 3):
        send(c_side[0][d - 1], r.gathered.at[sub], r.gathered.at[sub], beside[d - 1])
    receive(c_far, r.gathered.at[other_sub, core])
    receive(c_across, r.gathered.at[other_sub, 1 - core])
    for d in (1, 2, 3):
        send(c_side[1][d - 1], r.gathered.at[other_sub], r.gathered.at[other_sub], beside[d - 1])
    for which in range(2):
        for d in (1, 2, 3):
            group = 2 * ((x + 4 - d) % 4) + (far if which == 0 else 1 - far)
            receive(c_side[which][d - 1], r.gathered.at[group])

    found = r.gathered[...].reshape(shots // 8, 2, 8, size)
    found = jnp.stack([found[:, 0], found[:, 1]], axis=0).reshape(2 * shots, size)
    r.found_high[...], r.found_low[...] = halves(found)
    turned = found.T
    r.separator_out[0] = turned[:, :shots]
    r.separator_out[1] = turned[:, shots:]

    def interior_of(b, carry):
        def product(left, high, low):
            left = halves(left)
            out = [dot3(left, (high[b, part], low[b, part])) for part in range(2)]
            return combine(out[0], out[1], 0)

        spread = r.spread[b]
        picked = dot(r.found_high[...], spread) + dot(r.found_low[...], spread)
        left = r.eliminated[b] - product(picked, r.coupling_high, r.coupling_low)
        turned = product(left, r.inverse_high, r.inverse_low).T
        r.interior_out[b, 0] = turned[:, :shots]
        r.interior_out[b, 1] = turned[:, shots:]
        return carry

    lax.fori_loop(0, blocks, interior_of, 0)

    for copy, when in unsent:
        if when is None:
            copy.wait_send()
        else:
            pl.when(when)(copy.wait_send)


CHANNELS = 32


def body(
    rhs_interior,
    rhs_separator,
    inverse_blocks,
    coupling,
    separator_rows,
    separator_inverse,
    transfer,
):
    _, nb, _, m, shots = rhs_interior.shape
    size = transfer.shape[-1]
    vmem = pltpu.VMEM
    inputs = {
        "rows": separator_rows[0][:, None, :],
        "rhs_hbm": rhs_interior[0],
        "separator_hbm": rhs_separator[0],
        "inverse_hbm": inverse_blocks[0],
        "coupling_hbm": coupling[0],
        "schur_hbm": separator_inverse[0],
        "transfer_hbm": transfer[0],
    }
    outputs = {
        "interior_out": jax.ShapeDtypeStruct((nb, 2, m, shots), F32),
        "separator_out": jax.ShapeDtypeStruct((2, size, shots), F32),
    }
    scratch = {
        "inverse": vmem((nb, 2, m, m), F32),
        "inverse_high": vmem((nb, 2, m, m), BF16),
        "inverse_low": vmem((nb, 2, m, m), BF16),
        "rhs": vmem((nb, 2, m, shots), F32),
        "coupling": vmem((nb, 2, size, m), F32),
        "coupling_high": vmem((nb, 2, size, m), BF16),
        "coupling_low": vmem((nb, 2, size, m), BF16),
        "spread": vmem((nb, size, size), BF16),
        "eliminated": vmem((nb, 2 * shots, m), F32),
        "given": vmem((2, size, shots), F32),
        "total": vmem((size, 2 * shots), F32),
        "load": vmem((8, 32, size), F32),
        "from_x": vmem((2, 3, 32, size), F32),
        "forward_sum": vmem((32, size), F32),
        "from_z": vmem((32, size), F32),
        "schur": vmem((2, size, size), F32),
        "schur_high": vmem((2, size, size), BF16),
        "schur_low": vmem((2, size, size), BF16),
        "pair": vmem((2, 2, size, size), F32),
        "pair_high": vmem((2, 2, size, size), BF16),
        "pair_low": vmem((2, 2, size, size), BF16),
        "twos": vmem((2, 2, 2, size // 2, size), F32),
        "two_high": vmem((2, 2, size, size), BF16),
        "two_low": vmem((2, 2, size, size), BF16),
        "four_high": vmem((2, size, size), BF16),
        "four_low": vmem((2, size, size), BF16),
        "spare": vmem((2, 16, size), F32),
        "local": vmem((2, 16, size), F32),
        "start": vmem((16, size), F32),
        "start_in": vmem((16, size), F32),
        "ahead_in": vmem((16, size), F32),
        "ahead_out": vmem((16, size), F32),
        "trace": vmem((2, 16, size), F32),
        "queued": vmem((16, size), F32),
        "queued_in": vmem((16, size), F32),
        "back_in": vmem((16, size), F32),
        "back_out": vmem((16, size), F32),
        "carried": vmem((16, size), F32),
        "found": vmem((2, 16, size), F32),
        "gathered": vmem((8, 2, 16, size), F32),
        "found_high": vmem((2 * shots, size), BF16),
        "found_low": vmem((2 * shots, size), BF16),
        "send_sem": pltpu.SemaphoreType.DMA((CHANNELS,)),
        "recv_sem": pltpu.SemaphoreType.DMA((CHANNELS,)),
        "here_sem": pltpu.SemaphoreType.DMA((3,)),
        "block_sem": pltpu.SemaphoreType.DMA((3, nb)),
    }
    names = list(inputs) + list(outputs) + list(scratch)

    def sweep_kernel(*refs):
        kernel(names, *refs)

    interior, separator = pl.pallas_call(
        sweep_kernel,
        out_shape=tuple(outputs.values()),
        in_specs=[pl.BlockSpec(memory_space=pltpu.VMEM)]
        + [pl.BlockSpec(memory_space=pl.ANY)] * (len(inputs) - 1),
        out_specs=(pl.BlockSpec(memory_space=pltpu.VMEM),) * 2,
        scratch_shapes=list(scratch.values()),
        compiler_params=pltpu.CompilerParams(
            collective_id=0, has_side_effects=True, vmem_limit_bytes=60 << 20
        ),
    )(*inputs.values())
    return (interior[None], separator[None])


def solution(mesh):
    in_specs = (
        P("slab", "sub", None, None, None),
        P("slab", None, None, None),
        P("slab", "sub", None, None, None),
        P("slab", "sub", None, None, None),
        P("slab", "sub", None),
        P("slab", None, None, None),
        P("slab", None, None, None),
    )
    out_specs = (P("slab", "sub", None, None, None), P("slab", None, None, None))
    return jax.shard_map(body, mesh=mesh, in_specs=in_specs, out_specs=out_specs, check_vma=False)
```

```python
import types

import jax
import jax.numpy as jnp
from jax import lax
from jax.experimental import pallas as pl
from jax.experimental.pallas import tpu as pltpu
from jax.sharding import PartitionSpec as P

MESH = pl.DeviceIdType.MESH
F32 = jnp.float32
BF16 = jnp.bfloat16
NN = (((1,), (0,)), ((), ()))
NT = (((1,), (1,)), ((), ()))
STRIP = 128


def halves(value):
    high = value.astype(BF16)
    return high, (value - high.astype(F32)).astype(BF16)


def dot(left, right, dims=NN):
    return lax.dot_general(left, right, dims, preferred_element_type=F32)


def dot3(left, right):
    return dot(
        jnp.concatenate([left[0], left[0], left[1]], axis=1),
        jnp.concatenate([right[0], right[1], right[0]], axis=0),
    )


def times(value, matrix, dims):
    high, low = matrix
    n = value.shape[0] // 2
    value_high, value_low = halves(value)
    both = jnp.concatenate([value_high, value_low], axis=0)
    out = []
    for part in range(2):
        whole = dot(both, high[part], dims)
        out.append(whole[: 2 * n] + (whole[2 * n :] + dot(value_high, low[part], dims)))
    return jnp.concatenate([out[0][:n] - out[1][n:], out[0][n:] + out[1][:n]], axis=0)


def kernel(names, *refs):
    r = types.SimpleNamespace(**dict(zip(names, refs)))
    slab, sub = lax.axis_index("slab"), lax.axis_index("sub")
    slabs = lax.axis_size("slab")
    core, role, duo = slab % 2, (slab // 2) % 2, slab // 4
    duos = slabs // 4
    x, far = sub // 2, sub % 2
    after, before = (2 * duos - 3 - duo) // (duos - 1), (duo + duos - 2) // (duos - 1)
    has_after, has_before = duo < duos - 1, duo > 0
    early, late = role == 0, role == 1
    blocks, _, size, m = r.coupling_hbm.shape
    shots = r.rhs_hbm.shape[-1]

    other_core, other_sub = slab + 1 - 2 * core, 2 * x + 1 - far
    partner = (other_core, sub)
    opposite = (slab, other_sub)
    across = (other_core, other_sub)
    mate = (slab + 2 - 4 * role, sub)
    beside = [(slab, ((x + d) % 4) * 2 + far) for d in (1, 2, 3)]
    next_late, next_early = ((slab + 4) % slabs, sub), ((slab + 2) % slabs, sub)
    last_early, last_late = ((slab + slabs - 4) % slabs, sub), ((slab + slabs - 2) % slabs, sub)

    count = [0]
    unsent = []

    def remote(index, source, target, device):
        return pltpu.make_async_remote_copy(
            src_ref=source,
            dst_ref=target,
            send_sem=r.send_sem.at[index],
            recv_sem=r.recv_sem.at[index],
            device_id=device,
            device_id_type=MESH,
        )

    def channel():
        count[0] += 1
        return count[0] - 1

    def send(index, source, target, device, when=None):
        copy = remote(index, source, target, device)
        if when is None:
            copy.start()
        unsent.append((copy, when))
        return copy

    def receive(index, target):
        remote(index, target, target, partner).wait_recv()

    def local_copies(b):
        return [
            pltpu.make_async_copy(r.inverse_hbm.at[b], r.inverse.at[b], r.block_sem.at[0, b]),
            pltpu.make_async_copy(r.rhs_hbm.at[b], r.rhs.at[b], r.block_sem.at[1, b]),
            pltpu.make_async_copy(r.coupling_hbm.at[b], r.coupling.at[b], r.block_sem.at[2, b]),
        ]

    own_transfer = pltpu.make_async_copy(r.transfer_hbm, r.pair.at[core], r.here_sem.at[0])
    own_given = pltpu.make_async_copy(r.separator_hbm, r.given, r.here_sem.at[1])
    own_schur = pltpu.make_async_copy(r.schur_hbm, r.schur, r.here_sem.at[2])
    own_transfer.start()

    r.total[...] = jnp.zeros_like(r.total)

    def spread_of(b, carry):
        for i in range(size // STRIP):
            at = slice(i * STRIP, (i + 1) * STRIP)
            place = lax.broadcasted_iota(jnp.int32, (STRIP, size), 0) + i * STRIP
            r.spread[b, at] = (place == r.rows[pl.ds(b, 1), :]).astype(BF16)
        return carry

    barrier = pltpu.get_barrier_semaphore()

    def greet(device):
        pl.semaphore_signal(barrier, inc=1, device_id=device, device_id_type=MESH)

    for device in [partner, opposite, across, mate] + beside:
        greet(device)

    @pl.when(has_after)
    def _():
        greet(next_late)

        @pl.when(late)
        def _():
            greet(next_early)

    @pl.when(has_before)
    def _():
        greet(last_early)

        @pl.when(early)
        def _():
            greet(last_late)

    pl.semaphore_wait(barrier, 7 + after + before + role * after + (1 - role) * before)

    c_transfer = channel()
    send(c_transfer, r.transfer_hbm, r.pair.at[core], partner)
    for b in range(blocks):
        for copy in local_copies(b):
            copy.start()
    own_given.start()
    own_schur.start()

    lax.fori_loop(0, blocks, spread_of, 0)
    own_transfer.wait()
    receive(c_transfer, r.pair.at[1 - core])

    def split_pair(step, carry):
        at = pl.ds(pl.multiple_of(step * STRIP, STRIP), STRIP)
        for slot in range(2):
            for part in range(2):
                r.pair_high[slot, part, at, :], r.pair_low[slot, part, at, :] = halves(
                    r.pair[slot, part, at, :]
                )
        return carry

    lax.fori_loop(0, size // STRIP, split_pair, 0)
    first = (r.pair_high.at[0], r.pair_low.at[0])
    second = (r.pair_high.at[1], r.pair_low.at[1])

    def merged_rows(left, at, right):
        rows_high = jnp.concatenate([left[0][0, at, :], left[0][1, at, :]], axis=0)
        rows_low = jnp.concatenate([left[1][0, at, :], left[1][1, at, :]], axis=0)
        out = [dot3((rows_high, rows_low), (right[0][part], right[1][part])) for part in range(2)]
        return out[0][:STRIP] - out[1][STRIP:], out[0][STRIP:] + out[1][:STRIP]

    half = size // 2
    strips = half // STRIP

    def merge_two(step, carry):
        at = pl.ds(pl.multiple_of(core * half + step * STRIP, STRIP), STRIP)
        merged = merged_rows(second, at, first)
        for part in range(2):
            r.twos[role, strips * core + step, part] = merged[part]
        return carry

    lax.fori_loop(0, half // STRIP, merge_two, 0)
    c_half = channel()
    c_mate, c_pass = [[channel() for i in range(strips)] for j in range(2)]
    halved = r.twos.at[role, pl.ds(strips * core, strips)]
    send(c_half, halved, halved, partner)

    def send_mate(i):
        piece = r.twos.at[role, strips * core + i]
        send(c_mate[i], piece, piece, mate)

    send_mate(0)

    def combine(real, imag, axis):
        n = real.shape[axis] // 2
        if axis == 1:
            return jnp.concatenate(
                [real[:, :n] - imag[:, n:], real[:, n:] + imag[:, :n]], axis=1
            )
        return jnp.concatenate([real[:n] - imag[n:], real[n:] + imag[:n]], axis=0)

    def load_of(b, carry):
        for copy in local_copies(b):
            copy.wait()
        r.rhs_high[...], r.rhs_low[...] = halves(
            jnp.concatenate([r.rhs[b, 0], r.rhs[b, 1]], axis=1)
        )

        def strip(at, source, high, low, right):
            out = []
            for part in range(2):
                left = halves(source[b, part, at])
                high[b, part, at], low[b, part, at] = left
                out.append(dot3(left, right))
            return combine(out[0], out[1], 1)

        for i in range(m // STRIP):
            at = slice(i * STRIP, (i + 1) * STRIP)
            right = (r.rhs_high[...], r.rhs_low[...])
            value = strip(at, r.inverse, r.inverse_high, r.inverse_low, right)
            r.eliminated[b, at] = value
            r.known_high[at], r.known_low[at] = halves(value)
        for i in range(size // STRIP):
            at = slice(i * STRIP, (i + 1) * STRIP)
            right = (r.known_high[...], r.known_low[...])
            value = strip(at, r.coupling, r.coupling_high, r.coupling_low, right)
            r.weighted_high[at], r.weighted_low[at] = halves(value)
        for i in range(size // STRIP):
            at = slice(i * STRIP, (i + 1) * STRIP)
            spread = r.spread[b, at]
            r.total[at] += dot(
                jnp.concatenate([spread, spread], axis=1),
                jnp.concatenate([r.weighted_high[...], r.weighted_low[...]], axis=0),
            )
        return carry

    lax.fori_loop(0, blocks, load_of, 0)
    own_given.wait()
    given = jnp.concatenate([r.given[0], r.given[1]], axis=1)
    rest = (jnp.where(sub == 0, given, jnp.zeros_like(given)) - r.total[...]).T
    rest = rest.reshape(2, shots // 8, 8, size)
    r.load[...] = jnp.stack([rest[0], rest[1]], axis=1).reshape(r.load.shape)

    c_x = [[channel() for d in range(3)] for which in range(2)]
    c_z = channel()
    for which in range(2):
        for d in (1, 2, 3):
            group = 2 * ((x + d) % 4) + (1 - far if which == 0 else far)
            send(
                c_x[which][d - 1], r.load.at[group], r.from_x.at[which, d - 1], beside[d - 1]
            )

    own_schur.wait()

    def split_schur(step, carry):
        at = pl.ds(pl.multiple_of(step * STRIP, STRIP), STRIP)
        for part in range(2):
            r.schur_high[part, :, at], r.schur_low[part, :, at] = halves(r.schur[part, at, :].T)
        return carry

    lax.fori_loop(0, size // STRIP, split_schur, 0)

    def side_sum(which, group):
        for d in range(3):
            receive(c_x[which][d], r.from_x.at[which, d])
        return (r.load[group] + r.from_x[which, 0]) + (r.from_x[which, 1] + r.from_x[which, 2])

    r.forward_sum[...] = side_sum(0, other_sub)
    send(c_z, r.forward_sum, r.from_z, opposite)
    for i in range(1, strips):
        send_mate(i)
    own_sum = side_sum(1, sub)

    receive(c_half, r.twos.at[role, pl.ds(strips * (1 - core), strips)])

    def split_two(which):
        def step_of(step, carry):
            to = pl.ds(pl.multiple_of(step * STRIP, STRIP), STRIP)
            for part in range(2):
                r.two_high[which, part, to, :], r.two_low[which, part, to, :] = halves(
                    r.twos[which, step, part]
                )
            return carry

        lax.fori_loop(0, size // STRIP, step_of, 0)

    split_two(role)
    two_early = (r.two_high.at[0], r.two_low.at[0])
    two_late = (r.two_high.at[1], r.two_low.at[1])
    four = (r.four_high, r.four_low)

    receive(c_z, r.from_z)
    summed = (own_sum + r.from_z[...]).reshape(2, 2, 8, size)
    summed = jnp.stack([summed[:, 0], summed[:, 1]], axis=0).reshape(32, size)
    solved = times(summed, (r.schur_high, r.schur_low), NN).reshape(2, 2, 8, size)
    solved = jnp.stack([solved[:, 0], solved[:, 1]], axis=0).reshape(2, 16, size)
    r.spare[...] = solved
    r.local[core] = r.spare[core]
    c_swap = channel()
    send(c_swap, r.spare.at[1 - core], r.local.at[core], partner)

    @pl.when(jnp.logical_not(has_before))
    def _():
        r.ahead_in[...] = jnp.zeros_like(r.ahead_in)

    @pl.when(jnp.logical_not(has_after))
    def _():
        r.back_in[...] = jnp.zeros_like(r.back_in)

    receive(c_swap, r.local.at[1 - core])
    start = r.local[1] - times(r.local[0], second, NT)
    c_start = channel()
    start_copy = send(c_start, r.start, r.start_in, mate, early)
    r.start[...] = start
    pl.when(early)(start_copy.start)

    c_late, c_early = channel(), channel()
    goes_on = jnp.logical_and(late, has_after)
    late_copy = send(c_late, r.ahead_out, r.ahead_in, next_late, goes_on)
    early_copy = send(c_early, r.ahead_out, r.ahead_in, next_early, goes_on)

    @pl.when(late)
    def _():
        receive(c_start, r.start_in)
        r.start[...] += times(r.start_in[...], two_late, NT)

        @pl.when(jnp.logical_not(has_before))
        def _():
            r.ahead_out[...] = r.start[...]
            late_copy.start()
            early_copy.start()

    for i in range(strips):
        piece = r.twos.at[1 - role, strips * core + i]
        receive(c_mate[i], piece)
        send(c_pass[i], piece, piece, partner)
    for i in range(strips):
        receive(c_pass[i], r.twos.at[1 - role, strips * (1 - core) + i])
    split_two(1 - role)

    @pl.when(has_before)
    def _():
        def merge_four(step, carry):
            at = pl.ds(pl.multiple_of(step * STRIP, STRIP), STRIP)
            merged = merged_rows(two_late, at, two_early)

            @pl.when(early)
            def _():
                for part in range(2):
                    r.four_high[part, at, :], r.four_low[part, at, :] = halves(merged[part])

            @pl.when(late)
            def _():
                for part in range(2):
                    r.four_high[part, :, at], r.four_low[part, :, at] = halves(merged[part].T)

            return carry

        lax.fori_loop(0, size // STRIP, merge_four, 0)

    def weights_of(b, carry):
        spread = r.spread[b]
        for part in range(2):
            r.placed_high[part] = dot(spread, r.coupling_high[b, part]).astype(BF16)
            r.placed_low[part] = dot(spread, r.coupling_low[b, part]).astype(BF16)

        def inverse(part):
            return r.inverse_high[b, part], r.inverse_low[b, part]

        def strip_of(step, carry):
            at = pl.ds(pl.multiple_of(step * STRIP, STRIP), STRIP)
            left = [
                jnp.concatenate([source[0, at, :], source[1, at, :]], axis=0)
                for source in (r.placed_high, r.placed_low)
            ]
            merged = combine(dot3(left, inverse(0)), dot3(left, inverse(1)), 0)
            for part in range(2):
                r.coupling_high[b, part, at, :], r.coupling_low[b, part, at, :] = halves(
                    merged[part * STRIP : (part + 1) * STRIP]
                )
            return carry

        lax.fori_loop(0, size // STRIP, strip_of, 0)
        left = halves(r.eliminated[b].T)
        r.eliminated[b] = combine(dot3(left, inverse(0)), dot3(left, inverse(1)), 0)
        return carry

    towards_end = duo >= duos - 2

    @pl.when(towards_end)
    def _():
        lax.fori_loop(0, blocks, weights_of, 0)

    @pl.when(late)
    def _():
        @pl.when(has_before)
        def _():
            receive(c_late, r.ahead_in)
            r.ahead_out[...] = r.start[...] + times(r.ahead_in[...], four, NN)

            @pl.when(has_after)
            def _():
                late_copy.start()
                early_copy.start()

        r.trace[1] = r.ahead_out[...]
        inner = r.start_in[...] + times(r.ahead_in[...], two_early, NT)
        r.trace[0] = r.local[0] - times(inner, first, NT)

    @pl.when(early)
    def _():
        pl.when(has_before)(lambda: receive(c_early, r.ahead_in))
        r.trace[0] = r.local[0] - times(r.ahead_in[...], first, NT)
        r.trace[1] = r.local[1] - times(r.trace[0], second, NT)

    queued = times(r.trace[0] - times(r.trace[1], second, NN), first, NN)
    r.queued[...] = queued
    c_queued = channel()
    queued_copy = send(c_queued, r.queued, r.queued_in, mate, late)
    pl.when(late)(queued_copy.start)

    @pl.when(jnp.logical_not(towards_end))
    def _():
        lax.fori_loop(0, blocks, weights_of, 0)

    c_back_early, c_back_late = channel(), channel()
    goes_back = jnp.logical_and(early, has_before)
    back_early = send(c_back_early, r.back_out, r.back_in, last_early, goes_back)
    back_late = send(c_back_late, r.back_out, r.back_in, last_late, goes_back)

    @pl.when(early)
    def _():
        receive(c_queued, r.queued_in)
        r.queued[...] += times(r.queued_in[...], two_early, NN)

        @pl.when(has_after)
        def _():
            receive(c_back_early, r.back_in)

        @pl.when(has_before)
        def _():
            r.back_out[...] = r.queued[...] + times(r.back_in[...], four, NN)
            back_early.start()
            back_late.start()

        r.carried[...] = r.queued_in[...] + times(r.back_in[...], two_late, NN)

    @pl.when(late)
    def _():
        pl.when(has_after)(lambda: receive(c_back_late, r.back_in))
        r.carried[...] = r.back_in[...]

    r.found[1] = r.trace[1] - r.carried[...]
    r.found[0] = r.trace[0] - times(r.found[1], second, NN)

    c_chip, c_far, c_across = channel(), channel(), channel()
    c_side = [[channel() for d in range(3)] for which in range(2)]
    place = r.gathered.at[sub, core]
    send(c_chip, r.found.at[1 - core], place, partner)
    send(c_far, r.found.at[core], place, opposite)
    send(c_across, r.found.at[1 - core], place, across)
    r.gathered[sub, core] = r.found[core]
    receive(c_chip, r.gathered.at[sub, 1 - core])
    for d in (1, 2, 3):
        send(c_side[0][d - 1], r.gathered.at[sub], r.gathered.at[sub], beside[d - 1])
    receive(c_far, r.gathered.at[other_sub, core])
    receive(c_across, r.gathered.at[other_sub, 1 - core])
    for d in (1, 2, 3):
        send(c_side[1][d - 1], r.gathered.at[other_sub], r.gathered.at[other_sub], beside[d - 1])
    for which in range(2):
        for d in (1, 2, 3):
            group = 2 * ((x + 4 - d) % 4) + (far if which == 0 else 1 - far)
            receive(c_side[which][d - 1], r.gathered.at[group])

    found = r.gathered[...].reshape(shots // 8, 2, 8, size)
    found = jnp.stack([found[:, 0], found[:, 1]], axis=0).reshape(2 * shots, size)
    r.found_high[...], r.found_low[...] = halves(found)
    turned = found.T
    r.separator_out[0] = turned[:, :shots]
    r.separator_out[1] = turned[:, shots:]

    def interior_of(b, carry):
        left = (r.found_high[...], r.found_low[...])
        out = [
            dot3(left, (r.coupling_high[b, part], r.coupling_low[b, part])) for part in range(2)
        ]
        turned = (r.eliminated[b] - combine(out[0], out[1], 0)).T
        r.interior_out[b, 0] = turned[:, :shots]
        r.interior_out[b, 1] = turned[:, shots:]
        return carry

    lax.fori_loop(0, blocks, interior_of, 0)

    for copy, when in unsent:
        if when is None:
            copy.wait_send()
        else:
            pl.when(when)(copy.wait_send)


CHANNELS = 32


def body(
    rhs_interior,
    rhs_separator,
    inverse_blocks,
    coupling,
    separator_rows,
    separator_inverse,
    transfer,
):
    _, nb, _, m, shots = rhs_interior.shape
    size = transfer.shape[-1]
    vmem = pltpu.VMEM
    inputs = {
        "rows": separator_rows[0],
        "rhs_hbm": rhs_interior[0],
        "separator_hbm": rhs_separator[0],
        "inverse_hbm": inverse_blocks[0],
        "coupling_hbm": coupling[0],
        "schur_hbm": separator_inverse[0],
        "transfer_hbm": transfer[0],
    }
    outputs = {
        "interior_out": jax.ShapeDtypeStruct((nb, 2, m, shots), F32),
        "separator_out": jax.ShapeDtypeStruct((2, size, shots), F32),
    }
    scratch = {
        "inverse": vmem((nb, 2, m, m), F32),
        "inverse_high": vmem((nb, 2, m, m), BF16),
        "inverse_low": vmem((nb, 2, m, m), BF16),
        "rhs": vmem((nb, 2, m, shots), F32),
        "coupling": vmem((nb, 2, size, m), F32),
        "coupling_high": vmem((nb, 2, size, m), BF16),
        "coupling_low": vmem((nb, 2, size, m), BF16),
        "spread": vmem((nb, size, size), BF16),
        "placed_high": vmem((2, size, m), BF16),
        "placed_low": vmem((2, size, m), BF16),
        "eliminated": vmem((nb, m, 2 * shots), F32),
        "rhs_high": vmem((m, 2 * shots), BF16),
        "rhs_low": vmem((m, 2 * shots), BF16),
        "known_high": vmem((m, 2 * shots), BF16),
        "known_low": vmem((m, 2 * shots), BF16),
        "weighted_high": vmem((size, 2 * shots), BF16),
        "weighted_low": vmem((size, 2 * shots), BF16),
        "given": vmem((2, size, shots), F32),
        "total": vmem((size, 2 * shots), F32),
        "load": vmem((8, 32, size), F32),
        "from_x": vmem((2, 3, 32, size), F32),
        "forward_sum": vmem((32, size), F32),
        "from_z": vmem((32, size), F32),
        "schur": vmem((2, size, size), F32),
        "schur_high": vmem((2, size, size), BF16),
        "schur_low": vmem((2, size, size), BF16),
        "pair": vmem((2, 2, size, size), F32),
        "pair_high": vmem((2, 2, size, size), BF16),
        "pair_low": vmem((2, 2, size, size), BF16),
        "twos": vmem((2, size // STRIP, 2, STRIP, size), F32),
        "two_high": vmem((2, 2, size, size), BF16),
        "two_low": vmem((2, 2, size, size), BF16),
        "four_high": vmem((2, size, size), BF16),
        "four_low": vmem((2, size, size), BF16),
        "spare": vmem((2, 16, size), F32),
        "local": vmem((2, 16, size), F32),
        "start": vmem((16, size), F32),
        "start_in": vmem((16, size), F32),
        "ahead_in": vmem((16, size), F32),
        "ahead_out": vmem((16, size), F32),
        "trace": vmem((2, 16, size), F32),
        "queued": vmem((16, size), F32),
        "queued_in": vmem((16, size), F32),
        "back_in": vmem((16, size), F32),
        "back_out": vmem((16, size), F32),
        "carried": vmem((16, size), F32),
        "found": vmem((2, 16, size), F32),
        "gathered": vmem((8, 2, 16, size), F32),
        "found_high": vmem((2 * shots, size), BF16),
        "found_low": vmem((2 * shots, size), BF16),
        "send_sem": pltpu.SemaphoreType.DMA((CHANNELS,)),
        "recv_sem": pltpu.SemaphoreType.DMA((CHANNELS,)),
        "here_sem": pltpu.SemaphoreType.DMA((3,)),
        "block_sem": pltpu.SemaphoreType.DMA((3, nb)),
    }
    names = list(inputs) + list(outputs) + list(scratch)

    def sweep_kernel(*refs):
        kernel(names, *refs)

    interior, separator = pl.pallas_call(
        sweep_kernel,
        out_shape=tuple(outputs.values()),
        in_specs=[pl.BlockSpec(memory_space=pltpu.VMEM)]
        + [pl.BlockSpec(memory_space=pltpu.HBM)] * (len(inputs) - 1),
        out_specs=(pl.BlockSpec(memory_space=pltpu.VMEM),) * 2,
        scratch_shapes=list(scratch.values()),
        compiler_params=pltpu.CompilerParams(
            collective_id=0, has_side_effects=True, vmem_limit_bytes=61 << 20
        ),
    )(*inputs.values())
    return (interior[None], separator[None])


def solution(mesh):
    in_specs = (
        P("slab", "sub", None, None, None),
        P("slab", None, None, None),
        P("slab", "sub", None, None, None),
        P("slab", "sub", None, None, None),
        P("slab", "sub", None),
        P("slab", None, None, None),
        P("slab", None, None, None),
    )
    out_specs = (P("slab", "sub", None, None, None), P("slab", None, None, None))
    return jax.shard_map(body, mesh=mesh, in_specs=in_specs, out_specs=out_specs, check_vma=False)
```

```python
import types

import jax
import jax.numpy as jnp
from jax import lax
from jax.experimental import pallas as pl
from jax.experimental.pallas import tpu as pltpu
from jax.sharding import PartitionSpec as P

MESH = pl.DeviceIdType.MESH
F32 = jnp.float32
BF16 = jnp.bfloat16
NN = (((1,), (0,)), ((), ()))
NT = (((1,), (1,)), ((), ()))
STRIP = 128


def halves(value):
    high = value.astype(BF16)
    return high, (value - high.astype(F32)).astype(BF16)


def dot(left, right, dims=NN):
    return lax.dot_general(left, right, dims, preferred_element_type=F32)


def dot3(left, right):
    return dot(
        jnp.concatenate([left[0], left[0], left[1]], axis=1),
        jnp.concatenate([right[0], right[1], right[0]], axis=0),
    )


def times(value, matrix, dims):
    high, low = matrix
    n = value.shape[0] // 2
    value_high, value_low = halves(value)
    both = jnp.concatenate([value_high, value_low], axis=0)
    out = []
    for part in range(2):
        whole = dot(both, high[part], dims)
        out.append(whole[: 2 * n] + (whole[2 * n :] + dot(value_high, low[part], dims)))
    return jnp.concatenate([out[0][:n] - out[1][n:], out[0][n:] + out[1][:n]], axis=0)


def kernel(names, *refs):
    r = types.SimpleNamespace(**dict(zip(names, refs)))
    slab, sub = lax.axis_index("slab"), lax.axis_index("sub")
    slabs = lax.axis_size("slab")
    core, role, duo = slab % 2, (slab // 2) % 2, slab // 4
    duos = slabs // 4
    x, far = sub // 2, sub % 2
    after, before = (2 * duos - 3 - duo) // (duos - 1), (duo + duos - 2) // (duos - 1)
    has_after, has_before = duo < duos - 1, duo > 0
    early, late = role == 0, role == 1
    row, upper = duo // 2, duo % 2
    rows = duos // 2
    row_after, row_before = (2 * rows - 3 - row) // (rows - 1), (row + rows - 2) // (rows - 1)
    has_row_after, has_row_before = row < rows - 1, row > 0
    leads = jnp.logical_and(early, upper == 0)
    helps = jnp.logical_and(early, upper == 1)
    blocks, _, size, m = r.coupling_hbm.shape
    shots = r.rhs_hbm.shape[-1]

    other_core, other_sub = slab + 1 - 2 * core, 2 * x + 1 - far
    partner = (other_core, sub)
    opposite = (slab, other_sub)
    across = (other_core, other_sub)
    mate = (slab + 2 - 4 * role, sub)
    beside = [(slab, ((x + d) % 4) * 2 + far) for d in (1, 2, 3)]
    next_late, next_early = ((slab + 4) % slabs, sub), ((slab + 2) % slabs, sub)
    last_early, last_late = ((slab + slabs - 4) % slabs, sub), ((slab + slabs - 2) % slabs, sub)
    next_lead, last_lead = ((slab + 8) % slabs, sub), ((slab + slabs - 8) % slabs, sub)

    count = [0]
    unsent = []

    def remote(index, source, target, device):
        return pltpu.make_async_remote_copy(
            src_ref=source,
            dst_ref=target,
            send_sem=r.send_sem.at[index],
            recv_sem=r.recv_sem.at[index],
            device_id=device,
            device_id_type=MESH,
        )

    def channel():
        count[0] += 1
        return count[0] - 1

    def send(index, source, target, device, when=None):
        copy = remote(index, source, target, device)
        if when is None:
            copy.start()
        unsent.append((copy, when))
        return copy

    def receive(index, target):
        remote(index, target, target, partner).wait_recv()

    def local_copies(b):
        return [
            pltpu.make_async_copy(r.inverse_hbm.at[b], r.inverse.at[b], r.block_sem.at[0, b]),
            pltpu.make_async_copy(r.rhs_hbm.at[b], r.rhs.at[b], r.block_sem.at[1, b]),
            pltpu.make_async_copy(r.coupling_hbm.at[b], r.coupling.at[b], r.block_sem.at[2, b]),
        ]

    own_transfer = pltpu.make_async_copy(r.transfer_hbm, r.pair.at[core], r.here_sem.at[0])
    own_given = pltpu.make_async_copy(r.separator_hbm, r.given, r.here_sem.at[1])
    own_schur = pltpu.make_async_copy(r.schur_hbm, r.schur, r.here_sem.at[2])
    own_transfer.start()

    r.total[...] = jnp.zeros_like(r.total)

    def spread_of(b, carry):
        for i in range(size // STRIP):
            at = slice(i * STRIP, (i + 1) * STRIP)
            place = lax.broadcasted_iota(jnp.int32, (STRIP, size), 0) + i * STRIP
            r.spread[b, at] = (place == r.rows[pl.ds(b, 1), :]).astype(BF16)
        return carry

    barrier = pltpu.get_barrier_semaphore()

    def greet(device):
        pl.semaphore_signal(barrier, inc=1, device_id=device, device_id_type=MESH)

    for device in [partner, opposite, across, mate] + beside:
        greet(device)

    @pl.when(has_after)
    def _():
        greet(next_late)

        @pl.when(late)
        def _():
            greet(next_early)

    @pl.when(has_before)
    def _():
        greet(last_early)

        @pl.when(early)
        def _():
            greet(last_late)

    @pl.when(jnp.logical_and(leads, has_row_after))
    def _():
        greet(next_lead)

    @pl.when(jnp.logical_and(leads, has_row_before))
    def _():
        greet(last_lead)

    pl.semaphore_wait(
        barrier,
        7
        + after
        + before
        + role * after
        + (1 - role) * before
        + (1 - role) * (1 - upper) * (row_after + row_before),
    )

    c_transfer = channel()
    send(c_transfer, r.transfer_hbm, r.pair.at[core], partner)
    for b in range(blocks):
        for copy in local_copies(b):
            copy.start()
    own_given.start()
    own_schur.start()

    lax.fori_loop(0, blocks, spread_of, 0)
    own_transfer.wait()
    receive(c_transfer, r.pair.at[1 - core])

    def split_pair(step, carry):
        at = pl.ds(pl.multiple_of(step * STRIP, STRIP), STRIP)
        for slot in range(2):
            for part in range(2):
                r.pair_high[slot, part, at, :], r.pair_low[slot, part, at, :] = halves(
                    r.pair[slot, part, at, :]
                )
        return carry

    lax.fori_loop(0, size // STRIP, split_pair, 0)
    first = (r.pair_high.at[0], r.pair_low.at[0])
    second = (r.pair_high.at[1], r.pair_low.at[1])

    def merged_rows(left, at, right):
        rows_high = jnp.concatenate([left[0][0, at, :], left[0][1, at, :]], axis=0)
        rows_low = jnp.concatenate([left[1][0, at, :], left[1][1, at, :]], axis=0)
        out = [dot3((rows_high, rows_low), (right[0][part], right[1][part])) for part in range(2)]
        return out[0][:STRIP] - out[1][STRIP:], out[0][STRIP:] + out[1][:STRIP]

    half = size // 2
    strips = half // STRIP

    def merge_two(step, carry):
        at = pl.ds(pl.multiple_of(core * half + step * STRIP, STRIP), STRIP)
        merged = merged_rows(second, at, first)
        for part in range(2):
            r.twos[role, strips * core + step, part] = merged[part]
        return carry

    lax.fori_loop(0, half // STRIP, merge_two, 0)
    c_half = channel()
    c_mate, c_pass = [[channel() for i in range(strips)] for j in range(2)]
    halved = r.twos.at[role, pl.ds(strips * core, strips)]
    send(c_half, halved, halved, partner)

    def send_mate(i):
        piece = r.twos.at[role, strips * core + i]
        send(c_mate[i], piece, piece, mate)

    send_mate(0)

    def combine(real, imag, axis):
        n = real.shape[axis] // 2
        if axis == 1:
            return jnp.concatenate(
                [real[:, :n] - imag[:, n:], real[:, n:] + imag[:, :n]], axis=1
            )
        return jnp.concatenate([real[:n] - imag[n:], real[n:] + imag[:n]], axis=0)

    def load_of(b, carry):
        for copy in local_copies(b):
            copy.wait()
        r.rhs_high[...], r.rhs_low[...] = halves(
            jnp.concatenate([r.rhs[b, 0], r.rhs[b, 1]], axis=1)
        )

        def strip(at, source, high, low, right):
            out = []
            for part in range(2):
                left = halves(source[b, part, at])
                high[b, part, at], low[b, part, at] = left
                out.append(dot3(left, right))
            return combine(out[0], out[1], 1)

        for i in range(m // STRIP):
            at = slice(i * STRIP, (i + 1) * STRIP)
            right = (r.rhs_high[...], r.rhs_low[...])
            value = strip(at, r.inverse, r.inverse_high, r.inverse_low, right)
            r.eliminated[b, at] = value
            r.known_high[at], r.known_low[at] = halves(value)
        for i in range(size // STRIP):
            at = slice(i * STRIP, (i + 1) * STRIP)
            right = (r.known_high[...], r.known_low[...])
            value = strip(at, r.coupling, r.coupling_high, r.coupling_low, right)
            r.weighted_high[at], r.weighted_low[at] = halves(value)
        for i in range(size // STRIP):
            at = slice(i * STRIP, (i + 1) * STRIP)
            spread = r.spread[b, at]
            r.total[at] += dot(
                jnp.concatenate([spread, spread], axis=1),
                jnp.concatenate([r.weighted_high[...], r.weighted_low[...]], axis=0),
            )
        return carry

    lax.fori_loop(0, blocks, load_of, 0)
    own_given.wait()
    given = jnp.concatenate([r.given[0], r.given[1]], axis=1)
    rest = (jnp.where(sub == 0, given, jnp.zeros_like(given)) - r.total[...]).T
    rest = rest.reshape(2, shots // 8, 8, size)
    r.load[...] = jnp.stack([rest[0], rest[1]], axis=1).reshape(r.load.shape)

    c_x = [[channel() for d in range(3)] for which in range(2)]
    c_z = channel()
    for which in range(2):
        for d in (1, 2, 3):
            group = 2 * ((x + d) % 4) + (1 - far if which == 0 else far)
            send(
                c_x[which][d - 1], r.load.at[group], r.from_x.at[which, d - 1], beside[d - 1]
            )

    own_schur.wait()

    def split_schur(step, carry):
        at = pl.ds(pl.multiple_of(step * STRIP, STRIP), STRIP)
        for part in range(2):
            r.schur_high[part, :, at], r.schur_low[part, :, at] = halves(r.schur[part, at, :].T)
        return carry

    lax.fori_loop(0, size // STRIP, split_schur, 0)

    def side_sum(which, group):
        for d in range(3):
            receive(c_x[which][d], r.from_x.at[which, d])
        return (r.load[group] + r.from_x[which, 0]) + (r.from_x[which, 1] + r.from_x[which, 2])

    r.forward_sum[...] = side_sum(0, other_sub)
    send(c_z, r.forward_sum, r.from_z, opposite)
    for i in range(1, strips):
        send_mate(i)
    own_sum = side_sum(1, sub)

    receive(c_half, r.twos.at[role, pl.ds(strips * (1 - core), strips)])

    def split_two(which):
        def step_of(step, carry):
            to = pl.ds(pl.multiple_of(step * STRIP, STRIP), STRIP)
            for part in range(2):
                r.two_high[which, part, to, :], r.two_low[which, part, to, :] = halves(
                    r.twos[which, step, part]
                )
            return carry

        lax.fori_loop(0, size // STRIP, step_of, 0)

    split_two(role)
    two_early = (r.two_high.at[0], r.two_low.at[0])
    two_late = (r.two_high.at[1], r.two_low.at[1])
    four = (r.four_high, r.four_low)

    receive(c_z, r.from_z)
    summed = (own_sum + r.from_z[...]).reshape(2, 2, 8, size)
    summed = jnp.stack([summed[:, 0], summed[:, 1]], axis=0).reshape(32, size)
    solved = times(summed, (r.schur_high, r.schur_low), NN).reshape(2, 2, 8, size)
    solved = jnp.stack([solved[:, 0], solved[:, 1]], axis=0).reshape(2, 16, size)
    r.spare[...] = solved
    r.local[core] = r.spare[core]
    c_swap = channel()
    send(c_swap, r.spare.at[1 - core], r.local.at[core], partner)

    @pl.when(jnp.logical_not(has_before))
    def _():
        r.ahead_in[...] = jnp.zeros_like(r.ahead_in)

    @pl.when(jnp.logical_not(has_after))
    def _():
        r.back_in[...] = jnp.zeros_like(r.back_in)

    receive(c_swap, r.local.at[1 - core])
    start = r.local[1] - times(r.local[0], second, NT)
    c_start = channel()
    start_copy = send(c_start, r.start, r.start_in, mate, early)
    r.start[...] = start
    pl.when(early)(start_copy.start)

    c_late, c_early = channel(), channel()
    goes_on = jnp.logical_and(late, has_after)
    late_copy = send(c_late, r.ahead_out, r.ahead_in, next_late, goes_on)
    early_copy = send(c_early, r.ahead_out, r.ahead_in, next_early, goes_on)

    @pl.when(late)
    def _():
        receive(c_start, r.start_in)
        r.start[...] += times(r.start_in[...], two_late, NT)

        @pl.when(jnp.logical_not(has_before))
        def _():
            r.ahead_out[...] = r.start[...]
            late_copy.start()
            early_copy.start()

    for i in range(strips):
        piece = r.twos.at[1 - role, strips * core + i]
        receive(c_mate[i], piece)
        send(c_pass[i], piece, piece, partner)
    for i in range(strips):
        receive(c_pass[i], r.twos.at[1 - role, strips * (1 - core) + i])
    split_two(1 - role)

    @pl.when(jnp.logical_and(duo > 1, jnp.logical_or(late, upper == 0)))
    def _():
        def merge_four(step, carry):
            at = pl.ds(pl.multiple_of(step * STRIP, STRIP), STRIP)
            merged = merged_rows(two_late, at, two_early)

            @pl.when(early)
            def _():
                for part in range(2):
                    r.four_high[part, at, :], r.four_low[part, at, :] = halves(merged[part])

            @pl.when(late)
            def _():
                for part in range(2):
                    r.four_high[part, :, at], r.four_low[part, :, at] = halves(merged[part].T)

            return carry

        lax.fori_loop(0, size // STRIP, merge_four, 0)

    gives = jnp.logical_and(helps, has_row_after)
    takes = jnp.logical_and(leads, has_row_after)
    c_four, c_four_pass = channel(), channel()
    half_four = pl.ds(strips * core, strips)
    four_copy = send(c_four, r.four_out, r.four_in.at[half_four], last_early, gives)

    @pl.when(gives)
    def _():
        def merge_half(step, carry):
            at = pl.ds(pl.multiple_of(core * half + step * STRIP, STRIP), STRIP)
            merged = merged_rows(two_late, at, two_early)
            for part in range(2):
                r.four_out[step, part] = merged[part]
            return carry

        lax.fori_loop(0, strips, merge_half, 0)
        four_copy.start()

    def weights_of(b, carry):
        spread = r.spread[b]
        for part in range(2):
            r.placed_high[part] = dot(spread, r.coupling_high[b, part]).astype(BF16)
            r.placed_low[part] = dot(spread, r.coupling_low[b, part]).astype(BF16)

        def inverse(part):
            return r.inverse_high[b, part], r.inverse_low[b, part]

        def strip_of(step, carry):
            at = pl.ds(pl.multiple_of(step * STRIP, STRIP), STRIP)
            left = [
                jnp.concatenate([source[0, at, :], source[1, at, :]], axis=0)
                for source in (r.placed_high, r.placed_low)
            ]
            merged = combine(dot3(left, inverse(0)), dot3(left, inverse(1)), 0)
            for part in range(2):
                r.coupling_high[b, part, at, :], r.coupling_low[b, part, at, :] = halves(
                    merged[part * STRIP : (part + 1) * STRIP]
                )
            return carry

        lax.fori_loop(0, size // STRIP, strip_of, 0)
        left = halves(r.eliminated[b].T)
        r.eliminated[b] = combine(dot3(left, inverse(0)), dot3(left, inverse(1)), 0)
        return carry

    towards_end = duo >= duos - 2

    @pl.when(towards_end)
    def _():
        lax.fori_loop(0, blocks, weights_of, 0)

    @pl.when(late)
    def _():
        @pl.when(has_before)
        def _():
            receive(c_late, r.ahead_in)

            @pl.when(duo > 1)
            def _():
                r.ahead_out[...] = r.start[...] + times(r.ahead_in[...], four, NN)

            @pl.when(duo == 1)
            def _():
                r.ahead_out[...] = r.start[...] + times(
                    times(r.ahead_in[...], two_early, NT), two_late, NT
                )

            @pl.when(has_after)
            def _():
                late_copy.start()
                early_copy.start()

        r.trace[1] = r.ahead_out[...]
        inner = r.start_in[...] + times(r.ahead_in[...], two_early, NT)
        r.trace[0] = r.local[0] - times(inner, first, NT)

    @pl.when(early)
    def _():
        pl.when(has_before)(lambda: receive(c_early, r.ahead_in))
        r.trace[0] = r.local[0] - times(r.ahead_in[...], first, NT)
        r.trace[1] = r.local[1] - times(r.trace[0], second, NT)

    queued = times(r.trace[0] - times(r.trace[1], second, NN), first, NN)
    r.queued[...] = queued
    c_queued = channel()
    queued_copy = send(c_queued, r.queued, r.queued_in, mate, late)
    pl.when(late)(queued_copy.start)

    @pl.when(jnp.logical_not(towards_end))
    def _():
        lax.fori_loop(0, blocks, weights_of, 0)

    c_upper, c_lower, c_lead, c_help, c_back_late = [channel() for i in range(5)]
    goes_back = jnp.logical_and(leads, has_row_before)
    upper_copy = send(c_upper, r.queued, r.upper_in, last_early, helps)
    lower_copy = send(c_lower, r.lower, r.lower_in, mate, leads)
    back_lead = send(c_lead, r.back_out, r.back_in, last_lead, goes_back)
    back_help = send(c_help, r.back_out, r.back_in, last_early, goes_back)
    back_late = send(c_back_late, r.back_out, r.back_in, last_late, goes_back)
    pass_copy = send(
        c_four_pass, r.four_in.at[half_four], r.four_in.at[half_four], partner, takes
    )
    top = (r.top_high, r.top_low)

    @pl.when(early)
    def _():
        receive(c_queued, r.queued_in)
        r.queued[...] += times(r.queued_in[...], two_early, NN)

    @pl.when(helps)
    def _():
        upper_copy.start()
        pl.when(has_row_after)(lambda: receive(c_help, r.back_in))
        r.carried[...] = r.queued_in[...] + times(r.back_in[...], two_late, NN)

    @pl.when(leads)
    def _():
        @pl.when(has_row_after)
        def _():
            receive(c_four, r.four_in.at[half_four])
            pass_copy.start()
            receive(c_four_pass, r.four_in.at[pl.ds(strips * (1 - core), strips)])

            def split_top(step, carry):
                to = pl.ds(pl.multiple_of(step * STRIP, STRIP), STRIP)
                for part in range(2):
                    r.top_high[part, to, :], r.top_low[part, to, :] = halves(r.four_in[step, part])
                return carry

            lax.fori_loop(0, size // STRIP, split_top, 0)

        receive(c_upper, r.upper_in)

        @pl.when(has_row_after)
        def _():
            receive(c_lead, r.back_in)
            r.lower[...] = r.upper_in[...] + times(r.back_in[...], top, NN)

        @pl.when(jnp.logical_not(has_row_after))
        def _():
            r.lower[...] = r.upper_in[...]

        lower_copy.start()

        @pl.when(has_row_before)
        def _():
            r.back_out[...] = r.queued[...] + times(r.lower[...], four, NN)
            back_lead.start()
            back_help.start()
            back_late.start()

        r.carried[...] = r.queued_in[...] + times(r.lower[...], two_late, NN)

    @pl.when(jnp.logical_and(late, upper == 1))
    def _():
        pl.when(has_row_after)(lambda: receive(c_back_late, r.back_in))
        r.carried[...] = r.back_in[...]

    @pl.when(jnp.logical_and(late, upper == 0))
    def _():
        receive(c_lower, r.lower_in)
        r.carried[...] = r.lower_in[...]

    r.found[1] = r.trace[1] - r.carried[...]
    r.found[0] = r.trace[0] - times(r.found[1], second, NN)

    c_chip, c_far, c_across = channel(), channel(), channel()
    c_side = [[channel() for d in range(3)] for which in range(2)]
    place = r.gathered.at[sub, core]
    send(c_chip, r.found.at[1 - core], place, partner)
    send(c_far, r.found.at[core], place, opposite)
    send(c_across, r.found.at[1 - core], place, across)
    r.gathered[sub, core] = r.found[core]
    receive(c_chip, r.gathered.at[sub, 1 - core])
    for d in (1, 2, 3):
        send(c_side[0][d - 1], r.gathered.at[sub], r.gathered.at[sub], beside[d - 1])
    receive(c_far, r.gathered.at[other_sub, core])
    receive(c_across, r.gathered.at[other_sub, 1 - core])
    for d in (1, 2, 3):
        send(c_side[1][d - 1], r.gathered.at[other_sub], r.gathered.at[other_sub], beside[d - 1])
    for which in range(2):
        for d in (1, 2, 3):
            group = 2 * ((x + 4 - d) % 4) + (far if which == 0 else 1 - far)
            receive(c_side[which][d - 1], r.gathered.at[group])

    found = r.gathered[...].reshape(shots // 8, 2, 8, size)
    found = jnp.stack([found[:, 0], found[:, 1]], axis=0).reshape(2 * shots, size)
    r.found_high[...], r.found_low[...] = halves(found)
    turned = found.T
    r.separator_out[0] = turned[:, :shots]
    r.separator_out[1] = turned[:, shots:]

    def interior_of(b, carry):
        left = (r.found_high[...], r.found_low[...])
        out = [
            dot3(left, (r.coupling_high[b, part], r.coupling_low[b, part])) for part in range(2)
        ]
        turned = (r.eliminated[b] - combine(out[0], out[1], 0)).T
        r.interior_out[b, 0] = turned[:, :shots]
        r.interior_out[b, 1] = turned[:, shots:]
        return carry

    lax.fori_loop(0, blocks, interior_of, 0)

    for copy, when in unsent:
        if when is None:
            copy.wait_send()
        else:
            pl.when(when)(copy.wait_send)


CHANNELS = 40


def body(
    rhs_interior,
    rhs_separator,
    inverse_blocks,
    coupling,
    separator_rows,
    separator_inverse,
    transfer,
):
    _, nb, _, m, shots = rhs_interior.shape
    size = transfer.shape[-1]
    vmem = pltpu.VMEM
    inputs = {
        "rows": separator_rows[0],
        "rhs_hbm": rhs_interior[0],
        "separator_hbm": rhs_separator[0],
        "inverse_hbm": inverse_blocks[0],
        "coupling_hbm": coupling[0],
        "schur_hbm": separator_inverse[0],
        "transfer_hbm": transfer[0],
    }
    outputs = {
        "interior_out": jax.ShapeDtypeStruct((nb, 2, m, shots), F32),
        "separator_out": jax.ShapeDtypeStruct((2, size, shots), F32),
    }
    scratch = {
        "inverse": vmem((nb, 2, m, m), F32),
        "inverse_high": vmem((nb, 2, m, m), BF16),
        "inverse_low": vmem((nb, 2, m, m), BF16),
        "rhs": vmem((nb, 2, m, shots), F32),
        "coupling": vmem((nb, 2, size, m), F32),
        "coupling_high": vmem((nb, 2, size, m), BF16),
        "coupling_low": vmem((nb, 2, size, m), BF16),
        "spread": vmem((nb, size, size), BF16),
        "placed_high": vmem((2, size, m), BF16),
        "placed_low": vmem((2, size, m), BF16),
        "eliminated": vmem((nb, m, 2 * shots), F32),
        "rhs_high": vmem((m, 2 * shots), BF16),
        "rhs_low": vmem((m, 2 * shots), BF16),
        "known_high": vmem((m, 2 * shots), BF16),
        "known_low": vmem((m, 2 * shots), BF16),
        "weighted_high": vmem((size, 2 * shots), BF16),
        "weighted_low": vmem((size, 2 * shots), BF16),
        "given": vmem((2, size, shots), F32),
        "total": vmem((size, 2 * shots), F32),
        "load": vmem((8, 32, size), F32),
        "from_x": vmem((2, 3, 32, size), F32),
        "forward_sum": vmem((32, size), F32),
        "from_z": vmem((32, size), F32),
        "schur": vmem((2, size, size), F32),
        "schur_high": vmem((2, size, size), BF16),
        "schur_low": vmem((2, size, size), BF16),
        "pair": vmem((2, 2, size, size), F32),
        "pair_high": vmem((2, 2, size, size), BF16),
        "pair_low": vmem((2, 2, size, size), BF16),
        "twos": vmem((2, size // STRIP, 2, STRIP, size), F32),
        "two_high": vmem((2, 2, size, size), BF16),
        "two_low": vmem((2, 2, size, size), BF16),
        "four_high": vmem((2, size, size), BF16),
        "four_low": vmem((2, size, size), BF16),
        "four_out": vmem((size // STRIP // 2, 2, STRIP, size), F32),
        "four_in": vmem((size // STRIP, 2, STRIP, size), F32),
        "top_high": vmem((2, size, size), BF16),
        "top_low": vmem((2, size, size), BF16),
        "upper_in": vmem((16, size), F32),
        "lower": vmem((16, size), F32),
        "lower_in": vmem((16, size), F32),
        "spare": vmem((2, 16, size), F32),
        "local": vmem((2, 16, size), F32),
        "start": vmem((16, size), F32),
        "start_in": vmem((16, size), F32),
        "ahead_in": vmem((16, size), F32),
        "ahead_out": vmem((16, size), F32),
        "trace": vmem((2, 16, size), F32),
        "queued": vmem((16, size), F32),
        "queued_in": vmem((16, size), F32),
        "back_in": vmem((16, size), F32),
        "back_out": vmem((16, size), F32),
        "carried": vmem((16, size), F32),
        "found": vmem((2, 16, size), F32),
        "gathered": vmem((8, 2, 16, size), F32),
        "found_high": vmem((2 * shots, size), BF16),
        "found_low": vmem((2 * shots, size), BF16),
        "send_sem": pltpu.SemaphoreType.DMA((CHANNELS,)),
        "recv_sem": pltpu.SemaphoreType.DMA((CHANNELS,)),
        "here_sem": pltpu.SemaphoreType.DMA((3,)),
        "block_sem": pltpu.SemaphoreType.DMA((3, nb)),
    }
    names = list(inputs) + list(outputs) + list(scratch)

    def sweep_kernel(*refs):
        kernel(names, *refs)

    interior, separator = pl.pallas_call(
        sweep_kernel,
        out_shape=tuple(outputs.values()),
        in_specs=[pl.BlockSpec(memory_space=pltpu.VMEM)]
        + [pl.BlockSpec(memory_space=pltpu.HBM)] * (len(inputs) - 1),
        out_specs=(pl.BlockSpec(memory_space=pltpu.VMEM),) * 2,
        scratch_shapes=list(scratch.values()),
        compiler_params=pltpu.CompilerParams(
            collective_id=0, has_side_effects=True, vmem_limit_bytes=61 << 20
        ),
    )(*inputs.values())
    return (interior[None], separator[None])


def solution(mesh):
    in_specs = (
        P("slab", "sub", None, None, None),
        P("slab", None, None, None),
        P("slab", "sub", None, None, None),
        P("slab", "sub", None, None, None),
        P("slab", "sub", None),
        P("slab", None, None, None),
        P("slab", None, None, None),
    )
    out_specs = (P("slab", "sub", None, None, None), P("slab", None, None, None))
    return jax.shard_map(body, mesh=mesh, in_specs=in_specs, out_specs=out_specs, check_vma=False)
```

```python
import types

import jax
import jax.numpy as jnp
from jax import lax
from jax.experimental import pallas as pl
from jax.experimental.pallas import tpu as pltpu
from jax.sharding import PartitionSpec as P

MESH = pl.DeviceIdType.MESH
F32 = jnp.float32
BF16 = jnp.bfloat16
NN = (((1,), (0,)), ((), ()))
NT = (((1,), (1,)), ((), ()))
STRIP = 128


def halves(value):
    high = value.astype(BF16)
    return high, (value - high.astype(F32)).astype(BF16)


def dot(left, right, dims=NN):
    return lax.dot_general(left, right, dims, preferred_element_type=F32)


def dot3(left, right):
    return dot(
        jnp.concatenate([left[0], left[0], left[1]], axis=1),
        jnp.concatenate([right[0], right[1], right[0]], axis=0),
    )


def times(value, matrix, dims):
    high, low = matrix
    n = value.shape[0] // 2
    value_high, value_low = halves(value)
    both = jnp.concatenate([value_high, value_low], axis=0)
    out = []
    for part in range(2):
        whole = dot(both, high[part], dims)
        out.append(whole[: 2 * n] + (whole[2 * n :] + dot(value_high, low[part], dims)))
    return jnp.concatenate([out[0][:n] - out[1][n:], out[0][n:] + out[1][:n]], axis=0)


def kernel(names, *refs):
    r = types.SimpleNamespace(**dict(zip(names, refs)))
    slab, sub = lax.axis_index("slab"), lax.axis_index("sub")
    slabs = lax.axis_size("slab")
    core, role, duo = slab % 2, (slab // 2) % 2, slab // 4
    duos = slabs // 4
    x, far = sub // 2, sub % 2
    after, before = (2 * duos - 3 - duo) // (duos - 1), (duo + duos - 2) // (duos - 1)
    has_after, has_before = duo < duos - 1, duo > 0
    early, late = role == 0, role == 1
    row, upper = duo // 2, duo % 2
    rows = duos // 2
    row_after, row_before = (2 * rows - 3 - row) // (rows - 1), (row + rows - 2) // (rows - 1)
    has_row_after, has_row_before = row < rows - 1, row > 0
    leads = jnp.logical_and(early, upper == 0)
    helps = jnp.logical_and(early, upper == 1)
    blocks, _, size, m = r.coupling_hbm.shape
    shots = r.rhs_hbm.shape[-1]

    other_core, other_sub = slab + 1 - 2 * core, 2 * x + 1 - far
    partner = (other_core, sub)
    opposite = (slab, other_sub)
    across = (other_core, other_sub)
    mate = (slab + 2 - 4 * role, sub)
    beside = [(slab, ((x + d) % 4) * 2 + far) for d in (1, 2, 3)]
    next_late, next_early = ((slab + 4) % slabs, sub), ((slab + 2) % slabs, sub)
    last_early, last_late = ((slab + slabs - 4) % slabs, sub), ((slab + slabs - 2) % slabs, sub)
    next_lead, last_lead = ((slab + 8) % slabs, sub), ((slab + slabs - 8) % slabs, sub)

    count = [0]
    unsent = []

    def remote(index, source, target, device):
        return pltpu.make_async_remote_copy(
            src_ref=source,
            dst_ref=target,
            send_sem=r.send_sem.at[index],
            recv_sem=r.recv_sem.at[index],
            device_id=device,
            device_id_type=MESH,
        )

    def channel():
        count[0] += 1
        return count[0] - 1

    def send(index, source, target, device, when=None):
        copy = remote(index, source, target, device)
        if when is None:
            copy.start()
        unsent.append((copy, when))
        return copy

    def receive(index, target):
        remote(index, target, target, partner).wait_recv()

    def local_copies(b):
        return [
            pltpu.make_async_copy(r.inverse_hbm.at[b], r.inverse.at[b], r.block_sem.at[0, b]),
            pltpu.make_async_copy(r.rhs_hbm.at[b], r.rhs.at[b], r.block_sem.at[1, b]),
            pltpu.make_async_copy(r.coupling_hbm.at[b], r.coupling.at[b], r.block_sem.at[2, b]),
        ]

    own_transfer = pltpu.make_async_copy(r.transfer_hbm, r.pair.at[core], r.here_sem.at[0])
    own_schur = pltpu.make_async_copy(r.schur_hbm, r.schur, r.here_sem.at[1])
    own_transfer.start()
    for b in range(blocks):
        for copy in local_copies(b):
            copy.start()
    own_schur.start()

    r.total[...] = jnp.zeros_like(r.total)

    def spread_of(b, carry):
        for i in range(size // STRIP):
            at = slice(i * STRIP, (i + 1) * STRIP)
            place = lax.broadcasted_iota(jnp.int32, (STRIP, size), 0) + i * STRIP
            r.spread[b, at] = (place == r.rows[pl.ds(b, 1), :]).astype(BF16)
        return carry

    barrier = pltpu.get_barrier_semaphore()

    def greet(device):
        pl.semaphore_signal(barrier, inc=1, device_id=device, device_id_type=MESH)

    for device in [partner, opposite, across, mate] + beside:
        greet(device)

    @pl.when(has_after)
    def _():
        greet(next_late)

        @pl.when(late)
        def _():
            greet(next_early)

    @pl.when(has_before)
    def _():
        greet(last_early)

        @pl.when(early)
        def _():
            greet(last_late)

    @pl.when(jnp.logical_and(leads, has_row_after))
    def _():
        greet(next_lead)

    @pl.when(jnp.logical_and(leads, has_row_before))
    def _():
        greet(last_lead)

    pl.semaphore_wait(
        barrier,
        7
        + after
        + before
        + role * after
        + (1 - role) * before
        + (1 - role) * (1 - upper) * (row_after + row_before),
    )

    c_transfer = channel()
    send(c_transfer, r.transfer_hbm, r.pair.at[core], partner)

    def combine(real, imag, axis):
        n = real.shape[axis] // 2
        if axis == 1:
            return jnp.concatenate(
                [real[:, :n] - imag[:, n:], real[:, n:] + imag[:, :n]], axis=1
            )
        return jnp.concatenate([real[:n] - imag[n:], real[n:] + imag[:n]], axis=0)

    def load_of(b, carry):
        for copy in local_copies(b):
            copy.wait()
        r.rhs_high[...], r.rhs_low[...] = halves(
            jnp.concatenate([r.rhs[b, 0], r.rhs[b, 1]], axis=1)
        )

        def strip(at, source, high, low, right):
            out = []
            for part in range(2):
                left = halves(source[b, part, at])
                high[b, part, at], low[b, part, at] = left
                out.append(dot3(left, right))
            return combine(out[0], out[1], 1)

        for i in range(m // STRIP):
            at = slice(i * STRIP, (i + 1) * STRIP)
            right = (r.rhs_high[...], r.rhs_low[...])
            value = strip(at, r.inverse, r.inverse_high, r.inverse_low, right)
            r.eliminated[b, at] = value
            r.known_high[at], r.known_low[at] = halves(value)
        for i in range(size // STRIP):
            at = slice(i * STRIP, (i + 1) * STRIP)
            right = (r.known_high[...], r.known_low[...])
            value = strip(at, r.coupling, r.coupling_high, r.coupling_low, right)
            r.weighted_high[at], r.weighted_low[at] = halves(value)
        for i in range(size // STRIP):
            at = slice(i * STRIP, (i + 1) * STRIP)
            spread = r.spread[b, at]
            r.total[at] += dot(
                jnp.concatenate([spread, spread], axis=1),
                jnp.concatenate([r.weighted_high[...], r.weighted_low[...]], axis=0),
            )
        return carry

    lax.fori_loop(0, blocks, spread_of, 0)
    lax.fori_loop(0, blocks // 2, load_of, 0)

    def split_pair(slot):
        def step_of(step, carry):
            at = pl.ds(pl.multiple_of(step * STRIP, STRIP), STRIP)
            for part in range(2):
                r.pair_high[slot, part, at, :], r.pair_low[slot, part, at, :] = halves(
                    r.pair[slot, part, at, :]
                )
            return carry

        lax.fori_loop(0, size // STRIP, step_of, 0)

    own_transfer.wait()
    split_pair(core)
    receive(c_transfer, r.pair.at[1 - core])
    split_pair(1 - core)
    first = (r.pair_high.at[0], r.pair_low.at[0])
    second = (r.pair_high.at[1], r.pair_low.at[1])

    def merged_rows(left, at, right):
        rows_high = jnp.concatenate([left[0][0, at, :], left[0][1, at, :]], axis=0)
        rows_low = jnp.concatenate([left[1][0, at, :], left[1][1, at, :]], axis=0)
        out = [dot3((rows_high, rows_low), (right[0][part], right[1][part])) for part in range(2)]
        return out[0][:STRIP] - out[1][STRIP:], out[0][STRIP:] + out[1][:STRIP]

    half = size // 2
    strips = half // STRIP

    def merge_two(step, carry):
        at = pl.ds(pl.multiple_of(core * half + step * STRIP, STRIP), STRIP)
        merged = merged_rows(second, at, first)
        for part in range(2):
            r.twos[role, strips * core + step, part] = merged[part]
        return carry

    lax.fori_loop(0, half // STRIP, merge_two, 0)
    c_half = channel()
    c_mate = channel()
    c_aside, c_pass = [[channel() for i in range(2)] for j in range(2)]
    odd = x % 2
    direct, indirect = strips * core + odd, strips * core + 1 - odd
    halved = r.twos.at[role, pl.ds(strips * core, strips)]
    send(c_half, halved, halved, partner)

    piece = r.twos.at[role, direct]
    send(c_mate, piece, piece, mate)

    lax.fori_loop(blocks // 2, blocks, load_of, 0)
    given = jnp.concatenate([r.given[0], r.given[1]], axis=1)
    rest = (jnp.where(sub == 0, given, jnp.zeros_like(given)) - r.total[...]).T
    rest = rest.reshape(2, shots // 8, 8, size)
    r.load[...] = jnp.stack([rest[0], rest[1]], axis=1).reshape(r.load.shape)

    c_x = [[channel() for d in range(3)] for which in range(2)]
    c_z = channel()
    for which in range(2):
        for d in (1, 2, 3):
            group = 2 * ((x + d) % 4) + (1 - far if which == 0 else far)
            send(
                c_x[which][d - 1], r.load.at[group], r.from_x.at[which, d - 1], beside[d - 1]
            )

    own_schur.wait()

    def split_schur(step, carry):
        at = pl.ds(pl.multiple_of(step * STRIP, STRIP), STRIP)
        for part in range(2):
            r.schur_high[part, :, at], r.schur_low[part, :, at] = halves(r.schur[part, at, :].T)
        return carry

    lax.fori_loop(0, size // STRIP, split_schur, 0)

    def side_sum(which, group):
        for d in range(3):
            receive(c_x[which][d], r.from_x.at[which, d])
        return (r.load[group] + r.from_x[which, 0]) + (r.from_x[which, 1] + r.from_x[which, 2])

    r.forward_sum[...] = side_sum(0, other_sub)
    send(c_z, r.forward_sum, r.from_z, opposite)

    piece = r.twos.at[1 - role, direct]
    receive(c_mate, piece)
    for part in range(2):
        aside = r.twos.at[1 - role, direct, part]
        send(c_aside[part], aside, aside, beside[2 * part])
    send(c_pass[0], piece, piece, partner)
    own_sum = side_sum(1, sub)

    receive(c_half, r.twos.at[role, pl.ds(strips * (1 - core), strips)])

    def split_two(which):
        def step_of(step, carry):
            to = pl.ds(pl.multiple_of(step * STRIP, STRIP), STRIP)
            for part in range(2):
                r.two_high[which, part, to, :], r.two_low[which, part, to, :] = halves(
                    r.twos[which, step, part]
                )
            return carry

        lax.fori_loop(0, size // STRIP, step_of, 0)

    split_two(role)
    two_early = (r.two_high.at[0], r.two_low.at[0])
    two_late = (r.two_high.at[1], r.two_low.at[1])
    four = (r.four_high, r.four_low)

    receive(c_z, r.from_z)
    summed = (own_sum + r.from_z[...]).reshape(2, 2, 8, size)
    summed = jnp.stack([summed[:, 0], summed[:, 1]], axis=0).reshape(32, size)
    solved = times(summed, (r.schur_high, r.schur_low), NN).reshape(2, 2, 8, size)
    solved = jnp.stack([solved[:, 0], solved[:, 1]], axis=0).reshape(2, 16, size)
    r.spare[...] = solved
    r.local[core] = r.spare[core]
    c_swap = channel()
    send(c_swap, r.spare.at[1 - core], r.local.at[core], partner)

    @pl.when(jnp.logical_not(has_before))
    def _():
        r.ahead_in[...] = jnp.zeros_like(r.ahead_in)

    @pl.when(jnp.logical_not(has_after))
    def _():
        r.back_in[...] = jnp.zeros_like(r.back_in)

    receive(c_swap, r.local.at[1 - core])
    start = r.local[1] - times(r.local[0], second, NT)
    c_start = channel()
    start_copy = send(c_start, r.start, r.start_in, mate, early)
    r.start[...] = start
    pl.when(early)(start_copy.start)

    c_late, c_early = channel(), channel()
    goes_on = jnp.logical_and(late, has_after)
    late_copy = send(c_late, r.ahead_out, r.ahead_in, next_late, goes_on)
    early_copy = send(c_early, r.ahead_out, r.ahead_in, next_early, goes_on)

    @pl.when(late)
    def _():
        receive(c_start, r.start_in)
        r.start[...] += times(r.start_in[...], two_late, NT)

        @pl.when(jnp.logical_not(has_before))
        def _():
            r.ahead_out[...] = r.start[...]
            late_copy.start()
            early_copy.start()

    for part in range(2):
        receive(c_aside[part], r.twos.at[1 - role, indirect, part])
    piece = r.twos.at[1 - role, indirect]
    send(c_pass[1], piece, piece, partner)
    for i in range(2):
        receive(c_pass[i], r.twos.at[1 - role, strips * (1 - core) + (odd if i == 0 else 1 - odd)])
    split_two(1 - role)

    @pl.when(jnp.logical_and(duo > 1, jnp.logical_or(late, upper == 0)))
    def _():
        def merge_four(step, carry):
            at = pl.ds(pl.multiple_of(step * STRIP, STRIP), STRIP)
            merged = merged_rows(two_late, at, two_early)

            @pl.when(early)
            def _():
                for part in range(2):
                    r.four_high[part, at, :], r.four_low[part, at, :] = halves(merged[part])

            @pl.when(late)
            def _():
                for part in range(2):
                    r.four_high[part, :, at], r.four_low[part, :, at] = halves(merged[part].T)

            return carry

        lax.fori_loop(0, size // STRIP, merge_four, 0)

    gives = jnp.logical_and(helps, has_row_after)
    takes = jnp.logical_and(leads, has_row_after)
    c_four, c_four_pass = channel(), channel()
    half_four = pl.ds(strips * core, strips)
    four_copy = send(c_four, r.four_out, r.four_in.at[half_four], last_early, gives)

    @pl.when(gives)
    def _():
        def merge_half(step, carry):
            at = pl.ds(pl.multiple_of(core * half + step * STRIP, STRIP), STRIP)
            merged = merged_rows(two_late, at, two_early)
            for part in range(2):
                r.four_out[step, part] = merged[part]
            return carry

        lax.fori_loop(0, strips, merge_half, 0)
        four_copy.start()

    def weights_of(b, carry):
        spread = r.spread[b]
        for part in range(2):
            r.placed_high[part] = dot(spread, r.coupling_high[b, part]).astype(BF16)
            r.placed_low[part] = dot(spread, r.coupling_low[b, part]).astype(BF16)

        def inverse(part):
            return r.inverse_high[b, part], r.inverse_low[b, part]

        def strip_of(step, carry):
            at = pl.ds(pl.multiple_of(step * STRIP, STRIP), STRIP)
            left = [
                jnp.concatenate([source[0, at, :], source[1, at, :]], axis=0)
                for source in (r.placed_high, r.placed_low)
            ]
            merged = combine(dot3(left, inverse(0)), dot3(left, inverse(1)), 0)
            for part in range(2):
                r.coupling_high[b, part, at, :], r.coupling_low[b, part, at, :] = halves(
                    merged[part * STRIP : (part + 1) * STRIP]
                )
            return carry

        lax.fori_loop(0, size // STRIP, strip_of, 0)
        left = halves(r.eliminated[b].T)
        r.eliminated[b] = combine(dot3(left, inverse(0)), dot3(left, inverse(1)), 0)
        return carry

    towards_end = duo >= duos - 2

    @pl.when(towards_end)
    def _():
        lax.fori_loop(0, blocks, weights_of, 0)

    @pl.when(late)
    def _():
        @pl.when(has_before)
        def _():
            receive(c_late, r.ahead_in)

            @pl.when(duo > 1)
            def _():
                r.ahead_out[...] = r.start[...] + times(r.ahead_in[...], four, NN)

            @pl.when(duo == 1)
            def _():
                r.ahead_out[...] = r.start[...] + times(
                    times(r.ahead_in[...], two_early, NT), two_late, NT
                )

            @pl.when(has_after)
            def _():
                late_copy.start()
                early_copy.start()

        r.trace[1] = r.ahead_out[...]
        inner = r.start_in[...] + times(r.ahead_in[...], two_early, NT)
        r.trace[0] = r.local[0] - times(inner, first, NT)

    @pl.when(early)
    def _():
        pl.when(has_before)(lambda: receive(c_early, r.ahead_in))
        r.trace[0] = r.local[0] - times(r.ahead_in[...], first, NT)
        r.trace[1] = r.local[1] - times(r.trace[0], second, NT)

    queued = times(r.trace[0] - times(r.trace[1], second, NN), first, NN)
    r.queued[...] = queued
    c_queued = channel()
    queued_copy = send(c_queued, r.queued, r.queued_in, mate, late)
    pl.when(late)(queued_copy.start)

    @pl.when(jnp.logical_not(towards_end))
    def _():
        lax.fori_loop(0, blocks, weights_of, 0)

    c_upper, c_lower, c_lead, c_help, c_back_late = [channel() for i in range(5)]
    goes_back = jnp.logical_and(leads, has_row_before)
    upper_copy = send(c_upper, r.queued, r.upper_in, last_early, helps)
    lower_copy = send(c_lower, r.lower, r.lower_in, mate, leads)
    back_lead = send(c_lead, r.back_out, r.back_in, last_lead, goes_back)
    back_help = send(c_help, r.back_out, r.back_in, last_early, goes_back)
    back_late = send(c_back_late, r.back_out, r.back_in, last_late, goes_back)
    pass_copy = send(
        c_four_pass, r.four_in.at[half_four], r.four_in.at[half_four], partner, takes
    )
    top = (r.top_high, r.top_low)

    @pl.when(early)
    def _():
        receive(c_queued, r.queued_in)
        r.queued[...] += times(r.queued_in[...], two_early, NN)

    @pl.when(helps)
    def _():
        upper_copy.start()
        pl.when(has_row_after)(lambda: receive(c_help, r.back_in))
        r.carried[...] = r.queued_in[...] + times(r.back_in[...], two_late, NN)

    @pl.when(leads)
    def _():
        @pl.when(has_row_after)
        def _():
            receive(c_four, r.four_in.at[half_four])
            pass_copy.start()
            receive(c_four_pass, r.four_in.at[pl.ds(strips * (1 - core), strips)])

            def split_top(step, carry):
                to = pl.ds(pl.multiple_of(step * STRIP, STRIP), STRIP)
                for part in range(2):
                    r.top_high[part, to, :], r.top_low[part, to, :] = halves(r.four_in[step, part])
                return carry

            lax.fori_loop(0, size // STRIP, split_top, 0)

        receive(c_upper, r.upper_in)

        @pl.when(has_row_after)
        def _():
            receive(c_lead, r.back_in)
            r.lower[...] = r.upper_in[...] + times(r.back_in[...], top, NN)

        @pl.when(jnp.logical_not(has_row_after))
        def _():
            r.lower[...] = r.upper_in[...]

        lower_copy.start()

        @pl.when(has_row_before)
        def _():
            r.back_out[...] = r.queued[...] + times(r.lower[...], four, NN)
            back_lead.start()
            back_help.start()
            back_late.start()

        r.carried[...] = r.queued_in[...] + times(r.lower[...], two_late, NN)

    @pl.when(jnp.logical_and(late, upper == 1))
    def _():
        pl.when(has_row_after)(lambda: receive(c_back_late, r.back_in))
        r.carried[...] = r.back_in[...]

    @pl.when(jnp.logical_and(late, upper == 0))
    def _():
        receive(c_lower, r.lower_in)
        r.carried[...] = r.lower_in[...]

    r.found[1] = r.trace[1] - r.carried[...]
    r.found[0] = r.trace[0] - times(r.found[1], second, NN)

    c_chip, c_far, c_across = channel(), channel(), channel()
    c_side = [[channel() for d in range(3)] for which in range(2)]
    place = r.gathered.at[sub, core]
    send(c_chip, r.found.at[1 - core], place, partner)
    send(c_far, r.found.at[core], place, opposite)
    send(c_across, r.found.at[1 - core], place, across)
    r.gathered[sub, core] = r.found[core]
    receive(c_chip, r.gathered.at[sub, 1 - core])
    for d in (1, 2, 3):
        send(c_side[0][d - 1], r.gathered.at[sub], r.gathered.at[sub], beside[d - 1])
    receive(c_far, r.gathered.at[other_sub, core])
    receive(c_across, r.gathered.at[other_sub, 1 - core])
    for d in (1, 2, 3):
        send(c_side[1][d - 1], r.gathered.at[other_sub], r.gathered.at[other_sub], beside[d - 1])
    for which in range(2):
        for d in (1, 2, 3):
            group = 2 * ((x + 4 - d) % 4) + (far if which == 0 else 1 - far)
            receive(c_side[which][d - 1], r.gathered.at[group])

    found = r.gathered[...].reshape(shots // 8, 2, 8, size)
    found = jnp.stack([found[:, 0], found[:, 1]], axis=0).reshape(2 * shots, size)
    r.found_high[...], r.found_low[...] = halves(found)
    turned = found.T
    r.separator_out[0] = turned[:, :shots]
    r.separator_out[1] = turned[:, shots:]

    def interior_of(b, carry):
        left = (r.found_high[...], r.found_low[...])
        out = [
            dot3(left, (r.coupling_high[b, part], r.coupling_low[b, part])) for part in range(2)
        ]
        turned = (r.eliminated[b] - combine(out[0], out[1], 0)).T
        r.interior_out[b, 0] = turned[:, :shots]
        r.interior_out[b, 1] = turned[:, shots:]
        return carry

    lax.fori_loop(0, blocks, interior_of, 0)

    for copy, when in unsent:
        if when is None:
            copy.wait_send()
        else:
            pl.when(when)(copy.wait_send)


CHANNELS = 40


def body(
    rhs_interior,
    rhs_separator,
    inverse_blocks,
    coupling,
    separator_rows,
    separator_inverse,
    transfer,
):
    _, nb, _, m, shots = rhs_interior.shape
    size = transfer.shape[-1]
    vmem = pltpu.VMEM
    inputs = {
        "rows": separator_rows[0],
        "given": rhs_separator[0],
        "rhs_hbm": rhs_interior[0],
        "inverse_hbm": inverse_blocks[0],
        "coupling_hbm": coupling[0],
        "schur_hbm": separator_inverse[0],
        "transfer_hbm": transfer[0],
    }
    outputs = {
        "interior_out": jax.ShapeDtypeStruct((nb, 2, m, shots), F32),
        "separator_out": jax.ShapeDtypeStruct((2, size, shots), F32),
    }
    scratch = {
        "inverse": vmem((nb, 2, m, m), F32),
        "inverse_high": vmem((nb, 2, m, m), BF16),
        "inverse_low": vmem((nb, 2, m, m), BF16),
        "rhs": vmem((nb, 2, m, shots), F32),
        "coupling": vmem((nb, 2, size, m), F32),
        "coupling_high": vmem((nb, 2, size, m), BF16),
        "coupling_low": vmem((nb, 2, size, m), BF16),
        "spread": vmem((nb, size, size), BF16),
        "placed_high": vmem((2, size, m), BF16),
        "placed_low": vmem((2, size, m), BF16),
        "eliminated": vmem((nb, m, 2 * shots), F32),
        "rhs_high": vmem((m, 2 * shots), BF16),
        "rhs_low": vmem((m, 2 * shots), BF16),
        "known_high": vmem((m, 2 * shots), BF16),
        "known_low": vmem((m, 2 * shots), BF16),
        "weighted_high": vmem((size, 2 * shots), BF16),
        "weighted_low": vmem((size, 2 * shots), BF16),
        "total": vmem((size, 2 * shots), F32),
        "load": vmem((8, 32, size), F32),
        "from_x": vmem((2, 3, 32, size), F32),
        "forward_sum": vmem((32, size), F32),
        "from_z": vmem((32, size), F32),
        "schur": vmem((2, size, size), F32),
        "schur_high": vmem((2, size, size), BF16),
        "schur_low": vmem((2, size, size), BF16),
        "pair": vmem((2, 2, size, size), F32),
        "pair_high": vmem((2, 2, size, size), BF16),
        "pair_low": vmem((2, 2, size, size), BF16),
        "twos": vmem((2, size // STRIP, 2, STRIP, size), F32),
        "two_high": vmem((2, 2, size, size), BF16),
        "two_low": vmem((2, 2, size, size), BF16),
        "four_high": vmem((2, size, size), BF16),
        "four_low": vmem((2, size, size), BF16),
        "four_out": vmem((size // STRIP // 2, 2, STRIP, size), F32),
        "four_in": vmem((size // STRIP, 2, STRIP, size), F32),
        "top_high": vmem((2, size, size), BF16),
        "top_low": vmem((2, size, size), BF16),
        "upper_in": vmem((16, size), F32),
        "lower": vmem((16, size), F32),
        "lower_in": vmem((16, size), F32),
        "spare": vmem((2, 16, size), F32),
        "local": vmem((2, 16, size), F32),
        "start": vmem((16, size), F32),
        "start_in": vmem((16, size), F32),
        "ahead_in": vmem((16, size), F32),
        "ahead_out": vmem((16, size), F32),
        "trace": vmem((2, 16, size), F32),
        "queued": vmem((16, size), F32),
        "queued_in": vmem((16, size), F32),
        "back_in": vmem((16, size), F32),
        "back_out": vmem((16, size), F32),
        "carried": vmem((16, size), F32),
        "found": vmem((2, 16, size), F32),
        "gathered": vmem((8, 2, 16, size), F32),
        "found_high": vmem((2 * shots, size), BF16),
        "found_low": vmem((2 * shots, size), BF16),
        "send_sem": pltpu.SemaphoreType.DMA((CHANNELS,)),
        "recv_sem": pltpu.SemaphoreType.DMA((CHANNELS,)),
        "here_sem": pltpu.SemaphoreType.DMA((2,)),
        "block_sem": pltpu.SemaphoreType.DMA((3, nb)),
    }
    names = list(inputs) + list(outputs) + list(scratch)

    def sweep_kernel(*refs):
        kernel(names, *refs)

    interior, separator = pl.pallas_call(
        sweep_kernel,
        out_shape=tuple(outputs.values()),
        in_specs=[pl.BlockSpec(memory_space=pltpu.VMEM)] * 2
        + [pl.BlockSpec(memory_space=pltpu.HBM)] * (len(inputs) - 2),
        out_specs=(pl.BlockSpec(memory_space=pltpu.VMEM),) * 2,
        scratch_shapes=list(scratch.values()),
        compiler_params=pltpu.CompilerParams(
            collective_id=0, has_side_effects=True, vmem_limit_bytes=51 << 20
        ),
    )(*inputs.values())
    return (interior[None], separator[None])


def solution(mesh):
    in_specs = (
        P("slab", "sub", None, None, None),
        P("slab", None, None, None),
        P("slab", "sub", None, None, None),
        P("slab", "sub", None, None, None),
        P("slab", "sub", None),
        P("slab", None, None, None),
        P("slab", None, None, None),
    )
    out_specs = (P("slab", "sub", None, None, None), P("slab", None, None, None))
    return jax.shard_map(body, mesh=mesh, in_specs=in_specs, out_specs=out_specs, check_vma=False)
```

```python
import types

import jax
import jax.numpy as jnp
from jax import lax
from jax.experimental import pallas as pl
from jax.experimental.pallas import tpu as pltpu
from jax.sharding import PartitionSpec as P

MESH = pl.DeviceIdType.MESH
F32 = jnp.float32
BF16 = jnp.bfloat16
NN = (((1,), (0,)), ((), ()))
NT = (((1,), (1,)), ((), ()))
STRIP = 128
WIDE = 256


def halves(value):
    high = value.astype(BF16)
    return high, (value - high.astype(F32)).astype(BF16)


def dot(left, right, dims=NN):
    return lax.dot_general(left, right, dims, preferred_element_type=F32)


def dot3(left, right):
    return dot(
        jnp.concatenate([left[0], left[0], left[1]], axis=1),
        jnp.concatenate([right[0], right[1], right[0]], axis=0),
    )


def times(value, matrix, dims):
    high, low = matrix
    n = value.shape[0] // 2
    value_high, value_low = halves(value)
    both = jnp.concatenate([value_high, value_low], axis=0)
    out = []
    for part in range(2):
        whole = dot(both, high[part], dims)
        out.append(whole[: 2 * n] + (whole[2 * n :] + dot(value_high, low[part], dims)))
    return jnp.concatenate([out[0][:n] - out[1][n:], out[0][n:] + out[1][:n]], axis=0)


def kernel(names, *refs):
    r = types.SimpleNamespace(**dict(zip(names, refs)))
    slab, sub = lax.axis_index("slab"), lax.axis_index("sub")
    slabs = lax.axis_size("slab")
    core, role, duo = slab % 2, (slab // 2) % 2, slab // 4
    duos = slabs // 4
    x, far = sub // 2, sub % 2
    after, before = (2 * duos - 3 - duo) // (duos - 1), (duo + duos - 2) // (duos - 1)
    has_after, has_before = duo < duos - 1, duo > 0
    early, late = role == 0, role == 1
    row, upper = duo // 2, duo % 2
    rows = duos // 2
    row_after, row_before = (2 * rows - 3 - row) // (rows - 1), (row + rows - 2) // (rows - 1)
    has_row_after, has_row_before = row < rows - 1, row > 0
    leads = jnp.logical_and(early, upper == 0)
    helps = jnp.logical_and(early, upper == 1)
    enters = jnp.logical_and(late, upper == 0)
    ends = jnp.logical_and(late, upper == 1)
    node = jnp.logical_or(enters, helps)
    blocks, _, size, m = r.coupling_hbm.shape
    shots = r.rhs_hbm.shape[-1]

    other_core, other_sub = slab + 1 - 2 * core, 2 * x + 1 - far
    partner = (other_core, sub)
    opposite = (slab, other_sub)
    across = (other_core, other_sub)
    mate = (slab + 2 - 4 * role, sub)
    beside = [(slab, ((x + d) % 4) * 2 + far) for d in (1, 2, 3)]
    def chip_at(offset):
        return ((slab + slabs + offset) % slabs, sub)

    critical, other = chip_at(2 + 4 * upper), chip_at(4)
    last_early, last_late = chip_at(-4), chip_at(-2)
    next_lead, last_lead = ((slab + 8) % slabs, sub), ((slab + slabs - 8) % slabs, sub)

    count = [0]
    unsent = []

    def remote(index, source, target, device):
        return pltpu.make_async_remote_copy(
            src_ref=source,
            dst_ref=target,
            send_sem=r.send_sem.at[index],
            recv_sem=r.recv_sem.at[index],
            device_id=device,
            device_id_type=MESH,
        )

    def channel():
        count[0] += 1
        return count[0] - 1

    def send(index, source, target, device, when=None):
        copy = remote(index, source, target, device)
        if when is None:
            copy.start()
        unsent.append((copy, when))
        return copy

    def receive(index, target):
        remote(index, target, target, partner).wait_recv()

    def local_copies(b):
        return [
            pltpu.make_async_copy(r.inverse_hbm.at[b], r.inverse.at[b], r.block_sem.at[0, b]),
            pltpu.make_async_copy(r.rhs_hbm.at[b], r.rhs.at[b], r.block_sem.at[1, b]),
            pltpu.make_async_copy(r.coupling_hbm.at[b], r.coupling.at[b], r.block_sem.at[2, b]),
        ]

    own_transfer = pltpu.make_async_copy(r.transfer_hbm, r.pair.at[core], r.here_sem.at[0])
    own_schur = pltpu.make_async_copy(r.schur_hbm, r.schur, r.here_sem.at[1])
    own_transfer.start()
    for b in range(blocks):
        for copy in local_copies(b):
            copy.start()
    own_schur.start()

    r.total[...] = jnp.zeros_like(r.total)

    def spread_of(b, carry):
        for i in range(size // STRIP):
            at = slice(i * STRIP, (i + 1) * STRIP)
            place = lax.broadcasted_iota(jnp.int32, (STRIP, size), 0) + i * STRIP
            r.spread[b, at] = (place == r.rows[pl.ds(b, 1), :]).astype(BF16)
        return carry

    barrier = pltpu.get_barrier_semaphore()

    def greet(device):
        pl.semaphore_signal(barrier, inc=1, device_id=device, device_id_type=MESH)

    for device in [partner, opposite, across, mate] + beside:
        greet(device)

    for who, always, before_too, after_too in (
        (leads, (4,), (-4, -2, -8), (8,)),
        (enters, (2, 4), (-6,), ()),
        (helps, (-2, -4), (), (4, 6)),
        (ends, (-4,), (), (2,)),
    ):
        for when, offsets in (
            (who, always),
            (jnp.logical_and(who, has_row_before), before_too),
            (jnp.logical_and(who, has_row_after), after_too),
        ):
            if offsets:

                @pl.when(when)
                def _(offsets=offsets):
                    for offset in offsets:
                        greet(chip_at(offset))

    pl.semaphore_wait(
        barrier,
        7
        + (1 - role) * (1 - upper) * (1 + 3 * row_before + row_after)
        + role * (1 - upper) * (2 + row_before)
        + (1 - role) * upper * (2 + 2 * row_after)
        + role * upper * (1 + row_after),
    )

    c_transfer = channel()
    send(c_transfer, r.transfer_hbm, r.pair.at[core], partner)

    def combine(real, imag, axis):
        n = real.shape[axis] // 2
        if axis == 1:
            return jnp.concatenate(
                [real[:, :n] - imag[:, n:], real[:, n:] + imag[:, :n]], axis=1
            )
        return jnp.concatenate([real[:n] - imag[n:], real[n:] + imag[:n]], axis=0)

    def load_of(b, carry):
        for copy in local_copies(b):
            copy.wait()
        r.rhs_high[...], r.rhs_low[...] = halves(
            jnp.concatenate([r.rhs[b, 0], r.rhs[b, 1]], axis=1)
        )

        def strip(at, source, high, low, right):
            out = []
            for part in range(2):
                left = halves(source[b, part, at])
                high[b, part, at], low[b, part, at] = left
                out.append(dot3(left, right))
            return combine(out[0], out[1], 1)

        for i in range(m // WIDE):
            at = slice(i * WIDE, (i + 1) * WIDE)
            right = (r.rhs_high[...], r.rhs_low[...])
            value = strip(at, r.inverse, r.inverse_high, r.inverse_low, right)
            r.eliminated[b, at] = value
            r.known_high[at], r.known_low[at] = halves(value)
        for i in range(size // WIDE):
            at = slice(i * WIDE, (i + 1) * WIDE)
            right = (r.known_high[...], r.known_low[...])
            value = strip(at, r.coupling, r.coupling_high, r.coupling_low, right)
            r.weighted_high[at], r.weighted_low[at] = halves(value)
        for i in range(size // WIDE):
            at = slice(i * WIDE, (i + 1) * WIDE)
            spread = r.spread[b, at]
            r.total[at] += dot(
                jnp.concatenate([spread, spread], axis=1),
                jnp.concatenate([r.weighted_high[...], r.weighted_low[...]], axis=0),
            )
        return carry

    lax.fori_loop(0, blocks, spread_of, 0)
    lax.fori_loop(0, blocks // 2, load_of, 0)

    def split_pair(slot):
        def step_of(step, carry):
            at = pl.ds(pl.multiple_of(step * STRIP, STRIP), STRIP)
            for part in range(2):
                r.pair_high[slot, part, at, :], r.pair_low[slot, part, at, :] = halves(
                    r.pair[slot, part, at, :]
                )
            return carry

        lax.fori_loop(0, size // STRIP, step_of, 0)

    own_transfer.wait()
    split_pair(core)
    receive(c_transfer, r.pair.at[1 - core])
    split_pair(1 - core)
    first = (r.pair_high.at[0], r.pair_low.at[0])
    second = (r.pair_high.at[1], r.pair_low.at[1])

    def merged_rows(left, at, right):
        rows_high = jnp.concatenate([left[0][0, at, :], left[0][1, at, :]], axis=0)
        rows_low = jnp.concatenate([left[1][0, at, :], left[1][1, at, :]], axis=0)
        out = [dot3((rows_high, rows_low), (right[0][part], right[1][part])) for part in range(2)]
        return out[0][:STRIP] - out[1][STRIP:], out[0][STRIP:] + out[1][:STRIP]

    half = size // 2
    strips = half // STRIP

    def merge_two(step, carry):
        at = pl.ds(pl.multiple_of(core * half + step * STRIP, STRIP), STRIP)
        merged = merged_rows(second, at, first)
        for part in range(2):
            r.twos[role, strips * core + step, part] = merged[part]
        return carry

    lax.fori_loop(0, half // STRIP, merge_two, 0)
    c_half = channel()
    c_mate = channel()
    c_aside, c_pass = [[channel() for i in range(2)] for j in range(2)]
    odd = x % 2
    direct, indirect = strips * core + odd, strips * core + 1 - odd
    halved = r.twos.at[role, pl.ds(strips * core, strips)]
    send(c_half, halved, halved, partner)

    piece = r.twos.at[role, direct]
    send(c_mate, piece, piece, mate)

    lax.fori_loop(blocks // 2, blocks, load_of, 0)
    given = jnp.concatenate([r.given[0], r.given[1]], axis=1)
    rest = (jnp.where(sub == 0, given, jnp.zeros_like(given)) - r.total[...]).T
    rest = rest.reshape(2, shots // 8, 8, size)
    r.load[...] = jnp.stack([rest[0], rest[1]], axis=1).reshape(r.load.shape)

    c_x = [[channel() for d in range(3)] for which in range(2)]
    c_z = channel()
    for which in range(2):
        for d in (2, 1, 3):
            group = 2 * ((x + d) % 4) + (1 - far if which == 0 else far)
            send(
                c_x[which][d - 1], r.load.at[group], r.from_x.at[which, d - 1], beside[d - 1]
            )

    own_schur.wait()

    def split_schur(step, carry):
        at = pl.ds(pl.multiple_of(step * STRIP, STRIP), STRIP)
        for part in range(2):
            r.schur_high[part, :, at], r.schur_low[part, :, at] = halves(r.schur[part, at, :].T)
        return carry

    lax.fori_loop(0, size // STRIP, split_schur, 0)

    def side_sum(which, group):
        for d in range(3):
            receive(c_x[which][d], r.from_x.at[which, d])
        return (r.load[group] + r.from_x[which, 0]) + (r.from_x[which, 1] + r.from_x[which, 2])

    r.forward_sum[...] = side_sum(0, other_sub)
    send(c_z, r.forward_sum, r.from_z, opposite)

    piece = r.twos.at[1 - role, direct]
    receive(c_mate, piece)
    for part in range(2):
        aside = r.twos.at[1 - role, direct, part]
        send(c_aside[part], aside, aside, beside[2 * part])
    send(c_pass[0], piece, piece, partner)
    own_sum = side_sum(1, sub)

    receive(c_half, r.twos.at[role, pl.ds(strips * (1 - core), strips)])

    def split_two(which):
        def step_of(step, carry):
            to = pl.ds(pl.multiple_of(step * STRIP, STRIP), STRIP)
            for part in range(2):
                r.two_high[which, part, to, :], r.two_low[which, part, to, :] = halves(
                    r.twos[which, step, part]
                )
            return carry

        lax.fori_loop(0, size // STRIP, step_of, 0)

    split_two(role)
    two_early = (r.two_high.at[0], r.two_low.at[0])
    two_late = (r.two_high.at[1], r.two_low.at[1])
    four = (r.four_high, r.four_low)

    receive(c_z, r.from_z)
    summed = (own_sum + r.from_z[...]).reshape(2, 2, 8, size)
    summed = jnp.stack([summed[:, 0], summed[:, 1]], axis=0).reshape(32, size)
    solved = times(summed, (r.schur_high, r.schur_low), NN).reshape(2, 2, 8, size)
    solved = jnp.stack([solved[:, 0], solved[:, 1]], axis=0).reshape(2, 16, size)
    r.spare[...] = solved
    r.local[core] = r.spare[core]
    c_swap = channel()
    send(c_swap, r.spare.at[1 - core], r.local.at[core], partner)

    @pl.when(jnp.logical_not(has_before))
    def _():
        r.ahead_in[...] = jnp.zeros_like(r.ahead_in)

    @pl.when(jnp.logical_not(has_after))
    def _():
        r.back_in[...] = jnp.zeros_like(r.back_in)

    receive(c_swap, r.local.at[1 - core])
    start = r.local[1] - times(r.local[0], second, NT)
    c_start = channel()
    gives_start = jnp.logical_or(early, upper == 1)
    start_copy = send(c_start, r.start, r.start_in, mate, gives_start)
    r.start[...] = start
    pl.when(gives_start)(start_copy.start)

    c_node, c_other = channel(), channel()
    goes_on = jnp.logical_and(node, has_after)
    node_copy = send(c_node, r.ahead_out, r.ahead_in, critical, goes_on)
    other_copy = send(c_other, r.ahead_out, r.ahead_in, other, goes_on)

    @pl.when(enters)
    def _():
        receive(c_start, r.start_in)
        r.node_start[...] = r.start[...] + times(r.start_in[...], two_late, NT)

        @pl.when(jnp.logical_not(has_before))
        def _():
            r.ahead_out[...] = r.node_start[...]
            node_copy.start()
            other_copy.start()

    for part in range(2):
        receive(c_aside[part], r.twos.at[1 - role, indirect, part])
    piece = r.twos.at[1 - role, indirect]
    send(c_pass[1], piece, piece, partner)
    for i in range(2):
        receive(c_pass[i], r.twos.at[1 - role, strips * (1 - core) + (odd if i == 0 else 1 - odd)])
    split_two(1 - role)

    pl.when(ends)(lambda: receive(c_start, r.start_in))

    @pl.when(helps)
    def _():
        receive(c_start, r.start_in)
        r.node_start[...] = r.start_in[...] + times(r.start[...], two_late, NT)

    gives = jnp.logical_and(helps, has_row_after)
    takes = jnp.logical_and(leads, has_row_after)
    c_four, c_four_pass = channel(), channel()
    half_four = pl.ds(strips * core, strips)
    four_copy = send(c_four, r.four_out, r.four_in.at[half_four], last_early, gives)

    @pl.when(jnp.logical_or(gives, jnp.logical_and(upper == 0, duo > 1)))
    def _():
        def merge_four(step, carry):
            at = pl.ds(pl.multiple_of(step * STRIP, STRIP), STRIP)
            merged = merged_rows(two_late, at, two_early)

            @pl.when(leads)
            def _():
                for part in range(2):
                    r.four_high[part, at, :], r.four_low[part, at, :] = halves(merged[part])

            @pl.when(node)
            def _():
                for part in range(2):
                    r.four_high[part, :, at], r.four_low[part, :, at] = halves(merged[part].T)

            @pl.when(step // strips == core)
            def _():
                for part in range(2):
                    r.four_out[step % strips, part] = merged[part]

            return carry

        whole = (duo + duos - 3) // (duos - 1)
        low = (1 - whole) * strips * core
        lax.fori_loop(low, low + strips * (1 + whole), merge_four, 0)
        pl.when(gives)(four_copy.start)

    def weights_of(b, carry):
        spread = r.spread[b]
        for part in range(2):
            r.placed_high[part] = dot(spread, r.coupling_high[b, part]).astype(BF16)
            r.placed_low[part] = dot(spread, r.coupling_low[b, part]).astype(BF16)

        def inverse(part):
            return r.inverse_high[b, part], r.inverse_low[b, part]

        def strip_of(step, carry):
            at = pl.ds(pl.multiple_of(step * STRIP, STRIP), STRIP)
            left = [
                jnp.concatenate([source[0, at, :], source[1, at, :]], axis=0)
                for source in (r.placed_high, r.placed_low)
            ]
            merged = combine(dot3(left, inverse(0)), dot3(left, inverse(1)), 0)
            for part in range(2):
                r.coupling_high[b, part, at, :], r.coupling_low[b, part, at, :] = halves(
                    merged[part * STRIP : (part + 1) * STRIP]
                )
            return carry

        lax.fori_loop(0, size // STRIP, strip_of, 0)
        left = halves(r.eliminated[b].T)
        r.eliminated[b] = combine(dot3(left, inverse(0)), dot3(left, inverse(1)), 0)
        return carry

    towards_end = duo >= duos - 2

    @pl.when(towards_end)
    def _():
        lax.fori_loop(0, blocks, weights_of, 0)

    @pl.when(jnp.logical_and(node, has_before))
    def _():
        receive(c_node, r.ahead_in)

        @pl.when(jnp.logical_and(duo > 1, has_after))
        def _():
            r.ahead_out[...] = r.node_start[...] + times(r.ahead_in[...], four, NN)

        @pl.when(duo == 1)
        def _():
            r.ahead_out[...] = r.node_start[...] + times(
                times(r.ahead_in[...], two_early, NT), two_late, NT
            )

        @pl.when(has_after)
        def _():
            node_copy.start()
            other_copy.start()

    @pl.when(ends)
    def _():
        receive(c_other, r.ahead_in)

    @pl.when(jnp.logical_and(leads, has_before))
    def _():
        receive(c_other, r.ahead_in)

    r.enter[...] = r.ahead_in[...]

    @pl.when(late)
    def _():
        r.enter[...] = r.start_in[...] + times(r.ahead_in[...], two_early, NT)

    r.trace[0] = r.local[0] - times(r.enter[...], first, NT)
    r.trace[1] = r.local[1] - times(r.trace[0], second, NT)
    queued = times(r.trace[0] - times(r.trace[1], second, NN), first, NN)
    r.queued[...] = queued
    c_queued = channel()
    queued_copy = send(c_queued, r.queued, r.queued_in, mate, late)
    pl.when(late)(queued_copy.start)

    @pl.when(jnp.logical_not(towards_end))
    def _():
        lax.fori_loop(0, blocks, weights_of, 0)

    c_upper, c_lower, c_lead, c_help, c_back_late = [channel() for i in range(5)]
    goes_back = jnp.logical_and(leads, has_row_before)
    upper_copy = send(c_upper, r.queued, r.upper_in, last_early, helps)
    lower_copy = send(c_lower, r.lower, r.lower_in, mate, leads)
    back_lead = send(c_lead, r.back_out, r.back_in, last_lead, goes_back)
    back_help = send(c_help, r.back_out, r.back_in, last_early, goes_back)
    back_late = send(c_back_late, r.back_out, r.back_in, last_late, goes_back)
    pass_copy = send(
        c_four_pass, r.four_in.at[half_four], r.four_in.at[half_four], partner, takes
    )
    top = (r.top_high, r.top_low)

    @pl.when(early)
    def _():
        receive(c_queued, r.queued_in)
        r.queued[...] += times(r.queued_in[...], two_early, NN)

    @pl.when(helps)
    def _():
        upper_copy.start()
        pl.when(has_row_after)(lambda: receive(c_help, r.back_in))
        r.carried[...] = r.queued_in[...] + times(r.back_in[...], two_late, NN)

    @pl.when(leads)
    def _():
        @pl.when(has_row_after)
        def _():
            receive(c_four, r.four_in.at[half_four])
            pass_copy.start()
            receive(c_four_pass, r.four_in.at[pl.ds(strips * (1 - core), strips)])

            def split_top(step, carry):
                to = pl.ds(pl.multiple_of(step * STRIP, STRIP), STRIP)
                for part in range(2):
                    r.top_high[part, to, :], r.top_low[part, to, :] = halves(r.four_in[step, part])
                return carry

            lax.fori_loop(0, size // STRIP, split_top, 0)

        receive(c_upper, r.upper_in)

        @pl.when(has_row_after)
        def _():
            receive(c_lead, r.back_in)
            r.lower[...] = r.upper_in[...] + times(r.back_in[...], top, NN)

        @pl.when(jnp.logical_not(has_row_after))
        def _():
            r.lower[...] = r.upper_in[...]

        lower_copy.start()

        @pl.when(has_row_before)
        def _():
            r.back_out[...] = r.queued[...] + times(r.lower[...], four, NN)
            back_lead.start()
            back_help.start()
            back_late.start()

        r.carried[...] = r.queued_in[...] + times(r.lower[...], two_late, NN)

    @pl.when(ends)
    def _():
        pl.when(has_row_after)(lambda: receive(c_back_late, r.back_in))
        r.carried[...] = r.back_in[...]

    @pl.when(enters)
    def _():
        receive(c_lower, r.lower_in)
        r.carried[...] = r.lower_in[...]

    r.found[1] = r.trace[1] - r.carried[...]
    r.found[0] = r.trace[0] - times(r.found[1], second, NN)

    c_chip, c_far, c_across = channel(), channel(), channel()
    c_side = [[channel() for d in range(3)] for which in range(2)]
    place = r.gathered.at[sub, core]
    send(c_chip, r.found.at[1 - core], place, partner)
    send(c_far, r.found.at[core], place, opposite)
    send(c_across, r.found.at[1 - core], place, across)
    r.gathered[sub, core] = r.found[core]
    receive(c_chip, r.gathered.at[sub, 1 - core])
    for d in (2, 1, 3):
        send(c_side[0][d - 1], r.gathered.at[sub], r.gathered.at[sub], beside[d - 1])
    receive(c_far, r.gathered.at[other_sub, core])
    receive(c_across, r.gathered.at[other_sub, 1 - core])
    for d in (2, 1, 3):
        send(c_side[1][d - 1], r.gathered.at[other_sub], r.gathered.at[other_sub], beside[d - 1])
    for which in range(2):
        for d in (1, 2, 3):
            group = 2 * ((x + 4 - d) % 4) + (far if which == 0 else 1 - far)
            receive(c_side[which][d - 1], r.gathered.at[group])

    found = r.gathered[...].reshape(shots // 8, 2, 8, size)
    found = jnp.stack([found[:, 0], found[:, 1]], axis=0).reshape(2 * shots, size)
    r.found_high[...], r.found_low[...] = halves(found)
    turned = found.T
    r.separator_out[0] = turned[:, :shots]
    r.separator_out[1] = turned[:, shots:]

    def interior_of(b, carry):
        left = (r.found_high[...], r.found_low[...])
        out = [
            dot3(left, (r.coupling_high[b, part], r.coupling_low[b, part])) for part in range(2)
        ]
        turned = (r.eliminated[b] - combine(out[0], out[1], 0)).T
        r.interior_out[b, 0] = turned[:, :shots]
        r.interior_out[b, 1] = turned[:, shots:]
        return carry

    lax.fori_loop(0, blocks, interior_of, 0)

    for copy, when in unsent:
        if when is None:
            copy.wait_send()
        else:
            pl.when(when)(copy.wait_send)


CHANNELS = 40


def body(
    rhs_interior,
    rhs_separator,
    inverse_blocks,
    coupling,
    separator_rows,
    separator_inverse,
    transfer,
):
    _, nb, _, m, shots = rhs_interior.shape
    size = transfer.shape[-1]
    vmem = pltpu.VMEM
    inputs = {
        "rows": separator_rows[0],
        "given": rhs_separator[0],
        "rhs_hbm": rhs_interior[0],
        "inverse_hbm": inverse_blocks[0],
        "coupling_hbm": coupling[0],
        "schur_hbm": separator_inverse[0],
        "transfer_hbm": transfer[0],
    }
    outputs = {
        "interior_out": jax.ShapeDtypeStruct((nb, 2, m, shots), F32),
        "separator_out": jax.ShapeDtypeStruct((2, size, shots), F32),
    }
    scratch = {
        "inverse": vmem((nb, 2, m, m), F32),
        "inverse_high": vmem((nb, 2, m, m), BF16),
        "inverse_low": vmem((nb, 2, m, m), BF16),
        "rhs": vmem((nb, 2, m, shots), F32),
        "coupling": vmem((nb, 2, size, m), F32),
        "coupling_high": vmem((nb, 2, size, m), BF16),
        "coupling_low": vmem((nb, 2, size, m), BF16),
        "spread": vmem((nb, size, size), BF16),
        "placed_high": vmem((2, size, m), BF16),
        "placed_low": vmem((2, size, m), BF16),
        "eliminated": vmem((nb, m, 2 * shots), F32),
        "rhs_high": vmem((m, 2 * shots), BF16),
        "rhs_low": vmem((m, 2 * shots), BF16),
        "known_high": vmem((m, 2 * shots), BF16),
        "known_low": vmem((m, 2 * shots), BF16),
        "weighted_high": vmem((size, 2 * shots), BF16),
        "weighted_low": vmem((size, 2 * shots), BF16),
        "total": vmem((size, 2 * shots), F32),
        "load": vmem((8, 32, size), F32),
        "from_x": vmem((2, 3, 32, size), F32),
        "forward_sum": vmem((32, size), F32),
        "from_z": vmem((32, size), F32),
        "schur": vmem((2, size, size), F32),
        "schur_high": vmem((2, size, size), BF16),
        "schur_low": vmem((2, size, size), BF16),
        "pair": vmem((2, 2, size, size), F32),
        "pair_high": vmem((2, 2, size, size), BF16),
        "pair_low": vmem((2, 2, size, size), BF16),
        "twos": vmem((2, size // STRIP, 2, STRIP, size), F32),
        "two_high": vmem((2, 2, size, size), BF16),
        "two_low": vmem((2, 2, size, size), BF16),
        "four_high": vmem((2, size, size), BF16),
        "four_low": vmem((2, size, size), BF16),
        "four_out": vmem((size // STRIP // 2, 2, STRIP, size), F32),
        "four_in": vmem((size // STRIP, 2, STRIP, size), F32),
        "top_high": vmem((2, size, size), BF16),
        "top_low": vmem((2, size, size), BF16),
        "upper_in": vmem((16, size), F32),
        "lower": vmem((16, size), F32),
        "lower_in": vmem((16, size), F32),
        "spare": vmem((2, 16, size), F32),
        "local": vmem((2, 16, size), F32),
        "start": vmem((16, size), F32),
        "start_in": vmem((16, size), F32),
        "node_start": vmem((16, size), F32),
        "enter": vmem((16, size), F32),
        "ahead_in": vmem((16, size), F32),
        "ahead_out": vmem((16, size), F32),
        "trace": vmem((2, 16, size), F32),
        "queued": vmem((16, size), F32),
        "queued_in": vmem((16, size), F32),
        "back_in": vmem((16, size), F32),
        "back_out": vmem((16, size), F32),
        "carried": vmem((16, size), F32),
        "found": vmem((2, 16, size), F32),
        "gathered": vmem((8, 2, 16, size), F32),
        "found_high": vmem((2 * shots, size), BF16),
        "found_low": vmem((2 * shots, size), BF16),
        "send_sem": pltpu.SemaphoreType.DMA((CHANNELS,)),
        "recv_sem": pltpu.SemaphoreType.DMA((CHANNELS,)),
        "here_sem": pltpu.SemaphoreType.DMA((2,)),
        "block_sem": pltpu.SemaphoreType.DMA((3, nb)),
    }
    names = list(inputs) + list(outputs) + list(scratch)

    def sweep_kernel(*refs):
        kernel(names, *refs)

    interior, separator = pl.pallas_call(
        sweep_kernel,
        out_shape=tuple(outputs.values()),
        in_specs=[pl.BlockSpec(memory_space=pltpu.VMEM)] * 2
        + [pl.BlockSpec(memory_space=pltpu.HBM)] * (len(inputs) - 2),
        out_specs=(pl.BlockSpec(memory_space=pltpu.VMEM),) * 2,
        scratch_shapes=list(scratch.values()),
        compiler_params=pltpu.CompilerParams(
            collective_id=0, has_side_effects=True, vmem_limit_bytes=51 << 20
        ),
    )(*inputs.values())
    return (interior[None], separator[None])


def solution(mesh):
    in_specs = (
        P("slab", "sub", None, None, None),
        P("slab", None, None, None),
        P("slab", "sub", None, None, None),
        P("slab", "sub", None, None, None),
        P("slab", "sub", None),
        P("slab", None, None, None),
        P("slab", None, None, None),
    )
    out_specs = (P("slab", "sub", None, None, None), P("slab", None, None, None))
    return jax.shard_map(body, mesh=mesh, in_specs=in_specs, out_specs=out_specs, check_vma=False)
```

```python
import types

import jax
import jax.numpy as jnp
from jax import lax
from jax.experimental import pallas as pl
from jax.experimental.pallas import tpu as pltpu
from jax.sharding import PartitionSpec as P

MESH = pl.DeviceIdType.MESH
F32 = jnp.float32
BF16 = jnp.bfloat16
NN = (((1,), (0,)), ((), ()))
NT = (((1,), (1,)), ((), ()))
STRIP = 128
WIDE = 256


def halves(value):
    high = value.astype(BF16)
    return high, (value - high.astype(F32)).astype(BF16)


def dot(left, right, dims=NN):
    return lax.dot_general(left, right, dims, preferred_element_type=F32)


def dot3(left, right):
    return dot(
        jnp.concatenate([left[0], left[0], left[1]], axis=1),
        jnp.concatenate([right[0], right[1], right[0]], axis=0),
    )


def times(value, matrix, dims):
    high, low = matrix
    n = value.shape[0] // 2
    value_high, value_low = halves(value)
    both = jnp.concatenate([value_high, value_low], axis=0)
    out = []
    for part in range(2):
        whole = dot(both, high[part], dims)
        out.append(whole[: 2 * n] + (whole[2 * n :] + dot(value_high, low[part], dims)))
    return jnp.concatenate([out[0][:n] - out[1][n:], out[0][n:] + out[1][:n]], axis=0)


def kernel(names, *refs):
    r = types.SimpleNamespace(**dict(zip(names, refs)))
    slab, sub = lax.axis_index("slab"), lax.axis_index("sub")
    slabs = lax.axis_size("slab")
    core, role, duo = slab % 2, (slab // 2) % 2, slab // 4
    duos = slabs // 4
    x, far = sub // 2, sub % 2
    after, before = (2 * duos - 3 - duo) // (duos - 1), (duo + duos - 2) // (duos - 1)
    has_after, has_before = duo < duos - 1, duo > 0
    early, late = role == 0, role == 1
    row, upper = duo // 2, duo % 2
    rows = duos // 2
    row_after, row_before = (2 * rows - 3 - row) // (rows - 1), (row + rows - 2) // (rows - 1)
    has_row_after, has_row_before = row < rows - 1, row > 0
    leads = jnp.logical_and(early, upper == 0)
    helps = jnp.logical_and(early, upper == 1)
    enters = jnp.logical_and(late, upper == 0)
    ends = jnp.logical_and(late, upper == 1)
    node = jnp.logical_or(enters, helps)
    blocks, _, size, m = r.coupling_hbm.shape
    shots = r.rhs_hbm.shape[-1]

    other_core, other_sub = slab + 1 - 2 * core, 2 * x + 1 - far
    partner = (other_core, sub)
    opposite = (slab, other_sub)
    across = (other_core, other_sub)
    mate = (slab + 2 - 4 * role, sub)
    beside = [(slab, ((x + d) % 4) * 2 + far) for d in (1, 2, 3)]
    def chip_at(offset):
        return ((slab + slabs + offset) % slabs, sub)

    critical, other = chip_at(2 + 4 * upper), chip_at(4)
    last_early, last_late = chip_at(-4), chip_at(-2)
    next_lead, last_lead = ((slab + 8) % slabs, sub), ((slab + slabs - 8) % slabs, sub)

    count = [0]
    unsent = []

    def remote(index, source, target, device):
        return pltpu.make_async_remote_copy(
            src_ref=source,
            dst_ref=target,
            send_sem=r.send_sem.at[index],
            recv_sem=r.recv_sem.at[index],
            device_id=device,
            device_id_type=MESH,
        )

    def channel():
        count[0] += 1
        return count[0] - 1

    def send(index, source, target, device, when=None):
        copy = remote(index, source, target, device)
        if when is None:
            copy.start()
        unsent.append((copy, when))
        return copy

    def receive(index, target):
        remote(index, target, target, partner).wait_recv()

    def local_copies(b):
        return [
            pltpu.make_async_copy(r.inverse_hbm.at[b], r.inverse.at[b], r.block_sem.at[0, b]),
            pltpu.make_async_copy(r.rhs_hbm.at[b], r.rhs.at[b], r.block_sem.at[1, b]),
            pltpu.make_async_copy(r.coupling_hbm.at[b], r.coupling.at[b], r.block_sem.at[2, b]),
        ]

    own_transfer = pltpu.make_async_copy(r.transfer_hbm, r.pair.at[core], r.here_sem.at[0])
    own_schur = pltpu.make_async_copy(r.schur_hbm, r.schur, r.here_sem.at[1])
    own_transfer.start()
    for b in range(blocks):
        for copy in local_copies(b):
            copy.start()
    own_schur.start()

    r.total[...] = jnp.zeros_like(r.total)

    def spread_of(b, carry):
        for i in range(size // STRIP):
            at = slice(i * STRIP, (i + 1) * STRIP)
            place = lax.broadcasted_iota(jnp.int32, (STRIP, size), 0) + i * STRIP
            r.spread[b, at] = (place == r.rows[pl.ds(b, 1), :]).astype(BF16)
        return carry

    barrier = pltpu.get_barrier_semaphore()

    def greet(device):
        pl.semaphore_signal(barrier, inc=1, device_id=device, device_id_type=MESH)

    for device in [partner, opposite, across, mate] + beside:
        greet(device)

    for who, always, before_too, after_too in (
        (leads, (4,), (-4, -2, -8), (8,)),
        (enters, (2, 4), (-6,), ()),
        (helps, (-2, -4), (), (4, 6)),
        (ends, (-4,), (), (2,)),
    ):
        for when, offsets in (
            (who, always),
            (jnp.logical_and(who, has_row_before), before_too),
            (jnp.logical_and(who, has_row_after), after_too),
        ):
            if offsets:

                @pl.when(when)
                def _(offsets=offsets):
                    for offset in offsets:
                        greet(chip_at(offset))

    pl.semaphore_wait(
        barrier,
        7
        + (1 - role) * (1 - upper) * (1 + 3 * row_before + row_after)
        + role * (1 - upper) * (2 + row_before)
        + (1 - role) * upper * (2 + 2 * row_after)
        + role * upper * (1 + row_after),
    )

    c_transfer = channel()
    send(c_transfer, r.transfer_hbm, r.pair.at[core], partner)

    def combine(real, imag, axis):
        n = real.shape[axis] // 2
        if axis == 1:
            return jnp.concatenate(
                [real[:, :n] - imag[:, n:], real[:, n:] + imag[:, :n]], axis=1
            )
        return jnp.concatenate([real[:n] - imag[n:], real[n:] + imag[:n]], axis=0)

    def load_of(b, carry):
        for copy in local_copies(b):
            copy.wait()
        r.rhs_high[...], r.rhs_low[...] = halves(
            jnp.concatenate([r.rhs[b, 0], r.rhs[b, 1]], axis=1)
        )

        def strip(at, source, high, low, right):
            out = []
            for part in range(2):
                left = halves(source[b, part, at])
                high[b, part, at], low[b, part, at] = left
                out.append(dot3(left, right))
            return combine(out[0], out[1], 1)

        for i in range(m // WIDE):
            at = slice(i * WIDE, (i + 1) * WIDE)
            right = (r.rhs_high[...], r.rhs_low[...])
            value = strip(at, r.inverse, r.inverse_high, r.inverse_low, right)
            r.eliminated[b, at] = value
            r.known_high[at], r.known_low[at] = halves(value)
        for i in range(size // WIDE):
            at = slice(i * WIDE, (i + 1) * WIDE)
            right = (r.known_high[...], r.known_low[...])
            value = strip(at, r.coupling, r.coupling_high, r.coupling_low, right)
            r.weighted_high[at], r.weighted_low[at] = halves(value)
        for i in range(size // WIDE):
            at = slice(i * WIDE, (i + 1) * WIDE)
            spread = r.spread[b, at]
            r.total[at] += dot(
                jnp.concatenate([spread, spread], axis=1),
                jnp.concatenate([r.weighted_high[...], r.weighted_low[...]], axis=0),
            )
        return carry

    lax.fori_loop(0, blocks, spread_of, 0)
    lax.fori_loop(0, blocks // 2, load_of, 0)

    def split_pair(slot):
        def step_of(step, carry):
            at = pl.ds(pl.multiple_of(step * STRIP, STRIP), STRIP)
            for part in range(2):
                r.pair_high[slot, part, at, :], r.pair_low[slot, part, at, :] = halves(
                    r.pair[slot, part, at, :]
                )
            return carry

        lax.fori_loop(0, size // STRIP, step_of, 0)

    own_transfer.wait()
    split_pair(core)
    receive(c_transfer, r.pair.at[1 - core])
    split_pair(1 - core)
    first = (r.pair_high.at[0], r.pair_low.at[0])
    second = (r.pair_high.at[1], r.pair_low.at[1])

    def merged_rows(left, at, right):
        rows_high = jnp.concatenate([left[0][0, at, :], left[0][1, at, :]], axis=0)
        rows_low = jnp.concatenate([left[1][0, at, :], left[1][1, at, :]], axis=0)
        out = [dot3((rows_high, rows_low), (right[0][part], right[1][part])) for part in range(2)]
        return out[0][:STRIP] - out[1][STRIP:], out[0][STRIP:] + out[1][:STRIP]

    half = size // 2
    strips = half // STRIP

    def merge_two(step, carry):
        at = pl.ds(pl.multiple_of(core * half + step * STRIP, STRIP), STRIP)
        merged = merged_rows(second, at, first)
        for part in range(2):
            r.twos[role, strips * core + step, part] = merged[part]
        return carry

    lax.fori_loop(0, half // STRIP, merge_two, 0)
    c_half = channel()
    c_mate = channel()
    c_aside, c_pass = [[channel() for i in range(2)] for j in range(2)]
    odd = x % 2
    direct, indirect = strips * core + odd, strips * core + 1 - odd
    halved = r.twos.at[role, pl.ds(strips * core, strips)]
    send(c_half, halved, halved, partner)

    piece = r.twos.at[role, direct]
    send(c_mate, piece, piece, mate)

    lax.fori_loop(blocks // 2, blocks, load_of, 0)
    given = jnp.concatenate([r.given[0], r.given[1]], axis=1)
    rest = (jnp.where(sub == 0, given, jnp.zeros_like(given)) - r.total[...]).T
    rest = rest.reshape(2, shots // 8, 8, size)
    r.load[...] = jnp.stack([rest[0], rest[1]], axis=1).reshape(r.load.shape)

    c_x = [[channel() for d in range(3)] for which in range(2)]
    c_z = channel()
    for which in range(2):
        for d in (2, 1, 3):
            group = 2 * ((x + d) % 4) + (1 - far if which == 0 else far)
            send(
                c_x[which][d - 1], r.load.at[group], r.from_x.at[which, d - 1], beside[d - 1]
            )

    own_schur.wait()

    def split_schur(step, carry):
        at = pl.ds(pl.multiple_of(step * STRIP, STRIP), STRIP)
        for part in range(2):
            r.schur_high[part, :, at], r.schur_low[part, :, at] = halves(r.schur[part, at, :].T)
        return carry

    lax.fori_loop(0, size // STRIP, split_schur, 0)

    def side_sum(which, group):
        for d in range(3):
            receive(c_x[which][d], r.from_x.at[which, d])
        return (r.load[group] + r.from_x[which, 0]) + (r.from_x[which, 1] + r.from_x[which, 2])

    r.forward_sum[...] = side_sum(0, other_sub)
    send(c_z, r.forward_sum, r.from_z, opposite)

    piece = r.twos.at[1 - role, direct]
    receive(c_mate, piece)
    for part in range(2):
        aside = r.twos.at[1 - role, direct, part]
        send(c_aside[part], aside, aside, beside[2 * part])
    send(c_pass[0], piece, piece, partner)
    own_sum = side_sum(1, sub)

    receive(c_half, r.twos.at[role, pl.ds(strips * (1 - core), strips)])

    def split_two(which):
        def step_of(step, carry):
            to = pl.ds(pl.multiple_of(step * STRIP, STRIP), STRIP)
            for part in range(2):
                r.two_high[which, part, to, :], r.two_low[which, part, to, :] = halves(
                    r.twos[which, step, part]
                )
            return carry

        lax.fori_loop(0, size // STRIP, step_of, 0)

    split_two(role)
    two_early = (r.two_high.at[0], r.two_low.at[0])
    two_late = (r.two_high.at[1], r.two_low.at[1])
    four = (r.four_high, r.four_low)

    receive(c_z, r.from_z)
    summed = (own_sum + r.from_z[...]).reshape(2, 2, 8, size)
    summed = jnp.stack([summed[:, 0], summed[:, 1]], axis=0).reshape(32, size)
    solved = times(summed, (r.schur_high, r.schur_low), NN).reshape(2, 2, 8, size)
    solved = jnp.stack([solved[:, 0], solved[:, 1]], axis=0).reshape(2, 16, size)
    r.spare[...] = solved
    r.local[core] = r.spare[core]
    c_swap = channel()
    send(c_swap, r.spare.at[1 - core], r.local.at[core], partner)

    @pl.when(jnp.logical_not(has_before))
    def _():
        r.ahead_in[...] = jnp.zeros_like(r.ahead_in)

    @pl.when(jnp.logical_not(has_after))
    def _():
        r.back_in[...] = jnp.zeros_like(r.back_in)

    receive(c_swap, r.local.at[1 - core])
    start = r.local[1] - times(r.local[0], second, NT)
    c_start = channel()
    gives_start = jnp.logical_or(early, upper == 1)
    start_copy = send(c_start, r.start, r.start_in, mate, gives_start)
    r.start[...] = start
    pl.when(gives_start)(start_copy.start)

    c_node, c_other = channel(), channel()
    goes_on = jnp.logical_and(node, has_after)
    node_copy = send(c_node, r.ahead_out, r.ahead_in, critical, goes_on)
    other_copy = send(c_other, r.ahead_out, r.ahead_in, other, goes_on)

    @pl.when(enters)
    def _():
        receive(c_start, r.start_in)
        r.node_start[...] = r.start[...] + times(r.start_in[...], two_late, NT)

        @pl.when(jnp.logical_not(has_before))
        def _():
            r.ahead_out[...] = r.node_start[...]
            node_copy.start()
            other_copy.start()

    for part in range(2):
        receive(c_aside[part], r.twos.at[1 - role, indirect, part])
    piece = r.twos.at[1 - role, indirect]
    send(c_pass[1], piece, piece, partner)
    for i in range(2):
        receive(c_pass[i], r.twos.at[1 - role, strips * (1 - core) + (odd if i == 0 else 1 - odd)])
    split_two(1 - role)

    pl.when(ends)(lambda: receive(c_start, r.start_in))

    @pl.when(helps)
    def _():
        receive(c_start, r.start_in)
        r.node_start[...] = r.start_in[...] + times(r.start[...], two_late, NT)

    gives = jnp.logical_and(helps, has_row_after)
    takes = jnp.logical_and(leads, has_row_after)
    c_four, c_four_pass = [channel() for i in range(strips)], channel()
    half_four = pl.ds(strips * core, strips)
    four_copies = [
        send(c_four[i], r.four_out.at[i], r.four_in.at[strips * core + i], last_early, gives)
        for i in range(strips)
    ]
    soon = jnp.logical_and(helps, row == rows - 2)
    not_soon = jnp.logical_and(helps, row < rows - 2)

    @pl.when(jnp.logical_or(gives, jnp.logical_and(upper == 0, duo > 1)))
    def _():
        def merge_four(step, carry):
            at = pl.ds(pl.multiple_of(step * STRIP, STRIP), STRIP)
            merged = merged_rows(two_late, at, two_early)

            @pl.when(leads)
            def _():
                for part in range(2):
                    r.four_high[part, at, :], r.four_low[part, at, :] = halves(merged[part])

            @pl.when(node)
            def _():
                for part in range(2):
                    r.four_high[part, :, at], r.four_low[part, :, at] = halves(merged[part].T)

            @pl.when(step // strips == core)
            def _():
                for part in range(2):
                    r.four_out[step % strips, part] = merged[part]

            return carry

        whole = (duo + duos - 3) // (duos - 1)
        low = (1 - whole) * strips * core
        lax.fori_loop(low, low + strips * (1 + whole), merge_four, 0)
        pl.when(soon)(four_copies[0].start)

    def weights_of(b, carry):
        spread = r.spread[b]
        for part in range(2):
            r.placed_high[part] = dot(spread, r.coupling_high[b, part]).astype(BF16)
            r.placed_low[part] = dot(spread, r.coupling_low[b, part]).astype(BF16)

        def inverse(part):
            return r.inverse_high[b, part], r.inverse_low[b, part]

        def strip_of(step, carry):
            at = pl.ds(pl.multiple_of(step * STRIP, STRIP), STRIP)
            left = [
                jnp.concatenate([source[0, at, :], source[1, at, :]], axis=0)
                for source in (r.placed_high, r.placed_low)
            ]
            merged = combine(dot3(left, inverse(0)), dot3(left, inverse(1)), 0)
            for part in range(2):
                r.coupling_high[b, part, at, :], r.coupling_low[b, part, at, :] = halves(
                    merged[part * STRIP : (part + 1) * STRIP]
                )
            return carry

        lax.fori_loop(0, size // STRIP, strip_of, 0)
        left = halves(r.eliminated[b].T)
        r.eliminated[b] = combine(dot3(left, inverse(0)), dot3(left, inverse(1)), 0)
        return carry

    towards_end = duo >= duos - 2

    @pl.when(towards_end)
    def _():
        lax.fori_loop(0, blocks, weights_of, 0)

    @pl.when(jnp.logical_and(node, has_before))
    def _():
        receive(c_node, r.ahead_in)

        @pl.when(jnp.logical_and(duo > 1, has_after))
        def _():
            r.ahead_out[...] = r.node_start[...] + times(r.ahead_in[...], four, NN)

        @pl.when(duo == 1)
        def _():
            r.ahead_out[...] = r.node_start[...] + times(
                times(r.ahead_in[...], two_early, NT), two_late, NT
            )

        @pl.when(has_after)
        def _():
            node_copy.start()
            other_copy.start()

    pl.when(not_soon)(four_copies[0].start)

    @pl.when(gives)
    def _():
        for copy in four_copies[1:]:
            copy.start()

    @pl.when(ends)
    def _():
        receive(c_other, r.ahead_in)

    @pl.when(jnp.logical_and(leads, has_before))
    def _():
        receive(c_other, r.ahead_in)

    r.enter[...] = r.ahead_in[...]

    @pl.when(late)
    def _():
        r.enter[...] = r.start_in[...] + times(r.ahead_in[...], two_early, NT)

    r.trace[0] = r.local[0] - times(r.enter[...], first, NT)
    r.trace[1] = r.local[1] - times(r.trace[0], second, NT)
    queued = times(r.trace[0] - times(r.trace[1], second, NN), first, NN)
    r.queued[...] = queued
    c_queued = channel()
    queued_copy = send(c_queued, r.queued, r.queued_in, mate, late)
    pl.when(late)(queued_copy.start)

    @pl.when(jnp.logical_not(towards_end))
    def _():
        lax.fori_loop(0, blocks, weights_of, 0)

    c_upper, c_lower, c_lead, c_help, c_back_late = [channel() for i in range(5)]
    goes_back = jnp.logical_and(leads, has_row_before)
    upper_copy = send(c_upper, r.queued, r.upper_in, last_early, helps)
    lower_copy = send(c_lower, r.lower, r.lower_in, mate, leads)
    back_lead = send(c_lead, r.back_out, r.back_in, last_lead, goes_back)
    back_help = send(c_help, r.back_out, r.back_in, last_early, goes_back)
    back_late = send(c_back_late, r.back_out, r.back_in, last_late, goes_back)
    pass_copy = send(
        c_four_pass, r.four_in.at[half_four], r.four_in.at[half_four], partner, takes
    )
    top = (r.top_high, r.top_low)

    @pl.when(early)
    def _():
        receive(c_queued, r.queued_in)
        r.queued[...] += times(r.queued_in[...], two_early, NN)

    @pl.when(helps)
    def _():
        upper_copy.start()
        pl.when(has_row_after)(lambda: receive(c_help, r.back_in))
        r.carried[...] = r.queued_in[...] + times(r.back_in[...], two_late, NN)

    @pl.when(leads)
    def _():
        @pl.when(has_row_after)
        def _():
            for i in range(strips):
                receive(c_four[i], r.four_in.at[strips * core + i])
            pass_copy.start()
            receive(c_four_pass, r.four_in.at[pl.ds(strips * (1 - core), strips)])

            def split_top(step, carry):
                to = pl.ds(pl.multiple_of(step * STRIP, STRIP), STRIP)
                for part in range(2):
                    r.top_high[part, to, :], r.top_low[part, to, :] = halves(r.four_in[step, part])
                return carry

            lax.fori_loop(0, size // STRIP, split_top, 0)

        receive(c_upper, r.upper_in)

        @pl.when(has_row_after)
        def _():
            receive(c_lead, r.back_in)
            r.lower[...] = r.upper_in[...] + times(r.back_in[...], top, NN)

        @pl.when(jnp.logical_not(has_row_after))
        def _():
            r.lower[...] = r.upper_in[...]

        lower_copy.start()

        @pl.when(has_row_before)
        def _():
            r.back_out[...] = r.queued[...] + times(r.lower[...], four, NN)
            back_lead.start()
            back_help.start()
            back_late.start()

        r.carried[...] = r.queued_in[...] + times(r.lower[...], two_late, NN)

    @pl.when(ends)
    def _():
        pl.when(has_row_after)(lambda: receive(c_back_late, r.back_in))
        r.carried[...] = r.back_in[...]

    @pl.when(enters)
    def _():
        receive(c_lower, r.lower_in)
        r.carried[...] = r.lower_in[...]

    r.found[1] = r.trace[1] - r.carried[...]
    r.found[0] = r.trace[0] - times(r.found[1], second, NN)

    c_chip, c_far, c_across = channel(), channel(), channel()
    c_side = [[channel() for d in range(3)] for which in range(2)]
    place = r.gathered.at[sub, core]
    send(c_chip, r.found.at[1 - core], place, partner)
    send(c_far, r.found.at[core], place, opposite)
    send(c_across, r.found.at[1 - core], place, across)
    r.gathered[sub, core] = r.found[core]
    receive(c_chip, r.gathered.at[sub, 1 - core])
    for d in (2, 1, 3):
        send(c_side[0][d - 1], r.gathered.at[sub], r.gathered.at[sub], beside[d - 1])
    receive(c_far, r.gathered.at[other_sub, core])
    receive(c_across, r.gathered.at[other_sub, 1 - core])
    for d in (2, 1, 3):
        send(c_side[1][d - 1], r.gathered.at[other_sub], r.gathered.at[other_sub], beside[d - 1])
    for which in range(2):
        for d in (1, 2, 3):
            group = 2 * ((x + 4 - d) % 4) + (far if which == 0 else 1 - far)
            receive(c_side[which][d - 1], r.gathered.at[group])

    found = r.gathered[...].reshape(shots // 8, 2, 8, size)
    found = jnp.stack([found[:, 0], found[:, 1]], axis=0).reshape(2 * shots, size)
    r.found_high[...], r.found_low[...] = halves(found)
    turned = found.T
    r.separator_out[0] = turned[:, :shots]
    r.separator_out[1] = turned[:, shots:]

    def interior_of(b, carry):
        left = (r.found_high[...], r.found_low[...])
        out = [
            dot3(left, (r.coupling_high[b, part], r.coupling_low[b, part])) for part in range(2)
        ]
        turned = (r.eliminated[b] - combine(out[0], out[1], 0)).T
        r.interior_out[b, 0] = turned[:, :shots]
        r.interior_out[b, 1] = turned[:, shots:]
        return carry

    lax.fori_loop(0, blocks, interior_of, 0)

    for copy, when in unsent:
        if when is None:
            copy.wait_send()
        else:
            pl.when(when)(copy.wait_send)


CHANNELS = 44


def body(
    rhs_interior,
    rhs_separator,
    inverse_blocks,
    coupling,
    separator_rows,
    separator_inverse,
    transfer,
):
    _, nb, _, m, shots = rhs_interior.shape
    size = transfer.shape[-1]
    vmem = pltpu.VMEM
    inputs = {
        "rows": separator_rows[0],
        "given": rhs_separator[0],
        "rhs_hbm": rhs_interior[0],
        "inverse_hbm": inverse_blocks[0],
        "coupling_hbm": coupling[0],
        "schur_hbm": separator_inverse[0],
        "transfer_hbm": transfer[0],
    }
    outputs = {
        "interior_out": jax.ShapeDtypeStruct((nb, 2, m, shots), F32),
        "separator_out": jax.ShapeDtypeStruct((2, size, shots), F32),
    }
    scratch = {
        "inverse": vmem((nb, 2, m, m), F32),
        "inverse_high": vmem((nb, 2, m, m), BF16),
        "inverse_low": vmem((nb, 2, m, m), BF16),
        "rhs": vmem((nb, 2, m, shots), F32),
        "coupling": vmem((nb, 2, size, m), F32),
        "coupling_high": vmem((nb, 2, size, m), BF16),
        "coupling_low": vmem((nb, 2, size, m), BF16),
        "spread": vmem((nb, size, size), BF16),
        "placed_high": vmem((2, size, m), BF16),
        "placed_low": vmem((2, size, m), BF16),
        "eliminated": vmem((nb, m, 2 * shots), F32),
        "rhs_high": vmem((m, 2 * shots), BF16),
        "rhs_low": vmem((m, 2 * shots), BF16),
        "known_high": vmem((m, 2 * shots), BF16),
        "known_low": vmem((m, 2 * shots), BF16),
        "weighted_high": vmem((size, 2 * shots), BF16),
        "weighted_low": vmem((size, 2 * shots), BF16),
        "total": vmem((size, 2 * shots), F32),
        "load": vmem((8, 32, size), F32),
        "from_x": vmem((2, 3, 32, size), F32),
        "forward_sum": vmem((32, size), F32),
        "from_z": vmem((32, size), F32),
        "schur": vmem((2, size, size), F32),
        "schur_high": vmem((2, size, size), BF16),
        "schur_low": vmem((2, size, size), BF16),
        "pair": vmem((2, 2, size, size), F32),
        "pair_high": vmem((2, 2, size, size), BF16),
        "pair_low": vmem((2, 2, size, size), BF16),
        "twos": vmem((2, size // STRIP, 2, STRIP, size), F32),
        "two_high": vmem((2, 2, size, size), BF16),
        "two_low": vmem((2, 2, size, size), BF16),
        "four_high": vmem((2, size, size), BF16),
        "four_low": vmem((2, size, size), BF16),
        "four_out": vmem((size // STRIP // 2, 2, STRIP, size), F32),
        "four_in": vmem((size // STRIP, 2, STRIP, size), F32),
        "top_high": vmem((2, size, size), BF16),
        "top_low": vmem((2, size, size), BF16),
        "upper_in": vmem((16, size), F32),
        "lower": vmem((16, size), F32),
        "lower_in": vmem((16, size), F32),
        "spare": vmem((2, 16, size), F32),
        "local": vmem((2, 16, size), F32),
        "start": vmem((16, size), F32),
        "start_in": vmem((16, size), F32),
        "node_start": vmem((16, size), F32),
        "enter": vmem((16, size), F32),
        "ahead_in": vmem((16, size), F32),
        "ahead_out": vmem((16, size), F32),
        "trace": vmem((2, 16, size), F32),
        "queued": vmem((16, size), F32),
        "queued_in": vmem((16, size), F32),
        "back_in": vmem((16, size), F32),
        "back_out": vmem((16, size), F32),
        "carried": vmem((16, size), F32),
        "found": vmem((2, 16, size), F32),
        "gathered": vmem((8, 2, 16, size), F32),
        "found_high": vmem((2 * shots, size), BF16),
        "found_low": vmem((2 * shots, size), BF16),
        "send_sem": pltpu.SemaphoreType.DMA((CHANNELS,)),
        "recv_sem": pltpu.SemaphoreType.DMA((CHANNELS,)),
        "here_sem": pltpu.SemaphoreType.DMA((2,)),
        "block_sem": pltpu.SemaphoreType.DMA((3, nb)),
    }
    names = list(inputs) + list(outputs) + list(scratch)

    def sweep_kernel(*refs):
        kernel(names, *refs)

    interior, separator = pl.pallas_call(
        sweep_kernel,
        out_shape=tuple(outputs.values()),
        in_specs=[pl.BlockSpec(memory_space=pltpu.VMEM)] * 2
        + [pl.BlockSpec(memory_space=pltpu.HBM)] * (len(inputs) - 2),
        out_specs=(pl.BlockSpec(memory_space=pltpu.VMEM),) * 2,
        scratch_shapes=list(scratch.values()),
        compiler_params=pltpu.CompilerParams(
            collective_id=0, has_side_effects=True, vmem_limit_bytes=51 << 20
        ),
    )(*inputs.values())
    return (interior[None], separator[None])


def solution(mesh):
    in_specs = (
        P("slab", "sub", None, None, None),
        P("slab", None, None, None),
        P("slab", "sub", None, None, None),
        P("slab", "sub", None, None, None),
        P("slab", "sub", None),
        P("slab", None, None, None),
        P("slab", None, None, None),
    )
    out_specs = (P("slab", "sub", None, None, None), P("slab", None, None, None))
    return jax.shard_map(body, mesh=mesh, in_specs=in_specs, out_specs=out_specs, check_vma=False)
```

```python
import types

import jax
import jax.numpy as jnp
from jax import lax
from jax.experimental import pallas as pl
from jax.experimental.pallas import tpu as pltpu
from jax.sharding import PartitionSpec as P

MESH = pl.DeviceIdType.MESH
F32 = jnp.float32
BF16 = jnp.bfloat16
NN = (((1,), (0,)), ((), ()))
NT = (((1,), (1,)), ((), ()))
STRIP = 128
WIDE = 256


def halves(value):
    high = value.astype(BF16)
    return high, (value - high.astype(F32)).astype(BF16)


def dot(left, right, dims=NN):
    return lax.dot_general(left, right, dims, preferred_element_type=F32)


def dot3(left, right):
    return dot(
        jnp.concatenate([left[0], left[0], left[1]], axis=1),
        jnp.concatenate([right[0], right[1], right[0]], axis=0),
    )


def times(value, matrix, dims):
    high, low = matrix
    n = value.shape[0] // 2
    value_high, value_low = halves(value)
    both = jnp.concatenate([value_high, value_low], axis=0)
    out = []
    for part in range(2):
        whole = dot(both, high[part], dims)
        out.append(whole[: 2 * n] + (whole[2 * n :] + dot(value_high, low[part], dims)))
    return jnp.concatenate([out[0][:n] - out[1][n:], out[0][n:] + out[1][:n]], axis=0)


def kernel(names, *refs):
    r = types.SimpleNamespace(**dict(zip(names, refs)))
    slab, sub = lax.axis_index("slab"), lax.axis_index("sub")
    slabs = lax.axis_size("slab")
    core, role, duo = slab % 2, (slab // 2) % 2, slab // 4
    duos = slabs // 4
    x, far = sub // 2, sub % 2
    after, before = (2 * duos - 3 - duo) // (duos - 1), (duo + duos - 2) // (duos - 1)
    has_after, has_before = duo < duos - 1, duo > 0
    early, late = role == 0, role == 1
    row, upper = duo // 2, duo % 2
    rows = duos // 2
    row_after, row_before = (2 * rows - 3 - row) // (rows - 1), (row + rows - 2) // (rows - 1)
    has_row_after, has_row_before = row < rows - 1, row > 0
    leads = jnp.logical_and(early, upper == 0)
    helps = jnp.logical_and(early, upper == 1)
    enters = jnp.logical_and(late, upper == 0)
    ends = jnp.logical_and(late, upper == 1)
    node = jnp.logical_or(enters, helps)
    blocks, _, size, m = r.coupling_hbm.shape
    shots = r.rhs_hbm.shape[-1]

    other_core, other_sub = slab + 1 - 2 * core, 2 * x + 1 - far
    partner = (other_core, sub)
    opposite = (slab, other_sub)
    across = (other_core, other_sub)
    mate = (slab + 2 - 4 * role, sub)
    beside = [(slab, ((x + d) % 4) * 2 + far) for d in (1, 2, 3)]
    def chip_at(offset):
        return ((slab + slabs + offset) % slabs, sub)

    critical, other = chip_at(2 + 4 * upper), chip_at(4)
    last_early, last_late = chip_at(-4), chip_at(-2)
    next_lead, last_lead = ((slab + 8) % slabs, sub), ((slab + slabs - 8) % slabs, sub)

    count = [0]
    unsent = []

    def remote(index, source, target, device):
        return pltpu.make_async_remote_copy(
            src_ref=source,
            dst_ref=target,
            send_sem=r.send_sem.at[index],
            recv_sem=r.recv_sem.at[index],
            device_id=device,
            device_id_type=MESH,
        )

    def channel():
        count[0] += 1
        return count[0] - 1

    def send(index, source, target, device, when=None):
        copy = remote(index, source, target, device)
        if when is None:
            copy.start()
        unsent.append((copy, when))
        return copy

    def receive(index, target):
        remote(index, target, target, partner).wait_recv()

    def local_copies(b):
        return [
            pltpu.make_async_copy(r.inverse_hbm.at[b], r.inverse.at[b], r.block_sem.at[0, b]),
            pltpu.make_async_copy(r.rhs_hbm.at[b], r.rhs.at[b], r.block_sem.at[1, b]),
            pltpu.make_async_copy(r.coupling_hbm.at[b], r.coupling.at[b], r.block_sem.at[2, b]),
        ]

    own_transfer = pltpu.make_async_copy(r.transfer_hbm, r.pair.at[core], r.here_sem.at[0])
    own_schur = pltpu.make_async_copy(r.schur_hbm, r.schur, r.here_sem.at[1])
    own_transfer.start()
    for b in range(blocks):
        for copy in local_copies(b):
            copy.start()
    own_schur.start()

    r.total[...] = jnp.zeros_like(r.total)

    def spread_of(b, carry):
        for i in range(size // STRIP):
            at = slice(i * STRIP, (i + 1) * STRIP)
            place = lax.broadcasted_iota(jnp.int32, (STRIP, size), 0) + i * STRIP
            r.spread[b, at] = (place == r.rows[pl.ds(b, 1), :]).astype(BF16)
        return carry

    barrier = pltpu.get_barrier_semaphore()

    def greet(device):
        pl.semaphore_signal(barrier, inc=1, device_id=device, device_id_type=MESH)

    for device in [partner, opposite, across, mate] + beside:
        greet(device)

    for who, always, before_too, after_too in (
        (leads, (4,), (-4, -2, -8), (8,)),
        (enters, (2, 4), (-6,), ()),
        (helps, (-2, -4), (), (4, 6)),
        (ends, (-4,), (), (2,)),
    ):
        for when, offsets in (
            (who, always),
            (jnp.logical_and(who, has_row_before), before_too),
            (jnp.logical_and(who, has_row_after), after_too),
        ):
            if offsets:

                @pl.when(when)
                def _(offsets=offsets):
                    for offset in offsets:
                        greet(chip_at(offset))

    pl.semaphore_wait(
        barrier,
        7
        + (1 - role) * (1 - upper) * (1 + 3 * row_before + row_after)
        + role * (1 - upper) * (2 + row_before)
        + (1 - role) * upper * (2 + 2 * row_after)
        + role * upper * (1 + row_after),
    )

    c_transfer = channel()
    send(c_transfer, r.transfer_hbm, r.pair.at[core], partner)

    def combine(real, imag, axis):
        n = real.shape[axis] // 2
        if axis == 1:
            return jnp.concatenate(
                [real[:, :n] - imag[:, n:], real[:, n:] + imag[:, :n]], axis=1
            )
        return jnp.concatenate([real[:n] - imag[n:], real[n:] + imag[:n]], axis=0)

    def load_of(b, carry):
        for copy in local_copies(b):
            copy.wait()
        r.rhs_high[...], r.rhs_low[...] = halves(
            jnp.concatenate([r.rhs[b, 0], r.rhs[b, 1]], axis=1)
        )

        def strip(at, source, high, low, right):
            out = []
            for part in range(2):
                left = halves(source[b, part, at])
                high[b, part, at], low[b, part, at] = left
                out.append(dot3(left, right))
            return combine(out[0], out[1], 1)

        for i in range(m // WIDE):
            at = slice(i * WIDE, (i + 1) * WIDE)
            right = (r.rhs_high[...], r.rhs_low[...])
            value = strip(at, r.inverse, r.inverse_high, r.inverse_low, right)
            r.eliminated[b, at] = value
            r.known_high[at], r.known_low[at] = halves(value)
        for i in range(size // WIDE):
            at = slice(i * WIDE, (i + 1) * WIDE)
            right = (r.known_high[...], r.known_low[...])
            value = strip(at, r.coupling, r.coupling_high, r.coupling_low, right)
            r.weighted_high[at], r.weighted_low[at] = halves(value)
        for i in range(size // WIDE):
            at = slice(i * WIDE, (i + 1) * WIDE)
            spread = r.spread[b, at]
            r.total[at] += dot(
                jnp.concatenate([spread, spread], axis=1),
                jnp.concatenate([r.weighted_high[...], r.weighted_low[...]], axis=0),
            )
        return carry

    lax.fori_loop(0, blocks, spread_of, 0)
    lax.fori_loop(0, blocks // 2, load_of, 0)

    def split_pair(slot):
        def step_of(step, carry):
            at = pl.ds(pl.multiple_of(step * STRIP, STRIP), STRIP)
            for part in range(2):
                r.pair_high[slot, part, at, :], r.pair_low[slot, part, at, :] = halves(
                    r.pair[slot, part, at, :]
                )
            return carry

        lax.fori_loop(0, size // STRIP, step_of, 0)

    own_transfer.wait()
    split_pair(core)
    receive(c_transfer, r.pair.at[1 - core])
    split_pair(1 - core)
    first = (r.pair_high.at[0], r.pair_low.at[0])
    second = (r.pair_high.at[1], r.pair_low.at[1])

    def merged_rows(left, at, right):
        rows_high = jnp.concatenate([left[0][0, at, :], left[0][1, at, :]], axis=0)
        rows_low = jnp.concatenate([left[1][0, at, :], left[1][1, at, :]], axis=0)
        out = [dot3((rows_high, rows_low), (right[0][part], right[1][part])) for part in range(2)]
        return out[0][:STRIP] - out[1][STRIP:], out[0][STRIP:] + out[1][:STRIP]

    half = size // 2
    strips = half // STRIP

    def merge_two(step, carry):
        at = pl.ds(pl.multiple_of(core * half + step * STRIP, STRIP), STRIP)
        merged = merged_rows(second, at, first)
        for part in range(2):
            r.twos[role, strips * core + step, part] = merged[part]
        return carry

    lax.fori_loop(0, half // STRIP, merge_two, 0)
    c_half = channel()
    c_mate = channel()
    c_aside, c_pass = [[channel() for i in range(2)] for j in range(2)]
    odd = x % 2
    direct, indirect = strips * core + odd, strips * core + 1 - odd
    halved = r.twos.at[role, pl.ds(strips * core, strips)]
    send(c_half, halved, halved, partner)

    piece = r.twos.at[role, direct]
    send(c_mate, piece, piece, mate)

    lax.fori_loop(blocks // 2, blocks, load_of, 0)
    given = jnp.concatenate([r.given[0], r.given[1]], axis=1)
    rest = (jnp.where(sub == 0, given, jnp.zeros_like(given)) - r.total[...]).T
    rest = rest.reshape(2, shots // 8, 8, size)
    r.load[...] = jnp.stack([rest[0], rest[1]], axis=1).reshape(r.load.shape)

    c_x = [[channel() for d in range(3)] for which in range(2)]
    c_z = channel()
    for which in range(2):
        for d in (2, 1, 3):
            group = 2 * ((x + d) % 4) + (1 - far if which == 0 else far)
            send(
                c_x[which][d - 1], r.load.at[group], r.from_x.at[which, d - 1], beside[d - 1]
            )

    own_schur.wait()

    def split_schur(step, carry):
        at = pl.ds(pl.multiple_of(step * STRIP, STRIP), STRIP)
        for part in range(2):
            r.schur_high[part, :, at], r.schur_low[part, :, at] = halves(r.schur[part, at, :].T)
        return carry

    lax.fori_loop(0, size // STRIP, split_schur, 0)

    def side_sum(which, group):
        for d in range(3):
            receive(c_x[which][d], r.from_x.at[which, d])
        return (r.load[group] + r.from_x[which, 0]) + (r.from_x[which, 1] + r.from_x[which, 2])

    r.forward_sum[...] = side_sum(0, other_sub)
    send(c_z, r.forward_sum, r.from_z, opposite)

    piece = r.twos.at[1 - role, direct]
    receive(c_mate, piece)
    for part in range(2):
        aside = r.twos.at[1 - role, direct, part]
        send(c_aside[part], aside, aside, beside[2 * part])
    send(c_pass[0], piece, piece, partner)
    own_sum = side_sum(1, sub)

    receive(c_half, r.twos.at[role, pl.ds(strips * (1 - core), strips)])

    def split_two(which):
        def step_of(step, carry):
            to = pl.ds(pl.multiple_of(step * STRIP, STRIP), STRIP)
            for part in range(2):
                r.two_high[which, part, to, :], r.two_low[which, part, to, :] = halves(
                    r.twos[which, step, part]
                )
            return carry

        lax.fori_loop(0, size // STRIP, step_of, 0)

    split_two(role)
    two_early = (r.two_high.at[0], r.two_low.at[0])
    two_late = (r.two_high.at[1], r.two_low.at[1])
    four = (r.four_high, r.four_low)

    receive(c_z, r.from_z)
    summed = (own_sum + r.from_z[...]).reshape(2, 2, 8, size)
    summed = jnp.stack([summed[:, 0], summed[:, 1]], axis=0).reshape(32, size)
    solved = times(summed, (r.schur_high, r.schur_low), NN).reshape(2, 2, 8, size)
    solved = jnp.stack([solved[:, 0], solved[:, 1]], axis=0).reshape(2, 16, size)
    r.spare[...] = solved
    r.local[core] = r.spare[core]
    c_swap = channel()
    send(c_swap, r.spare.at[1 - core], r.local.at[core], partner)

    @pl.when(jnp.logical_not(has_before))
    def _():
        r.ahead_in[...] = jnp.zeros_like(r.ahead_in)

    @pl.when(jnp.logical_not(has_after))
    def _():
        r.back_in[...] = jnp.zeros_like(r.back_in)

    receive(c_swap, r.local.at[1 - core])
    start = r.local[1] - times(r.local[0], second, NT)
    c_start = channel()
    gives_start = jnp.logical_or(early, upper == 1)
    start_copy = send(c_start, r.start, r.start_in, mate, gives_start)
    r.start[...] = start
    pl.when(gives_start)(start_copy.start)

    c_node, c_other = channel(), channel()
    goes_on = jnp.logical_and(node, has_after)
    node_copy = send(c_node, r.ahead_out, r.ahead_in, critical, goes_on)
    other_copy = send(c_other, r.ahead_out, r.ahead_in, other, goes_on)

    @pl.when(enters)
    def _():
        receive(c_start, r.start_in)
        r.node_start[...] = r.start[...] + times(r.start_in[...], two_late, NT)

        @pl.when(jnp.logical_not(has_before))
        def _():
            r.ahead_out[...] = r.node_start[...]
            node_copy.start()
            other_copy.start()

    for part in range(2):
        receive(c_aside[part], r.twos.at[1 - role, indirect, part])
    piece = r.twos.at[1 - role, indirect]
    send(c_pass[1], piece, piece, partner)
    for i in range(2):
        receive(c_pass[i], r.twos.at[1 - role, strips * (1 - core) + (odd if i == 0 else 1 - odd)])
    split_two(1 - role)

    pl.when(ends)(lambda: receive(c_start, r.start_in))

    @pl.when(helps)
    def _():
        receive(c_start, r.start_in)
        r.node_start[...] = r.start_in[...] + times(r.start[...], two_late, NT)

    gives = jnp.logical_and(helps, has_row_after)
    takes = jnp.logical_and(leads, has_row_after)
    c_four = channel()
    c_four_aside, c_four_pass = [[channel() for i in range(2)] for j in range(2)]
    four_copy = send(c_four, r.four_out, r.four_in.at[direct], last_early, gives)
    soon = jnp.logical_and(helps, row == rows - 2)
    not_soon = jnp.logical_and(helps, row < rows - 2)

    def give():
        at = pl.ds(pl.multiple_of(direct * STRIP, STRIP), STRIP)
        merged = merged_rows(two_late, at, two_early)
        for part in range(2):
            r.four_out[part] = merged[part]
        four_copy.start()

    pl.when(soon)(give)

    @pl.when(jnp.logical_and(duo > 1, jnp.logical_or(gives, upper == 0)))
    def _():
        def merge_four(step, carry):
            at = pl.ds(pl.multiple_of(step * STRIP, STRIP), STRIP)
            merged = merged_rows(two_late, at, two_early)

            @pl.when(leads)
            def _():
                for part in range(2):
                    r.four_high[part, at, :], r.four_low[part, at, :] = halves(merged[part])

            @pl.when(node)
            def _():
                for part in range(2):
                    r.four_high[part, :, at], r.four_low[part, :, at] = halves(merged[part].T)

            return carry

        lax.fori_loop(0, size // STRIP, merge_four, 0)

    def weights_of(b, carry):
        spread = r.spread[b]
        for part in range(2):
            r.placed_high[part] = dot(spread, r.coupling_high[b, part]).astype(BF16)
            r.placed_low[part] = dot(spread, r.coupling_low[b, part]).astype(BF16)

        def inverse(part):
            return r.inverse_high[b, part], r.inverse_low[b, part]

        def strip_of(step, carry):
            at = pl.ds(pl.multiple_of(step * STRIP, STRIP), STRIP)
            left = [
                jnp.concatenate([source[0, at, :], source[1, at, :]], axis=0)
                for source in (r.placed_high, r.placed_low)
            ]
            merged = combine(dot3(left, inverse(0)), dot3(left, inverse(1)), 0)
            for part in range(2):
                r.coupling_high[b, part, at, :], r.coupling_low[b, part, at, :] = halves(
                    merged[part * STRIP : (part + 1) * STRIP]
                )
            return carry

        lax.fori_loop(0, size // STRIP, strip_of, 0)
        left = halves(r.eliminated[b].T)
        r.eliminated[b] = combine(dot3(left, inverse(0)), dot3(left, inverse(1)), 0)
        return carry

    towards_end = duo >= duos - 2

    @pl.when(towards_end)
    def _():
        lax.fori_loop(0, blocks, weights_of, 0)

    @pl.when(jnp.logical_and(node, has_before))
    def _():
        receive(c_node, r.ahead_in)

        @pl.when(jnp.logical_and(duo > 1, has_after))
        def _():
            r.ahead_out[...] = r.node_start[...] + times(r.ahead_in[...], four, NN)

        @pl.when(duo == 1)
        def _():
            r.ahead_out[...] = r.node_start[...] + times(
                times(r.ahead_in[...], two_early, NT), two_late, NT
            )

        @pl.when(has_after)
        def _():
            node_copy.start()
            other_copy.start()

    pl.when(not_soon)(give)

    @pl.when(ends)
    def _():
        receive(c_other, r.ahead_in)

    @pl.when(jnp.logical_and(leads, has_before))
    def _():
        receive(c_other, r.ahead_in)

    r.enter[...] = r.ahead_in[...]

    @pl.when(late)
    def _():
        r.enter[...] = r.start_in[...] + times(r.ahead_in[...], two_early, NT)

    r.trace[0] = r.local[0] - times(r.enter[...], first, NT)
    r.trace[1] = r.local[1] - times(r.trace[0], second, NT)
    queued = times(r.trace[0] - times(r.trace[1], second, NN), first, NN)
    r.queued[...] = queued
    c_queued = channel()
    queued_copy = send(c_queued, r.queued, r.queued_in, mate, late)
    pl.when(late)(queued_copy.start)

    @pl.when(jnp.logical_not(towards_end))
    def _():
        lax.fori_loop(0, blocks, weights_of, 0)

    c_upper, c_lower, c_lead, c_help, c_back_late = [channel() for i in range(5)]
    goes_back = jnp.logical_and(leads, has_row_before)
    upper_copy = send(c_upper, r.queued, r.upper_in, last_early, helps)
    lower_copy = send(c_lower, r.lower, r.lower_in, mate, leads)
    back_lead = send(c_lead, r.back_out, r.back_in, last_lead, goes_back)
    back_help = send(c_help, r.back_out, r.back_in, last_early, goes_back)
    back_late = send(c_back_late, r.back_out, r.back_in, last_late, goes_back)
    piece = r.four_in.at[direct]
    take_copies = [
        send(c_four_aside[part], piece.at[part], piece.at[part], beside[2 * part], takes)
        for part in range(2)
    ] + [send(c_four_pass[0], piece, piece, partner, takes)]
    piece = r.four_in.at[indirect]
    pass_copy = send(c_four_pass[1], piece, piece, partner, takes)
    top = (r.top_high, r.top_low)

    @pl.when(early)
    def _():
        receive(c_queued, r.queued_in)
        r.queued[...] += times(r.queued_in[...], two_early, NN)

    @pl.when(helps)
    def _():
        upper_copy.start()
        pl.when(has_row_after)(lambda: receive(c_help, r.back_in))
        r.carried[...] = r.queued_in[...] + times(r.back_in[...], two_late, NN)

    @pl.when(leads)
    def _():
        @pl.when(has_row_after)
        def _():
            receive(c_four, r.four_in.at[direct])
            for copy in take_copies:
                copy.start()
            for part in range(2):
                receive(c_four_aside[part], r.four_in.at[indirect, part])
            pass_copy.start()
            for i in range(2):
                receive(
                    c_four_pass[i],
                    r.four_in.at[strips * (1 - core) + (odd if i == 0 else 1 - odd)],
                )

            def split_top(step, carry):
                to = pl.ds(pl.multiple_of(step * STRIP, STRIP), STRIP)
                for part in range(2):
                    r.top_high[part, to, :], r.top_low[part, to, :] = halves(r.four_in[step, part])
                return carry

            lax.fori_loop(0, size // STRIP, split_top, 0)

        receive(c_upper, r.upper_in)

        @pl.when(has_row_after)
        def _():
            receive(c_lead, r.back_in)
            r.lower[...] = r.upper_in[...] + times(r.back_in[...], top, NN)

        @pl.when(jnp.logical_not(has_row_after))
        def _():
            r.lower[...] = r.upper_in[...]

        lower_copy.start()

        @pl.when(has_row_before)
        def _():
            r.back_out[...] = r.queued[...] + times(r.lower[...], four, NN)
            back_lead.start()
            back_help.start()
            back_late.start()

        r.carried[...] = r.queued_in[...] + times(r.lower[...], two_late, NN)

    @pl.when(ends)
    def _():
        pl.when(has_row_after)(lambda: receive(c_back_late, r.back_in))
        r.carried[...] = r.back_in[...]

    @pl.when(enters)
    def _():
        receive(c_lower, r.lower_in)
        r.carried[...] = r.lower_in[...]

    r.found[1] = r.trace[1] - r.carried[...]
    r.found[0] = r.trace[0] - times(r.found[1], second, NN)

    c_chip, c_far, c_across = channel(), channel(), channel()
    c_side = [[channel() for d in range(3)] for which in range(2)]
    place = r.gathered.at[sub, core]
    send(c_chip, r.found.at[1 - core], place, partner)
    send(c_far, r.found.at[core], place, opposite)
    send(c_across, r.found.at[1 - core], place, across)
    r.gathered[sub, core] = r.found[core]
    receive(c_chip, r.gathered.at[sub, 1 - core])
    for d in (2, 1, 3):
        send(c_side[0][d - 1], r.gathered.at[sub], r.gathered.at[sub], beside[d - 1])
    receive(c_far, r.gathered.at[other_sub, core])
    receive(c_across, r.gathered.at[other_sub, 1 - core])
    for d in (2, 1, 3):
        send(c_side[1][d - 1], r.gathered.at[other_sub], r.gathered.at[other_sub], beside[d - 1])
    for which in range(2):
        for d in (1, 2, 3):
            group = 2 * ((x + 4 - d) % 4) + (far if which == 0 else 1 - far)
            receive(c_side[which][d - 1], r.gathered.at[group])

    found = r.gathered[...].reshape(shots // 8, 2, 8, size)
    found = jnp.stack([found[:, 0], found[:, 1]], axis=0).reshape(2 * shots, size)
    r.found_high[...], r.found_low[...] = halves(found)
    turned = found.T
    r.separator_out[0] = turned[:, :shots]
    r.separator_out[1] = turned[:, shots:]

    def interior_of(b, carry):
        left = (r.found_high[...], r.found_low[...])
        out = [
            dot3(left, (r.coupling_high[b, part], r.coupling_low[b, part])) for part in range(2)
        ]
        turned = (r.eliminated[b] - combine(out[0], out[1], 0)).T
        r.interior_out[b, 0] = turned[:, :shots]
        r.interior_out[b, 1] = turned[:, shots:]
        return carry

    lax.fori_loop(0, blocks, interior_of, 0)

    for copy, when in unsent:
        if when is None:
            copy.wait_send()
        else:
            pl.when(when)(copy.wait_send)


CHANNELS = 48


def body(
    rhs_interior,
    rhs_separator,
    inverse_blocks,
    coupling,
    separator_rows,
    separator_inverse,
    transfer,
):
    _, nb, _, m, shots = rhs_interior.shape
    size = transfer.shape[-1]
    vmem = pltpu.VMEM
    inputs = {
        "rows": separator_rows[0],
        "given": rhs_separator[0],
        "rhs_hbm": rhs_interior[0],
        "inverse_hbm": inverse_blocks[0],
        "coupling_hbm": coupling[0],
        "schur_hbm": separator_inverse[0],
        "transfer_hbm": transfer[0],
    }
    outputs = {
        "interior_out": jax.ShapeDtypeStruct((nb, 2, m, shots), F32),
        "separator_out": jax.ShapeDtypeStruct((2, size, shots), F32),
    }
    scratch = {
        "inverse": vmem((nb, 2, m, m), F32),
        "inverse_high": vmem((nb, 2, m, m), BF16),
        "inverse_low": vmem((nb, 2, m, m), BF16),
        "rhs": vmem((nb, 2, m, shots), F32),
        "coupling": vmem((nb, 2, size, m), F32),
        "coupling_high": vmem((nb, 2, size, m), BF16),
        "coupling_low": vmem((nb, 2, size, m), BF16),
        "spread": vmem((nb, size, size), BF16),
        "placed_high": vmem((2, size, m), BF16),
        "placed_low": vmem((2, size, m), BF16),
        "eliminated": vmem((nb, m, 2 * shots), F32),
        "rhs_high": vmem((m, 2 * shots), BF16),
        "rhs_low": vmem((m, 2 * shots), BF16),
        "known_high": vmem((m, 2 * shots), BF16),
        "known_low": vmem((m, 2 * shots), BF16),
        "weighted_high": vmem((size, 2 * shots), BF16),
        "weighted_low": vmem((size, 2 * shots), BF16),
        "total": vmem((size, 2 * shots), F32),
        "load": vmem((8, 32, size), F32),
        "from_x": vmem((2, 3, 32, size), F32),
        "forward_sum": vmem((32, size), F32),
        "from_z": vmem((32, size), F32),
        "schur": vmem((2, size, size), F32),
        "schur_high": vmem((2, size, size), BF16),
        "schur_low": vmem((2, size, size), BF16),
        "pair": vmem((2, 2, size, size), F32),
        "pair_high": vmem((2, 2, size, size), BF16),
        "pair_low": vmem((2, 2, size, size), BF16),
        "twos": vmem((2, size // STRIP, 2, STRIP, size), F32),
        "two_high": vmem((2, 2, size, size), BF16),
        "two_low": vmem((2, 2, size, size), BF16),
        "four_high": vmem((2, size, size), BF16),
        "four_low": vmem((2, size, size), BF16),
        "four_out": vmem((2, STRIP, size), F32),
        "four_in": vmem((size // STRIP, 2, STRIP, size), F32),
        "top_high": vmem((2, size, size), BF16),
        "top_low": vmem((2, size, size), BF16),
        "upper_in": vmem((16, size), F32),
        "lower": vmem((16, size), F32),
        "lower_in": vmem((16, size), F32),
        "spare": vmem((2, 16, size), F32),
        "local": vmem((2, 16, size), F32),
        "start": vmem((16, size), F32),
        "start_in": vmem((16, size), F32),
        "node_start": vmem((16, size), F32),
        "enter": vmem((16, size), F32),
        "ahead_in": vmem((16, size), F32),
        "ahead_out": vmem((16, size), F32),
        "trace": vmem((2, 16, size), F32),
        "queued": vmem((16, size), F32),
        "queued_in": vmem((16, size), F32),
        "back_in": vmem((16, size), F32),
        "back_out": vmem((16, size), F32),
        "carried": vmem((16, size), F32),
        "found": vmem((2, 16, size), F32),
        "gathered": vmem((8, 2, 16, size), F32),
        "found_high": vmem((2 * shots, size), BF16),
        "found_low": vmem((2 * shots, size), BF16),
        "send_sem": pltpu.SemaphoreType.DMA((CHANNELS,)),
        "recv_sem": pltpu.SemaphoreType.DMA((CHANNELS,)),
        "here_sem": pltpu.SemaphoreType.DMA((2,)),
        "block_sem": pltpu.SemaphoreType.DMA((3, nb)),
    }
    names = list(inputs) + list(outputs) + list(scratch)

    def sweep_kernel(*refs):
        kernel(names, *refs)

    interior, separator = pl.pallas_call(
        sweep_kernel,
        out_shape=tuple(outputs.values()),
        in_specs=[pl.BlockSpec(memory_space=pltpu.VMEM)] * 2
        + [pl.BlockSpec(memory_space=pltpu.HBM)] * (len(inputs) - 2),
        out_specs=(pl.BlockSpec(memory_space=pltpu.VMEM),) * 2,
        scratch_shapes=list(scratch.values()),
        compiler_params=pltpu.CompilerParams(
            collective_id=0, has_side_effects=True, vmem_limit_bytes=51 << 20
        ),
    )(*inputs.values())
    return (interior[None], separator[None])


def solution(mesh):
    in_specs = (
        P("slab", "sub", None, None, None),
        P("slab", None, None, None),
        P("slab", "sub", None, None, None),
        P("slab", "sub", None, None, None),
        P("slab", "sub", None),
        P("slab", None, None, None),
        P("slab", None, None, None),
    )
    out_specs = (P("slab", "sub", None, None, None), P("slab", None, None, None))
    return jax.shard_map(body, mesh=mesh, in_specs=in_specs, out_specs=out_specs, check_vma=False)
```

```python
import types

import jax
import jax.numpy as jnp
from jax import lax
from jax.experimental import pallas as pl
from jax.experimental.pallas import tpu as pltpu
from jax.sharding import PartitionSpec as P

MESH = pl.DeviceIdType.MESH
F32 = jnp.float32
BF16 = jnp.bfloat16
NN = (((1,), (0,)), ((), ()))
NT = (((1,), (1,)), ((), ()))
STRIP = 128
WIDE = 256


def halves(value):
    high = value.astype(BF16)
    return high, (value - high.astype(F32)).astype(BF16)


def dot(left, right, dims=NN):
    return lax.dot_general(left, right, dims, preferred_element_type=F32)


def dot3(left, right):
    return dot(
        jnp.concatenate([left[0], left[0], left[1]], axis=1),
        jnp.concatenate([right[0], right[1], right[0]], axis=0),
    )


def times(value, matrix, dims):
    high, low = matrix
    n = value.shape[0] // 2
    value_high, value_low = halves(value)
    both = jnp.concatenate([value_high, value_low], axis=0)
    out = []
    for part in range(2):
        whole = dot(both, high[part], dims)
        out.append(whole[: 2 * n] + (whole[2 * n :] + dot(value_high, low[part], dims)))
    return jnp.concatenate([out[0][:n] - out[1][n:], out[0][n:] + out[1][:n]], axis=0)


def kernel(names, *refs):
    r = types.SimpleNamespace(**dict(zip(names, refs)))
    slab, sub = lax.axis_index("slab"), lax.axis_index("sub")
    slabs = lax.axis_size("slab")
    core, role, duo = slab % 2, (slab // 2) % 2, slab // 4
    duos = slabs // 4
    x, far = sub // 2, sub % 2
    after, before = (2 * duos - 3 - duo) // (duos - 1), (duo + duos - 2) // (duos - 1)
    has_after, has_before = duo < duos - 1, duo > 0
    early, late = role == 0, role == 1
    row, upper = duo // 2, duo % 2
    rows = duos // 2
    row_after, row_before = (2 * rows - 3 - row) // (rows - 1), (row + rows - 2) // (rows - 1)
    has_row_after, has_row_before = row < rows - 1, row > 0
    leads = jnp.logical_and(early, upper == 0)
    helps = jnp.logical_and(early, upper == 1)
    enters = jnp.logical_and(late, upper == 0)
    ends = jnp.logical_and(late, upper == 1)
    node = jnp.logical_or(enters, helps)
    blocks, _, size, m = r.coupling_hbm.shape
    shots = r.rhs_hbm.shape[-1]

    other_core, other_sub = slab + 1 - 2 * core, 2 * x + 1 - far
    partner = (other_core, sub)
    opposite = (slab, other_sub)
    across = (other_core, other_sub)
    mate = (slab + 2 - 4 * role, sub)
    beside = [(slab, ((x + d) % 4) * 2 + far) for d in (1, 2, 3)]
    def chip_at(offset):
        return ((slab + slabs + offset) % slabs, sub)

    critical, other = chip_at(2 + 4 * upper), chip_at(4)
    last_early, last_late = chip_at(-4), chip_at(-2)
    next_lead, last_lead = ((slab + 8) % slabs, sub), ((slab + slabs - 8) % slabs, sub)

    count = [0]
    unsent = []

    def remote(index, source, target, device):
        return pltpu.make_async_remote_copy(
            src_ref=source,
            dst_ref=target,
            send_sem=r.send_sem.at[index],
            recv_sem=r.recv_sem.at[index],
            device_id=device,
            device_id_type=MESH,
        )

    def channel():
        count[0] += 1
        return count[0] - 1

    def send(index, source, target, device, when=None):
        copy = remote(index, source, target, device)
        if when is None:
            copy.start()
        unsent.append((copy, when))
        return copy

    def receive(index, target):
        remote(index, target, target, partner).wait_recv()

    def local_copies(b):
        return [
            pltpu.make_async_copy(r.inverse_hbm.at[b], r.inverse.at[b], r.block_sem.at[0, b]),
            pltpu.make_async_copy(r.rhs_hbm.at[b], r.rhs.at[b], r.block_sem.at[1, b]),
            pltpu.make_async_copy(r.coupling_hbm.at[b], r.coupling.at[b], r.block_sem.at[2, b]),
        ]

    own_transfer = pltpu.make_async_copy(r.transfer_hbm, r.pair.at[core], r.here_sem.at[0])
    own_schur = pltpu.make_async_copy(r.schur_hbm, r.schur, r.here_sem.at[1])
    own_transfer.start()
    for b in range(blocks):
        for copy in local_copies(b):
            copy.start()
    own_schur.start()

    r.total[...] = jnp.zeros_like(r.total)

    def spread_of(b, carry):
        for i in range(size // STRIP):
            at = slice(i * STRIP, (i + 1) * STRIP)
            place = lax.broadcasted_iota(jnp.int32, (STRIP, size), 0) + i * STRIP
            r.spread[b, at] = (place == r.rows[pl.ds(b, 1), :]).astype(BF16)
        return carry

    barrier = pltpu.get_barrier_semaphore()

    def greet(device):
        pl.semaphore_signal(barrier, inc=1, device_id=device, device_id_type=MESH)

    for device in [partner, opposite, across, mate] + beside:
        greet(device)

    for who, always, before_too, after_too in (
        (leads, (4,), (-4, -2, -8), (8,)),
        (enters, (2, 4), (-6,), ()),
        (helps, (-2, -4), (), (4, 6)),
        (ends, (-4,), (), (2,)),
    ):
        for when, offsets in (
            (who, always),
            (jnp.logical_and(who, has_row_before), before_too),
            (jnp.logical_and(who, has_row_after), after_too),
        ):
            if offsets:

                @pl.when(when)
                def _(offsets=offsets):
                    for offset in offsets:
                        greet(chip_at(offset))

    lax.fori_loop(0, blocks, spread_of, 0)
    pl.semaphore_wait(
        barrier,
        7
        + (1 - role) * (1 - upper) * (1 + 3 * row_before + row_after)
        + role * (1 - upper) * (2 + row_before)
        + (1 - role) * upper * (2 + 2 * row_after)
        + role * upper * (1 + row_after),
    )

    c_transfer = channel()
    send(c_transfer, r.transfer_hbm, r.pair.at[core], partner)

    def combine(real, imag, axis):
        n = real.shape[axis] // 2
        if axis == 1:
            return jnp.concatenate(
                [real[:, :n] - imag[:, n:], real[:, n:] + imag[:, :n]], axis=1
            )
        return jnp.concatenate([real[:n] - imag[n:], real[n:] + imag[:n]], axis=0)

    def load_of(b, carry):
        for copy in local_copies(b):
            copy.wait()
        r.rhs_high[...], r.rhs_low[...] = halves(
            jnp.concatenate([r.rhs[b, 0], r.rhs[b, 1]], axis=1)
        )

        def strip(at, source, high, low, right):
            out = []
            for part in range(2):
                left = halves(source[b, part, at])
                high[b, part, at], low[b, part, at] = left
                out.append(dot3(left, right))
            return combine(out[0], out[1], 1)

        for i in range(m // WIDE):
            at = slice(i * WIDE, (i + 1) * WIDE)
            right = (r.rhs_high[...], r.rhs_low[...])
            value = strip(at, r.inverse, r.inverse_high, r.inverse_low, right)
            r.eliminated[b, at] = value
            r.known_high[at], r.known_low[at] = halves(value)
        for i in range(size // WIDE):
            at = slice(i * WIDE, (i + 1) * WIDE)
            right = (r.known_high[...], r.known_low[...])
            value = strip(at, r.coupling, r.coupling_high, r.coupling_low, right)
            r.weighted_high[at], r.weighted_low[at] = halves(value)
        for i in range(size // WIDE):
            at = slice(i * WIDE, (i + 1) * WIDE)
            spread = r.spread[b, at]
            r.total[at] += dot(
                jnp.concatenate([spread, spread], axis=1),
                jnp.concatenate([r.weighted_high[...], r.weighted_low[...]], axis=0),
            )
        return carry

    lax.fori_loop(0, blocks // 2, load_of, 0)

    def split_pair(slot):
        def step_of(step, carry):
            at = pl.ds(pl.multiple_of(step * STRIP, STRIP), STRIP)
            for part in range(2):
                r.pair_high[slot, part, at, :], r.pair_low[slot, part, at, :] = halves(
                    r.pair[slot, part, at, :]
                )
            return carry

        lax.fori_loop(0, size // STRIP, step_of, 0)

    own_transfer.wait()
    split_pair(core)
    receive(c_transfer, r.pair.at[1 - core])
    split_pair(1 - core)
    first = (r.pair_high.at[0], r.pair_low.at[0])
    second = (r.pair_high.at[1], r.pair_low.at[1])

    def merged_rows(left, at, right):
        rows_high = jnp.concatenate([left[0][0, at, :], left[0][1, at, :]], axis=0)
        rows_low = jnp.concatenate([left[1][0, at, :], left[1][1, at, :]], axis=0)
        out = [dot3((rows_high, rows_low), (right[0][part], right[1][part])) for part in range(2)]
        return out[0][:STRIP] - out[1][STRIP:], out[0][STRIP:] + out[1][:STRIP]

    half = size // 2
    strips = half // STRIP

    c_half = channel()
    c_mate = channel()
    c_aside, c_pass = [[channel() for i in range(2)] for j in range(2)]
    odd = x % 2
    direct, indirect = strips * core + odd, strips * core + 1 - odd

    def merge_two(strip):
        merged = merged_rows(second, pl.ds(pl.multiple_of(strip * STRIP, STRIP), STRIP), first)
        for part in range(2):
            r.twos[role, strip, part] = merged[part]

    merge_two(direct)
    piece = r.twos.at[role, direct]
    send(c_mate, piece, piece, mate)
    merge_two(indirect)
    halved = r.twos.at[role, pl.ds(strips * core, strips)]
    send(c_half, halved, halved, partner)

    lax.fori_loop(blocks // 2, blocks, load_of, 0)
    given = jnp.concatenate([r.given[0], r.given[1]], axis=1)
    rest = (jnp.where(sub == 0, given, jnp.zeros_like(given)) - r.total[...]).T
    rest = rest.reshape(2, shots // 8, 8, size)
    r.load[...] = jnp.stack([rest[0], rest[1]], axis=1).reshape(r.load.shape)

    c_x = [[channel() for d in range(3)] for which in range(2)]
    c_z = channel()
    for which in range(2):
        for d in (2, 1, 3):
            group = 2 * ((x + d) % 4) + (1 - far if which == 0 else far)
            send(
                c_x[which][d - 1], r.load.at[group], r.from_x.at[which, d - 1], beside[d - 1]
            )

    own_schur.wait()

    def split_schur(step, carry):
        at = pl.ds(pl.multiple_of(step * STRIP, STRIP), STRIP)
        for part in range(2):
            r.schur_high[part, :, at], r.schur_low[part, :, at] = halves(r.schur[part, at, :].T)
        return carry

    lax.fori_loop(0, size // STRIP, split_schur, 0)

    def side_sum(which, group):
        for d in range(3):
            receive(c_x[which][d], r.from_x.at[which, d])
        return (r.load[group] + r.from_x[which, 0]) + (r.from_x[which, 1] + r.from_x[which, 2])

    r.forward_sum[...] = side_sum(0, other_sub)
    send(c_z, r.forward_sum, r.from_z, opposite)

    piece = r.twos.at[1 - role, direct]
    receive(c_mate, piece)
    for part in range(2):
        aside = r.twos.at[1 - role, direct, part]
        send(c_aside[part], aside, aside, beside[2 * part])
    send(c_pass[0], piece, piece, partner)
    own_sum = side_sum(1, sub)

    receive(c_half, r.twos.at[role, pl.ds(strips * (1 - core), strips)])

    def split_two(which):
        def step_of(step, carry):
            to = pl.ds(pl.multiple_of(step * STRIP, STRIP), STRIP)
            for part in range(2):
                r.two_high[which, part, to, :], r.two_low[which, part, to, :] = halves(
                    r.twos[which, step, part]
                )
            return carry

        lax.fori_loop(0, size // STRIP, step_of, 0)

    split_two(role)
    two_early = (r.two_high.at[0], r.two_low.at[0])
    two_late = (r.two_high.at[1], r.two_low.at[1])
    four = (r.four_high, r.four_low)

    receive(c_z, r.from_z)
    summed = (own_sum + r.from_z[...]).reshape(2, 2, 8, size)
    summed = jnp.stack([summed[:, 0], summed[:, 1]], axis=0).reshape(32, size)
    solved = times(summed, (r.schur_high, r.schur_low), NN).reshape(2, 2, 8, size)
    solved = jnp.stack([solved[:, 0], solved[:, 1]], axis=0).reshape(2, 16, size)
    r.spare[...] = solved
    r.local[core] = r.spare[core]
    c_swap = channel()
    send(c_swap, r.spare.at[1 - core], r.local.at[core], partner)

    @pl.when(jnp.logical_not(has_before))
    def _():
        r.ahead_in[...] = jnp.zeros_like(r.ahead_in)

    @pl.when(jnp.logical_not(has_after))
    def _():
        r.back_in[...] = jnp.zeros_like(r.back_in)

    receive(c_swap, r.local.at[1 - core])
    start = r.local[1] - times(r.local[0], second, NT)
    c_start = channel()
    gives_start = jnp.logical_or(early, upper == 1)
    start_copy = send(c_start, r.start, r.start_in, mate, gives_start)
    r.start[...] = start
    pl.when(gives_start)(start_copy.start)

    c_node, c_other = channel(), channel()
    goes_on = jnp.logical_and(node, has_after)
    node_copy = send(c_node, r.ahead_out, r.ahead_in, critical, goes_on)
    other_copy = send(c_other, r.ahead_out, r.ahead_in, other, goes_on)

    @pl.when(enters)
    def _():
        receive(c_start, r.start_in)
        r.node_start[...] = r.start[...] + times(r.start_in[...], two_late, NT)

        @pl.when(jnp.logical_not(has_before))
        def _():
            r.ahead_out[...] = r.node_start[...]
            node_copy.start()
            other_copy.start()

    for part in range(2):
        receive(c_aside[part], r.twos.at[1 - role, indirect, part])
    piece = r.twos.at[1 - role, indirect]
    send(c_pass[1], piece, piece, partner)
    for i in range(2):
        receive(c_pass[i], r.twos.at[1 - role, strips * (1 - core) + (odd if i == 0 else 1 - odd)])
    split_two(1 - role)

    pl.when(ends)(lambda: receive(c_start, r.start_in))

    @pl.when(helps)
    def _():
        receive(c_start, r.start_in)
        r.node_start[...] = r.start_in[...] + times(r.start[...], two_late, NT)

    gives = jnp.logical_and(helps, has_row_after)
    takes = jnp.logical_and(leads, has_row_after)
    c_four = channel()
    c_four_aside, c_four_pass = [[channel() for i in range(2)] for j in range(2)]
    four_copy = send(c_four, r.four_out, r.four_in.at[direct], last_early, gives)
    soon = jnp.logical_and(helps, row == rows - 2)
    not_soon = jnp.logical_and(helps, row < rows - 2)

    def give():
        at = pl.ds(pl.multiple_of(direct * STRIP, STRIP), STRIP)
        merged = merged_rows(two_late, at, two_early)
        for part in range(2):
            r.four_out[part] = merged[part]
        four_copy.start()

    pl.when(soon)(give)

    @pl.when(jnp.logical_and(duo > 1, jnp.logical_or(gives, upper == 0)))
    def _():
        def merge_four(step, carry):
            at = pl.ds(pl.multiple_of(step * STRIP, STRIP), STRIP)
            merged = merged_rows(two_late, at, two_early)

            @pl.when(leads)
            def _():
                for part in range(2):
                    r.four_high[part, at, :], r.four_low[part, at, :] = halves(merged[part])

            @pl.when(node)
            def _():
                for part in range(2):
                    r.four_high[part, :, at], r.four_low[part, :, at] = halves(merged[part].T)

            return carry

        lax.fori_loop(0, size // STRIP, merge_four, 0)

    def weights_of(b, carry):
        spread = r.spread[b]
        for part in range(2):
            r.placed_high[part] = dot(spread, r.coupling_high[b, part]).astype(BF16)
            r.placed_low[part] = dot(spread, r.coupling_low[b, part]).astype(BF16)

        def inverse(part):
            return r.inverse_high[b, part], r.inverse_low[b, part]

        def strip_of(step, carry):
            at = pl.ds(pl.multiple_of(step * STRIP, STRIP), STRIP)
            left = [
                jnp.concatenate([source[0, at, :], source[1, at, :]], axis=0)
                for source in (r.placed_high, r.placed_low)
            ]
            merged = combine(dot3(left, inverse(0)), dot3(left, inverse(1)), 0)
            for part in range(2):
                r.coupling_high[b, part, at, :], r.coupling_low[b, part, at, :] = halves(
                    merged[part * STRIP : (part + 1) * STRIP]
                )
            return carry

        lax.fori_loop(0, size // STRIP, strip_of, 0)
        left = halves(r.eliminated[b].T)
        r.eliminated[b] = combine(dot3(left, inverse(0)), dot3(left, inverse(1)), 0)
        return carry

    towards_end = duo >= duos - 2

    @pl.when(towards_end)
    def _():
        lax.fori_loop(0, blocks, weights_of, 0)

    @pl.when(jnp.logical_and(node, has_before))
    def _():
        receive(c_node, r.ahead_in)

        @pl.when(jnp.logical_and(duo > 1, has_after))
        def _():
            r.ahead_out[...] = r.node_start[...] + times(r.ahead_in[...], four, NN)

        @pl.when(duo == 1)
        def _():
            r.ahead_out[...] = r.node_start[...] + times(
                times(r.ahead_in[...], two_early, NT), two_late, NT
            )

        @pl.when(has_after)
        def _():
            node_copy.start()
            other_copy.start()

    pl.when(not_soon)(give)

    @pl.when(ends)
    def _():
        receive(c_other, r.ahead_in)

    @pl.when(jnp.logical_and(leads, has_before))
    def _():
        receive(c_other, r.ahead_in)

    r.enter[...] = r.ahead_in[...]

    @pl.when(late)
    def _():
        r.enter[...] = r.start_in[...] + times(r.ahead_in[...], two_early, NT)

    r.trace[0] = r.local[0] - times(r.enter[...], first, NT)
    r.trace[1] = r.local[1] - times(r.trace[0], second, NT)
    queued = times(r.trace[0] - times(r.trace[1], second, NN), first, NN)
    r.queued[...] = queued
    c_queued = channel()
    queued_copy = send(c_queued, r.queued, r.queued_in, mate, late)
    pl.when(late)(queued_copy.start)

    @pl.when(jnp.logical_not(towards_end))
    def _():
        lax.fori_loop(0, blocks, weights_of, 0)

    c_upper, c_lower, c_lead, c_help, c_back_late = [channel() for i in range(5)]
    goes_back = jnp.logical_and(leads, has_row_before)
    upper_copy = send(c_upper, r.queued, r.upper_in, last_early, helps)
    lower_copy = send(c_lower, r.lower, r.lower_in, mate, leads)
    back_lead = send(c_lead, r.back_out, r.back_in, last_lead, goes_back)
    back_help = send(c_help, r.back_out, r.back_in, last_early, goes_back)
    back_late = send(c_back_late, r.back_out, r.back_in, last_late, goes_back)
    piece = r.four_in.at[direct]
    take_copies = [
        send(c_four_aside[part], piece.at[part], piece.at[part], beside[2 * part], takes)
        for part in range(2)
    ] + [send(c_four_pass[0], piece, piece, partner, takes)]
    piece = r.four_in.at[indirect]
    pass_copy = send(c_four_pass[1], piece, piece, partner, takes)
    top = (r.top_high, r.top_low)

    @pl.when(early)
    def _():
        receive(c_queued, r.queued_in)
        r.queued[...] += times(r.queued_in[...], two_early, NN)

    @pl.when(helps)
    def _():
        upper_copy.start()
        pl.when(has_row_after)(lambda: receive(c_help, r.back_in))
        r.carried[...] = r.queued_in[...] + times(r.back_in[...], two_late, NN)

    @pl.when(leads)
    def _():
        @pl.when(has_row_after)
        def _():
            receive(c_four, r.four_in.at[direct])
            for copy in take_copies:
                copy.start()
            for part in range(2):
                receive(c_four_aside[part], r.four_in.at[indirect, part])
            pass_copy.start()
            for i in range(2):
                receive(
                    c_four_pass[i],
                    r.four_in.at[strips * (1 - core) + (odd if i == 0 else 1 - odd)],
                )

            def split_top(step, carry):
                to = pl.ds(pl.multiple_of(step * STRIP, STRIP), STRIP)
                for part in range(2):
                    r.top_high[part, to, :], r.top_low[part, to, :] = halves(r.four_in[step, part])
                return carry

            lax.fori_loop(0, size // STRIP, split_top, 0)

        receive(c_upper, r.upper_in)

        @pl.when(has_row_after)
        def _():
            receive(c_lead, r.back_in)
            r.lower[...] = r.upper_in[...] + times(r.back_in[...], top, NN)

        @pl.when(jnp.logical_not(has_row_after))
        def _():
            r.lower[...] = r.upper_in[...]

        lower_copy.start()

        @pl.when(has_row_before)
        def _():
            r.back_out[...] = r.queued[...] + times(r.lower[...], four, NN)
            back_lead.start()
            back_help.start()
            back_late.start()

        r.carried[...] = r.queued_in[...] + times(r.lower[...], two_late, NN)

    @pl.when(ends)
    def _():
        pl.when(has_row_after)(lambda: receive(c_back_late, r.back_in))
        r.carried[...] = r.back_in[...]

    @pl.when(enters)
    def _():
        receive(c_lower, r.lower_in)
        r.carried[...] = r.lower_in[...]

    r.found[1] = r.trace[1] - r.carried[...]
    r.found[0] = r.trace[0] - times(r.found[1], second, NN)

    c_chip, c_far, c_across = channel(), channel(), channel()
    c_side = [[channel() for d in range(3)] for which in range(2)]
    place = r.gathered.at[sub, core]
    send(c_far, r.found.at[core], place, opposite)
    send(c_across, r.found.at[1 - core], place, across)
    send(c_chip, r.found.at[1 - core], place, partner)
    r.gathered[sub, core] = r.found[core]
    receive(c_chip, r.gathered.at[sub, 1 - core])
    for d in (2, 1, 3):
        send(c_side[0][d - 1], r.gathered.at[sub], r.gathered.at[sub], beside[d - 1])
    receive(c_far, r.gathered.at[other_sub, core])
    receive(c_across, r.gathered.at[other_sub, 1 - core])
    for d in (2, 1, 3):
        send(c_side[1][d - 1], r.gathered.at[other_sub], r.gathered.at[other_sub], beside[d - 1])
    for which in range(2):
        for d in (1, 2, 3):
            group = 2 * ((x + 4 - d) % 4) + (far if which == 0 else 1 - far)
            receive(c_side[which][d - 1], r.gathered.at[group])

    found = r.gathered[...].reshape(shots // 8, 2, 8, size)
    found = jnp.stack([found[:, 0], found[:, 1]], axis=0).reshape(2 * shots, size)
    r.found_high[...], r.found_low[...] = halves(found)
    turned = found.T
    r.separator_out[0] = turned[:, :shots]
    r.separator_out[1] = turned[:, shots:]

    def interior_of(b, carry):
        left = (r.found_high[...], r.found_low[...])
        out = [
            dot3(left, (r.coupling_high[b, part], r.coupling_low[b, part])) for part in range(2)
        ]
        turned = (r.eliminated[b] - combine(out[0], out[1], 0)).T
        r.interior_out[b, 0] = turned[:, :shots]
        r.interior_out[b, 1] = turned[:, shots:]
        return carry

    lax.fori_loop(0, blocks, interior_of, 0)

    for copy, when in unsent:
        if when is None:
            copy.wait_send()
        else:
            pl.when(when)(copy.wait_send)


CHANNELS = 48


def body(
    rhs_interior,
    rhs_separator,
    inverse_blocks,
    coupling,
    separator_rows,
    separator_inverse,
    transfer,
):
    _, nb, _, m, shots = rhs_interior.shape
    size = transfer.shape[-1]
    vmem = pltpu.VMEM
    inputs = {
        "rows": separator_rows[0],
        "given": rhs_separator[0],
        "rhs_hbm": rhs_interior[0],
        "inverse_hbm": inverse_blocks[0],
        "coupling_hbm": coupling[0],
        "schur_hbm": separator_inverse[0],
        "transfer_hbm": transfer[0],
    }
    outputs = {
        "interior_out": jax.ShapeDtypeStruct((nb, 2, m, shots), F32),
        "separator_out": jax.ShapeDtypeStruct((2, size, shots), F32),
    }
    scratch = {
        "inverse": vmem((nb, 2, m, m), F32),
        "inverse_high": vmem((nb, 2, m, m), BF16),
        "inverse_low": vmem((nb, 2, m, m), BF16),
        "rhs": vmem((nb, 2, m, shots), F32),
        "coupling": vmem((nb, 2, size, m), F32),
        "coupling_high": vmem((nb, 2, size, m), BF16),
        "coupling_low": vmem((nb, 2, size, m), BF16),
        "spread": vmem((nb, size, size), BF16),
        "placed_high": vmem((2, size, m), BF16),
        "placed_low": vmem((2, size, m), BF16),
        "eliminated": vmem((nb, m, 2 * shots), F32),
        "rhs_high": vmem((m, 2 * shots), BF16),
        "rhs_low": vmem((m, 2 * shots), BF16),
        "known_high": vmem((m, 2 * shots), BF16),
        "known_low": vmem((m, 2 * shots), BF16),
        "weighted_high": vmem((size, 2 * shots), BF16),
        "weighted_low": vmem((size, 2 * shots), BF16),
        "total": vmem((size, 2 * shots), F32),
        "load": vmem((8, 32, size), F32),
        "from_x": vmem((2, 3, 32, size), F32),
        "forward_sum": vmem((32, size), F32),
        "from_z": vmem((32, size), F32),
        "schur": vmem((2, size, size), F32),
        "schur_high": vmem((2, size, size), BF16),
        "schur_low": vmem((2, size, size), BF16),
        "pair": vmem((2, 2, size, size), F32),
        "pair_high": vmem((2, 2, size, size), BF16),
        "pair_low": vmem((2, 2, size, size), BF16),
        "twos": vmem((2, size // STRIP, 2, STRIP, size), F32),
        "two_high": vmem((2, 2, size, size), BF16),
        "two_low": vmem((2, 2, size, size), BF16),
        "four_high": vmem((2, size, size), BF16),
        "four_low": vmem((2, size, size), BF16),
        "four_out": vmem((2, STRIP, size), F32),
        "four_in": vmem((size // STRIP, 2, STRIP, size), F32),
        "top_high": vmem((2, size, size), BF16),
        "top_low": vmem((2, size, size), BF16),
        "upper_in": vmem((16, size), F32),
        "lower": vmem((16, size), F32),
        "lower_in": vmem((16, size), F32),
        "spare": vmem((2, 16, size), F32),
        "local": vmem((2, 16, size), F32),
        "start": vmem((16, size), F32),
        "start_in": vmem((16, size), F32),
        "node_start": vmem((16, size), F32),
        "enter": vmem((16, size), F32),
        "ahead_in": vmem((16, size), F32),
        "ahead_out": vmem((16, size), F32),
        "trace": vmem((2, 16, size), F32),
        "queued": vmem((16, size), F32),
        "queued_in": vmem((16, size), F32),
        "back_in": vmem((16, size), F32),
        "back_out": vmem((16, size), F32),
        "carried": vmem((16, size), F32),
        "found": vmem((2, 16, size), F32),
        "gathered": vmem((8, 2, 16, size), F32),
        "found_high": vmem((2 * shots, size), BF16),
        "found_low": vmem((2 * shots, size), BF16),
        "send_sem": pltpu.SemaphoreType.DMA((CHANNELS,)),
        "recv_sem": pltpu.SemaphoreType.DMA((CHANNELS,)),
        "here_sem": pltpu.SemaphoreType.DMA((2,)),
        "block_sem": pltpu.SemaphoreType.DMA((3, nb)),
    }
    names = list(inputs) + list(outputs) + list(scratch)

    def sweep_kernel(*refs):
        kernel(names, *refs)

    interior, separator = pl.pallas_call(
        sweep_kernel,
        out_shape=tuple(outputs.values()),
        in_specs=[pl.BlockSpec(memory_space=pltpu.VMEM)] * 2
        + [pl.BlockSpec(memory_space=pltpu.HBM)] * (len(inputs) - 2),
        out_specs=(pl.BlockSpec(memory_space=pltpu.VMEM),) * 2,
        scratch_shapes=list(scratch.values()),
        compiler_params=pltpu.CompilerParams(
            collective_id=0, has_side_effects=True, vmem_limit_bytes=51 << 20
        ),
    )(*inputs.values())
    return (interior[None], separator[None])


def solution(mesh):
    in_specs = (
        P("slab", "sub", None, None, None),
        P("slab", None, None, None),
        P("slab", "sub", None, None, None),
        P("slab", "sub", None, None, None),
        P("slab", "sub", None),
        P("slab", None, None, None),
        P("slab", None, None, None),
    )
    out_specs = (P("slab", "sub", None, None, None), P("slab", None, None, None))
    return jax.shard_map(body, mesh=mesh, in_specs=in_specs, out_specs=out_specs, check_vma=False)
```

```python
import types

import jax
import jax.numpy as jnp
from jax import lax
from jax.experimental import pallas as pl
from jax.experimental.pallas import tpu as pltpu
from jax.sharding import PartitionSpec as P

MESH = pl.DeviceIdType.MESH
F32 = jnp.float32
BF16 = jnp.bfloat16
NN = (((1,), (0,)), ((), ()))
NT = (((1,), (1,)), ((), ()))
STRIP = 128
WIDE = 256


def halves(value):
    high = value.astype(BF16)
    return high, (value - high.astype(F32)).astype(BF16)


def dot(left, right, dims=NN):
    return lax.dot_general(left, right, dims, preferred_element_type=F32)


def dot3(left, right):
    return dot(
        jnp.concatenate([left[0], left[0], left[1]], axis=1),
        jnp.concatenate([right[0], right[1], right[0]], axis=0),
    )


def times(value, matrix, dims):
    high, low = matrix
    n = value.shape[0] // 2
    value_high, value_low = halves(value)
    both = jnp.concatenate([value_high, value_low], axis=0)
    out = []
    for part in range(2):
        whole = dot(both, high[part], dims)
        out.append(whole[: 2 * n] + (whole[2 * n :] + dot(value_high, low[part], dims)))
    return jnp.concatenate([out[0][:n] - out[1][n:], out[0][n:] + out[1][:n]], axis=0)


def kernel(names, *refs):
    r = types.SimpleNamespace(**dict(zip(names, refs)))
    slab, sub = lax.axis_index("slab"), lax.axis_index("sub")
    slabs = lax.axis_size("slab")
    core, role, duo = slab % 2, (slab // 2) % 2, slab // 4
    duos = slabs // 4
    x, far = sub // 2, sub % 2
    after, before = (2 * duos - 3 - duo) // (duos - 1), (duo + duos - 2) // (duos - 1)
    has_after, has_before = duo < duos - 1, duo > 0
    early, late = role == 0, role == 1
    row, upper = duo // 2, duo % 2
    rows = duos // 2
    row_after, row_before = (2 * rows - 3 - row) // (rows - 1), (row + rows - 2) // (rows - 1)
    has_row_after, has_row_before = row < rows - 1, row > 0
    leads = jnp.logical_and(early, upper == 0)
    helps = jnp.logical_and(early, upper == 1)
    enters = jnp.logical_and(late, upper == 0)
    ends = jnp.logical_and(late, upper == 1)
    node = jnp.logical_or(enters, helps)
    blocks, _, size, m = r.coupling_hbm.shape
    shots = r.rhs_hbm.shape[-1]

    other_core, other_sub = slab + 1 - 2 * core, 2 * x + 1 - far
    partner = (other_core, sub)
    opposite = (slab, other_sub)
    across = (other_core, other_sub)
    mate = (slab + 2 - 4 * role, sub)
    beside = [(slab, ((x + d) % 4) * 2 + far) for d in (1, 2, 3)]
    def chip_at(offset):
        return ((slab + slabs + offset) % slabs, sub)

    critical, other = chip_at(2 + 4 * upper), chip_at(4)
    last_early, last_late = chip_at(-4), chip_at(-2)
    next_lead, last_lead = ((slab + 8) % slabs, sub), ((slab + slabs - 8) % slabs, sub)

    count = [0]
    unsent = []

    def remote(index, source, target, device):
        return pltpu.make_async_remote_copy(
            src_ref=source,
            dst_ref=target,
            send_sem=r.send_sem.at[index],
            recv_sem=r.recv_sem.at[index],
            device_id=device,
            device_id_type=MESH,
        )

    def channel():
        count[0] += 1
        return count[0] - 1

    def send(index, source, target, device, when=None):
        copy = remote(index, source, target, device)
        if when is None:
            copy.start()
        unsent.append((copy, when))
        return copy

    def receive(index, target):
        remote(index, target, target, partner).wait_recv()

    def local_copies(b):
        return [
            pltpu.make_async_copy(r.inverse_hbm.at[b], r.inverse.at[b], r.block_sem.at[0, b]),
            pltpu.make_async_copy(r.rhs_hbm.at[b], r.rhs.at[b], r.block_sem.at[1, b]),
            pltpu.make_async_copy(r.coupling_hbm.at[b], r.coupling.at[b], r.block_sem.at[2, b]),
        ]

    own_transfer = pltpu.make_async_copy(r.transfer_hbm, r.pair.at[core], r.here_sem.at[0])
    own_schur = pltpu.make_async_copy(r.schur_hbm, r.schur, r.here_sem.at[1])
    own_transfer.start()
    for b in range(blocks):
        for copy in local_copies(b):
            copy.start()
    own_schur.start()

    r.total[...] = jnp.zeros_like(r.total)

    def spread_of(b, carry):
        for i in range(size // STRIP):
            at = slice(i * STRIP, (i + 1) * STRIP)
            place = lax.broadcasted_iota(jnp.int32, (STRIP, size), 0) + i * STRIP
            r.spread[b, at] = (place == r.rows[pl.ds(b, 1), :]).astype(BF16)
        return carry

    barrier = pltpu.get_barrier_semaphore()

    def greet(device):
        pl.semaphore_signal(barrier, inc=1, device_id=device, device_id_type=MESH)

    for device in [partner, opposite, across, mate] + beside:
        greet(device)

    for who, always, before_too, after_too in (
        (leads, (4,), (-4, -2, -8), (8,)),
        (enters, (2, 4), (-6,), ()),
        (helps, (-2, -4), (), (4, 6)),
        (ends, (-4,), (), (2,)),
    ):
        for when, offsets in (
            (who, always),
            (jnp.logical_and(who, has_row_before), before_too),
            (jnp.logical_and(who, has_row_after), after_too),
        ):
            if offsets:

                @pl.when(when)
                def _(offsets=offsets):
                    for offset in offsets:
                        greet(chip_at(offset))

    lax.fori_loop(0, blocks, spread_of, 0)
    pl.semaphore_wait(
        barrier,
        7
        + (1 - role) * (1 - upper) * (1 + 3 * row_before + row_after)
        + role * (1 - upper) * (2 + row_before)
        + (1 - role) * upper * (2 + 2 * row_after)
        + role * upper * (1 + row_after),
    )

    c_transfer = channel()
    send(c_transfer, r.transfer_hbm, r.pair.at[core], partner)

    def combine(real, imag, axis):
        n = real.shape[axis] // 2
        if axis == 1:
            return jnp.concatenate(
                [real[:, :n] - imag[:, n:], real[:, n:] + imag[:, :n]], axis=1
            )
        return jnp.concatenate([real[:n] - imag[n:], real[n:] + imag[:n]], axis=0)

    def load_of(b, carry):
        for copy in local_copies(b):
            copy.wait()
        r.rhs_high[...], r.rhs_low[...] = halves(
            jnp.concatenate([r.rhs[b, 0], r.rhs[b, 1]], axis=1)
        )

        def strip(at, source, high, low, right):
            out = []
            for part in range(2):
                left = halves(source[b, part, at])
                high[b, part, at], low[b, part, at] = left
                out.append(dot3(left, right))
            return combine(out[0], out[1], 1)

        for i in range(m // WIDE):
            at = slice(i * WIDE, (i + 1) * WIDE)
            right = (r.rhs_high[...], r.rhs_low[...])
            value = strip(at, r.inverse, r.inverse_high, r.inverse_low, right)
            r.eliminated[b, at] = value
            r.known_high[at], r.known_low[at] = halves(value)
        for i in range(size // WIDE):
            at = slice(i * WIDE, (i + 1) * WIDE)
            right = (r.known_high[...], r.known_low[...])
            value = strip(at, r.coupling, r.coupling_high, r.coupling_low, right)
            r.weighted_high[at], r.weighted_low[at] = halves(value)
        for i in range(size // WIDE):
            at = slice(i * WIDE, (i + 1) * WIDE)
            spread = r.spread[b, at]
            r.total[at] += dot(
                jnp.concatenate([spread, spread], axis=1),
                jnp.concatenate([r.weighted_high[...], r.weighted_low[...]], axis=0),
            )
        return carry

    lax.fori_loop(0, blocks // 2, load_of, 0, unroll=True)

    def split_pair(slot):
        def step_of(step, carry):
            at = pl.ds(pl.multiple_of(step * STRIP, STRIP), STRIP)
            for part in range(2):
                r.pair_high[slot, part, at, :], r.pair_low[slot, part, at, :] = halves(
                    r.pair[slot, part, at, :]
                )
            return carry

        lax.fori_loop(0, size // STRIP, step_of, 0)

    own_transfer.wait()
    split_pair(core)
    receive(c_transfer, r.pair.at[1 - core])
    split_pair(1 - core)
    first = (r.pair_high.at[0], r.pair_low.at[0])
    second = (r.pair_high.at[1], r.pair_low.at[1])

    def merged_rows(left, at, right):
        rows_high = jnp.concatenate([left[0][0, at, :], left[0][1, at, :]], axis=0)
        rows_low = jnp.concatenate([left[1][0, at, :], left[1][1, at, :]], axis=0)
        out = [dot3((rows_high, rows_low), (right[0][part], right[1][part])) for part in range(2)]
        return out[0][:STRIP] - out[1][STRIP:], out[0][STRIP:] + out[1][:STRIP]

    half = size // 2
    strips = half // STRIP

    c_half = channel()
    c_mate = channel()
    c_aside, c_pass = [[channel() for i in range(2)] for j in range(2)]
    odd = x % 2
    direct, indirect = strips * core + odd, strips * core + 1 - odd

    def merge_two(strip):
        merged = merged_rows(second, pl.ds(pl.multiple_of(strip * STRIP, STRIP), STRIP), first)
        for part in range(2):
            r.twos[role, strip, part] = merged[part]

    merge_two(direct)
    piece = r.twos.at[role, direct]
    send(c_mate, piece, piece, mate)
    merge_two(indirect)
    halved = r.twos.at[role, pl.ds(strips * core, strips)]
    send(c_half, halved, halved, partner)

    lax.fori_loop(blocks // 2, blocks, load_of, 0, unroll=True)
    given = jnp.concatenate([r.given[0], r.given[1]], axis=1)
    rest = (jnp.where(sub == 0, given, jnp.zeros_like(given)) - r.total[...]).T
    rest = rest.reshape(2, shots // 8, 8, size)
    r.load[...] = jnp.stack([rest[0], rest[1]], axis=1).reshape(r.load.shape)

    c_x = [[channel() for d in range(3)] for which in range(2)]
    c_z = channel()
    for which in range(2):
        for d in (2, 1, 3):
            group = 2 * ((x + d) % 4) + (1 - far if which == 0 else far)
            send(
                c_x[which][d - 1], r.load.at[group], r.from_x.at[which, d - 1], beside[d - 1]
            )

    own_schur.wait()

    def split_schur(step, carry):
        at = pl.ds(pl.multiple_of(step * STRIP, STRIP), STRIP)
        for part in range(2):
            r.schur_high[part, :, at], r.schur_low[part, :, at] = halves(r.schur[part, at, :].T)
        return carry

    lax.fori_loop(0, size // STRIP, split_schur, 0)

    def side_sum(which, group):
        for d in range(3):
            receive(c_x[which][d], r.from_x.at[which, d])
        return (r.load[group] + r.from_x[which, 0]) + (r.from_x[which, 1] + r.from_x[which, 2])

    r.forward_sum[...] = side_sum(0, other_sub)
    send(c_z, r.forward_sum, r.from_z, opposite)

    piece = r.twos.at[1 - role, direct]
    receive(c_mate, piece)
    for part in range(2):
        aside = r.twos.at[1 - role, direct, part]
        send(c_aside[part], aside, aside, beside[2 * part])
    send(c_pass[0], piece, piece, partner)
    own_sum = side_sum(1, sub)

    receive(c_half, r.twos.at[role, pl.ds(strips * (1 - core), strips)])

    def split_two(which):
        def step_of(step, carry):
            to = pl.ds(pl.multiple_of(step * STRIP, STRIP), STRIP)
            for part in range(2):
                r.two_high[which, part, to, :], r.two_low[which, part, to, :] = halves(
                    r.twos[which, step, part]
                )
            return carry

        lax.fori_loop(0, size // STRIP, step_of, 0)

    split_two(role)
    two_early = (r.two_high.at[0], r.two_low.at[0])
    two_late = (r.two_high.at[1], r.two_low.at[1])
    four = (r.four_high, r.four_low)

    receive(c_z, r.from_z)
    summed = (own_sum + r.from_z[...]).reshape(2, 2, 8, size)
    summed = jnp.stack([summed[:, 0], summed[:, 1]], axis=0).reshape(32, size)
    solved = times(summed, (r.schur_high, r.schur_low), NN).reshape(2, 2, 8, size)
    solved = jnp.stack([solved[:, 0], solved[:, 1]], axis=0).reshape(2, 16, size)
    r.spare[...] = solved
    r.local[core] = r.spare[core]
    c_swap = channel()
    send(c_swap, r.spare.at[1 - core], r.local.at[core], partner)

    @pl.when(jnp.logical_not(has_before))
    def _():
        r.ahead_in[...] = jnp.zeros_like(r.ahead_in)

    @pl.when(jnp.logical_not(has_after))
    def _():
        r.back_in[...] = jnp.zeros_like(r.back_in)

    receive(c_swap, r.local.at[1 - core])
    start = r.local[1] - times(r.local[0], second, NT)
    c_start = channel()
    gives_start = jnp.logical_or(early, upper == 1)
    start_copy = send(c_start, r.start, r.start_in, mate, gives_start)
    r.start[...] = start
    pl.when(gives_start)(start_copy.start)

    c_node, c_other = channel(), channel()
    goes_on = jnp.logical_and(node, has_after)
    node_copy = send(c_node, r.ahead_out, r.ahead_in, critical, goes_on)
    other_copy = send(c_other, r.ahead_out, r.ahead_in, other, goes_on)

    @pl.when(enters)
    def _():
        receive(c_start, r.start_in)
        r.node_start[...] = r.start[...] + times(r.start_in[...], two_late, NT)

        @pl.when(jnp.logical_not(has_before))
        def _():
            r.ahead_out[...] = r.node_start[...]
            node_copy.start()
            other_copy.start()

    for part in range(2):
        receive(c_aside[part], r.twos.at[1 - role, indirect, part])
    piece = r.twos.at[1 - role, indirect]
    send(c_pass[1], piece, piece, partner)
    for i in range(2):
        receive(c_pass[i], r.twos.at[1 - role, strips * (1 - core) + (odd if i == 0 else 1 - odd)])
    split_two(1 - role)

    pl.when(ends)(lambda: receive(c_start, r.start_in))

    @pl.when(helps)
    def _():
        receive(c_start, r.start_in)
        r.node_start[...] = r.start_in[...] + times(r.start[...], two_late, NT)

    gives = jnp.logical_and(helps, has_row_after)
    takes = jnp.logical_and(leads, has_row_after)
    c_four = channel()
    c_four_aside, c_four_pass = [[channel() for i in range(2)] for j in range(2)]
    four_copy = send(c_four, r.four_out, r.four_in.at[direct], last_early, gives)
    soon = jnp.logical_and(helps, row == rows - 2)
    not_soon = jnp.logical_and(helps, row < rows - 2)

    def give():
        at = pl.ds(pl.multiple_of(direct * STRIP, STRIP), STRIP)
        merged = merged_rows(two_late, at, two_early)
        for part in range(2):
            r.four_out[part] = merged[part]
        four_copy.start()

    pl.when(soon)(give)

    @pl.when(jnp.logical_and(duo > 1, jnp.logical_or(gives, upper == 0)))
    def _():
        def merge_four(step, carry):
            at = pl.ds(pl.multiple_of(step * STRIP, STRIP), STRIP)
            merged = merged_rows(two_late, at, two_early)

            @pl.when(leads)
            def _():
                for part in range(2):
                    r.four_high[part, at, :], r.four_low[part, at, :] = halves(merged[part])

            @pl.when(node)
            def _():
                for part in range(2):
                    r.four_high[part, :, at], r.four_low[part, :, at] = halves(merged[part].T)

            return carry

        lax.fori_loop(0, size // STRIP, merge_four, 0)

    def weights_of(b, carry):
        spread = r.spread[b]
        for part in range(2):
            r.placed_high[part] = dot(spread, r.coupling_high[b, part]).astype(BF16)
            r.placed_low[part] = dot(spread, r.coupling_low[b, part]).astype(BF16)

        def inverse(part):
            return r.inverse_high[b, part], r.inverse_low[b, part]

        def strip_of(step, carry):
            at = pl.ds(pl.multiple_of(step * STRIP, STRIP), STRIP)
            left = [
                jnp.concatenate([source[0, at, :], source[1, at, :]], axis=0)
                for source in (r.placed_high, r.placed_low)
            ]
            merged = combine(dot3(left, inverse(0)), dot3(left, inverse(1)), 0)
            for part in range(2):
                r.coupling_high[b, part, at, :], r.coupling_low[b, part, at, :] = halves(
                    merged[part * STRIP : (part + 1) * STRIP]
                )
            return carry

        lax.fori_loop(0, size // STRIP, strip_of, 0)
        left = halves(r.eliminated[b].T)
        r.eliminated[b] = combine(dot3(left, inverse(0)), dot3(left, inverse(1)), 0)
        return carry

    towards_end = duo >= duos - 2

    @pl.when(towards_end)
    def _():
        lax.fori_loop(0, blocks, weights_of, 0)

    @pl.when(jnp.logical_and(node, has_before))
    def _():
        receive(c_node, r.ahead_in)

        @pl.when(jnp.logical_and(duo > 1, has_after))
        def _():
            r.ahead_out[...] = r.node_start[...] + times(r.ahead_in[...], four, NN)

        @pl.when(duo == 1)
        def _():
            r.ahead_out[...] = r.node_start[...] + times(
                times(r.ahead_in[...], two_early, NT), two_late, NT
            )

        @pl.when(has_after)
        def _():
            node_copy.start()
            other_copy.start()

    pl.when(not_soon)(give)

    @pl.when(ends)
    def _():
        receive(c_other, r.ahead_in)

    @pl.when(jnp.logical_and(leads, has_before))
    def _():
        receive(c_other, r.ahead_in)

    r.enter[...] = r.ahead_in[...]

    @pl.when(late)
    def _():
        r.enter[...] = r.start_in[...] + times(r.ahead_in[...], two_early, NT)

    r.trace[0] = r.local[0] - times(r.enter[...], first, NT)
    r.trace[1] = r.local[1] - times(r.trace[0], second, NT)
    queued = times(r.trace[0] - times(r.trace[1], second, NN), first, NN)
    r.queued[...] = queued
    c_queued = channel()
    queued_copy = send(c_queued, r.queued, r.queued_in, mate, late)
    pl.when(late)(queued_copy.start)

    @pl.when(jnp.logical_not(towards_end))
    def _():
        lax.fori_loop(0, blocks, weights_of, 0)

    c_upper, c_lower, c_lead, c_help, c_back_late = [channel() for i in range(5)]
    goes_back = jnp.logical_and(leads, has_row_before)
    upper_copy = send(c_upper, r.queued, r.upper_in, last_early, helps)
    lower_copy = send(c_lower, r.lower, r.lower_in, mate, leads)
    back_lead = send(c_lead, r.back_out, r.back_in, last_lead, goes_back)
    back_help = send(c_help, r.back_out, r.back_in, last_early, goes_back)
    back_late = send(c_back_late, r.back_out, r.back_in, last_late, goes_back)
    piece = r.four_in.at[direct]
    take_copies = [
        send(c_four_aside[part], piece.at[part], piece.at[part], beside[2 * part], takes)
        for part in range(2)
    ] + [send(c_four_pass[0], piece, piece, partner, takes)]
    piece = r.four_in.at[indirect]
    pass_copy = send(c_four_pass[1], piece, piece, partner, takes)
    top = (r.top_high, r.top_low)

    @pl.when(early)
    def _():
        receive(c_queued, r.queued_in)
        r.queued[...] += times(r.queued_in[...], two_early, NN)

    @pl.when(helps)
    def _():
        upper_copy.start()
        pl.when(has_row_after)(lambda: receive(c_help, r.back_in))
        r.carried[...] = r.queued_in[...] + times(r.back_in[...], two_late, NN)

    @pl.when(leads)
    def _():
        @pl.when(has_row_after)
        def _():
            receive(c_four, r.four_in.at[direct])
            for copy in take_copies:
                copy.start()
            for part in range(2):
                receive(c_four_aside[part], r.four_in.at[indirect, part])
            pass_copy.start()
            for i in range(2):
                receive(
                    c_four_pass[i],
                    r.four_in.at[strips * (1 - core) + (odd if i == 0 else 1 - odd)],
                )

            def split_top(step, carry):
                to = pl.ds(pl.multiple_of(step * STRIP, STRIP), STRIP)
                for part in range(2):
                    r.top_high[part, to, :], r.top_low[part, to, :] = halves(r.four_in[step, part])
                return carry

            lax.fori_loop(0, size // STRIP, split_top, 0)

        receive(c_upper, r.upper_in)

        @pl.when(has_row_after)
        def _():
            receive(c_lead, r.back_in)
            r.lower[...] = r.upper_in[...] + times(r.back_in[...], top, NN)

        @pl.when(jnp.logical_not(has_row_after))
        def _():
            r.lower[...] = r.upper_in[...]

        lower_copy.start()

        @pl.when(has_row_before)
        def _():
            r.back_out[...] = r.queued[...] + times(r.lower[...], four, NN)
            back_lead.start()
            back_help.start()
            back_late.start()

        r.carried[...] = r.queued_in[...] + times(r.lower[...], two_late, NN)

    @pl.when(ends)
    def _():
        pl.when(has_row_after)(lambda: receive(c_back_late, r.back_in))
        r.carried[...] = r.back_in[...]

    @pl.when(enters)
    def _():
        receive(c_lower, r.lower_in)
        r.carried[...] = r.lower_in[...]

    r.found[1] = r.trace[1] - r.carried[...]
    r.found[0] = r.trace[0] - times(r.found[1], second, NN)

    c_chip, c_far, c_across = channel(), channel(), channel()
    c_side = [[channel() for d in range(3)] for which in range(2)]
    place = r.gathered.at[sub, core]
    send(c_far, r.found.at[core], place, opposite)
    send(c_across, r.found.at[1 - core], place, across)
    send(c_chip, r.found.at[1 - core], place, partner)
    r.gathered[sub, core] = r.found[core]
    receive(c_chip, r.gathered.at[sub, 1 - core])
    for d in (2, 1, 3):
        send(c_side[0][d - 1], r.gathered.at[sub], r.gathered.at[sub], beside[d - 1])
    receive(c_far, r.gathered.at[other_sub, core])
    receive(c_across, r.gathered.at[other_sub, 1 - core])
    for d in (2, 1, 3):
        send(c_side[1][d - 1], r.gathered.at[other_sub], r.gathered.at[other_sub], beside[d - 1])
    for which in range(2):
        for d in (1, 2, 3):
            group = 2 * ((x + 4 - d) % 4) + (far if which == 0 else 1 - far)
            receive(c_side[which][d - 1], r.gathered.at[group])

    found = r.gathered[...].reshape(shots // 8, 2, 8, size)
    found = jnp.stack([found[:, 0], found[:, 1]], axis=0).reshape(2 * shots, size)
    r.found_high[...], r.found_low[...] = halves(found)
    turned = found.T
    r.separator_out[0] = turned[:, :shots]
    r.separator_out[1] = turned[:, shots:]

    def interior_of(b, carry):
        left = (r.found_high[...], r.found_low[...])
        out = [
            dot3(left, (r.coupling_high[b, part], r.coupling_low[b, part])) for part in range(2)
        ]
        turned = (r.eliminated[b] - combine(out[0], out[1], 0)).T
        r.interior_out[b, 0] = turned[:, :shots]
        r.interior_out[b, 1] = turned[:, shots:]
        return carry

    lax.fori_loop(0, blocks, interior_of, 0, unroll=True)

    for copy, when in unsent:
        if when is None:
            copy.wait_send()
        else:
            pl.when(when)(copy.wait_send)


CHANNELS = 48


def body(
    rhs_interior,
    rhs_separator,
    inverse_blocks,
    coupling,
    separator_rows,
    separator_inverse,
    transfer,
):
    _, nb, _, m, shots = rhs_interior.shape
    size = transfer.shape[-1]
    vmem = pltpu.VMEM
    inputs = {
        "rows": separator_rows[0],
        "given": rhs_separator[0],
        "rhs_hbm": rhs_interior[0],
        "inverse_hbm": inverse_blocks[0],
        "coupling_hbm": coupling[0],
        "schur_hbm": separator_inverse[0],
        "transfer_hbm": transfer[0],
    }
    outputs = {
        "interior_out": jax.ShapeDtypeStruct((nb, 2, m, shots), F32),
        "separator_out": jax.ShapeDtypeStruct((2, size, shots), F32),
    }
    scratch = {
        "inverse": vmem((nb, 2, m, m), F32),
        "inverse_high": vmem((nb, 2, m, m), BF16),
        "inverse_low": vmem((nb, 2, m, m), BF16),
        "rhs": vmem((nb, 2, m, shots), F32),
        "coupling": vmem((nb, 2, size, m), F32),
        "coupling_high": vmem((nb, 2, size, m), BF16),
        "coupling_low": vmem((nb, 2, size, m), BF16),
        "spread": vmem((nb, size, size), BF16),
        "placed_high": vmem((2, size, m), BF16),
        "placed_low": vmem((2, size, m), BF16),
        "eliminated": vmem((nb, m, 2 * shots), F32),
        "rhs_high": vmem((m, 2 * shots), BF16),
        "rhs_low": vmem((m, 2 * shots), BF16),
        "known_high": vmem((m, 2 * shots), BF16),
        "known_low": vmem((m, 2 * shots), BF16),
        "weighted_high": vmem((size, 2 * shots), BF16),
        "weighted_low": vmem((size, 2 * shots), BF16),
        "total": vmem((size, 2 * shots), F32),
        "load": vmem((8, 32, size), F32),
        "from_x": vmem((2, 3, 32, size), F32),
        "forward_sum": vmem((32, size), F32),
        "from_z": vmem((32, size), F32),
        "schur": vmem((2, size, size), F32),
        "schur_high": vmem((2, size, size), BF16),
        "schur_low": vmem((2, size, size), BF16),
        "pair": vmem((2, 2, size, size), F32),
        "pair_high": vmem((2, 2, size, size), BF16),
        "pair_low": vmem((2, 2, size, size), BF16),
        "twos": vmem((2, size // STRIP, 2, STRIP, size), F32),
        "two_high": vmem((2, 2, size, size), BF16),
        "two_low": vmem((2, 2, size, size), BF16),
        "four_high": vmem((2, size, size), BF16),
        "four_low": vmem((2, size, size), BF16),
        "four_out": vmem((2, STRIP, size), F32),
        "four_in": vmem((size // STRIP, 2, STRIP, size), F32),
        "top_high": vmem((2, size, size), BF16),
        "top_low": vmem((2, size, size), BF16),
        "upper_in": vmem((16, size), F32),
        "lower": vmem((16, size), F32),
        "lower_in": vmem((16, size), F32),
        "spare": vmem((2, 16, size), F32),
        "local": vmem((2, 16, size), F32),
        "start": vmem((16, size), F32),
        "start_in": vmem((16, size), F32),
        "node_start": vmem((16, size), F32),
        "enter": vmem((16, size), F32),
        "ahead_in": vmem((16, size), F32),
        "ahead_out": vmem((16, size), F32),
        "trace": vmem((2, 16, size), F32),
        "queued": vmem((16, size), F32),
        "queued_in": vmem((16, size), F32),
        "back_in": vmem((16, size), F32),
        "back_out": vmem((16, size), F32),
        "carried": vmem((16, size), F32),
        "found": vmem((2, 16, size), F32),
        "gathered": vmem((8, 2, 16, size), F32),
        "found_high": vmem((2 * shots, size), BF16),
        "found_low": vmem((2 * shots, size), BF16),
        "send_sem": pltpu.SemaphoreType.DMA((CHANNELS,)),
        "recv_sem": pltpu.SemaphoreType.DMA((CHANNELS,)),
        "here_sem": pltpu.SemaphoreType.DMA((2,)),
        "block_sem": pltpu.SemaphoreType.DMA((3, nb)),
    }
    names = list(inputs) + list(outputs) + list(scratch)

    def sweep_kernel(*refs):
        kernel(names, *refs)

    interior, separator = pl.pallas_call(
        sweep_kernel,
        out_shape=tuple(outputs.values()),
        in_specs=[pl.BlockSpec(memory_space=pltpu.VMEM)] * 2
        + [pl.BlockSpec(memory_space=pltpu.HBM)] * (len(inputs) - 2),
        out_specs=(pl.BlockSpec(memory_space=pltpu.VMEM),) * 2,
        scratch_shapes=list(scratch.values()),
        compiler_params=pltpu.CompilerParams(
            collective_id=0, has_side_effects=True, vmem_limit_bytes=51 << 20
        ),
    )(*inputs.values())
    return (interior[None], separator[None])


def solution(mesh):
    in_specs = (
        P("slab", "sub", None, None, None),
        P("slab", None, None, None),
        P("slab", "sub", None, None, None),
        P("slab", "sub", None, None, None),
        P("slab", "sub", None),
        P("slab", None, None, None),
        P("slab", None, None, None),
    )
    out_specs = (P("slab", "sub", None, None, None), P("slab", None, None, None))
    return jax.shard_map(body, mesh=mesh, in_specs=in_specs, out_specs=out_specs, check_vma=False)
```
